32 devices in a mesh: dp: 8 (over y, x, core), seq: 4 (over z).
Axes of the slice: x: 2, y: 2, z: 4, core: 2. Of those that a mesh axis runs over, the one named last changes fastest.
Arguments:
- layer_input: bfloat16 [8, 1024, 2048], P('dp', 'seq'), may hold values from -6 to 6
- segments: int32 [8, 1024], P('dp'), may hold values from 0 to 3, never falling along the last dimension, each value on 1 to 512 neighbouring positions
- w_query: bfloat16 [2048, 2048], P(('dp', 'seq')), may hold values from -0.125 to 0.125
- w_key: bfloat16 [2048, 2048], P(('dp', 'seq')), may hold values from -0.125 to 0.125
- w_value: bfloat16 [2048, 2048], P(('dp', 'seq')), may hold values from -0.125 to 0.125
- w_output: bfloat16 [2048, 2048], P(('dp', 'seq')), may hold values from -0.125 to 0.125
- w_gate: bfloat16 [2048, 8192], P(('dp', 'seq')), may hold values from -0.125 to 0.125
- w_up: bfloat16 [2048, 8192], P(('dp', 'seq')), may hold values from -0.125 to 0.125
- w_down: bfloat16 [8192, 2048], P(None, ('dp', 'seq')), may hold values from -0.0625 to 0.0625
- query_gain: float32 [2048], replicated, may hold values from 0.1 to 1.9
- key_gain: float32 [2048], replicated, may hold values from 0.1 to 1.9
- attn_gain: float32 [2048], replicated, may hold values from 0.1 to 1.9
- ff_gain: float32 [2048], replicated, may hold values from 0.1 to 1.9
- cotangent: bfloat16 [8, 1024, 2048], P('dp', 'seq'), may hold values from -6 to 6
Outputs:
- activation: bfloat16 [8, 1024, 2048], P('dp', 'seq')
- input_grad: bfloat16 [8, 1024, 2048], P('dp', 'seq')
- grad_query: float32 [2048, 2048], P(('dp', 'seq'))
- grad_key: float32 [2048, 2048], P(('dp', 'seq'))
- grad_value: float32 [2048, 2048], P(('dp', 'seq'))
- grad_output: float32 [2048, 2048], P(('dp', 'seq'))
- grad_gate: float32 [2048, 8192], P(('dp', 'seq'))
- grad_up: float32 [2048, 8192], P(('dp', 'seq'))
- grad_down: float32 [8192, 2048], P(None, ('dp', 'seq'))
- grad_query_gain: float32 [2048], P(('dp', 'seq'))
- grad_key_gain: float32 [2048], P(('dp', 'seq'))
- grad_attn_gain: float32 [2048], P(('dp', 'seq'))
- grad_ff_gain: float32 [2048], P(('dp', 'seq'))
The draws below stay inside these ranges and needn't reach their ends.
Inputs may be any that keep to these rules, and one draw needn't show every extreme that they name: `segments`: segment numbers never fall along a row, and a document holds at most half of 1024 tokens.
All inputs are finite; a program needn't handle non-finite values.
Results may differ from the reference program's by a relative error of at most 0.017.
Values may be sent and summed in bfloat16 or wider, within the bound.
No kernel may reach another device: no remote copies, remote signals or barrier semaphores. Data moves between devices by JAX's collectives and lax.ppermute only.
A program may use at most 384 MiB of HBM per device.

```python
import math
import jax
import jax.numpy as jnp
import numpy as np
from jax import lax

D = 2048
H = 16
HD = 128
FF = 8192
SEQ_LEN = 1024
BATCH = 8


def with_spikes(entries, rng, source, target, shards_of, factor):
    def block_of(dim):
        return (jnp.arange(entries.shape[dim]) // (entries.shape[dim] // shards_of)).reshape((-1,) + (1,) * (entries.ndim - 1 - dim))

    one_side = jax.random.permutation(rng, shards_of)[block_of(target)]
    second = (block_of(target) + shards_of // 2) % shards_of
    return jnp.where((block_of(source) == one_side) | (block_of(source) == second), factor * entries, entries)


def steps_of(key, dims, cuts, low, largest):
    def one(axis_at, shards_of):
        steps = jax.random.uniform(jax.random.fold_in(jax.random.fold_in(key, 6), axis_at), (shards_of,), jnp.float32, low / len(cuts), largest / len(cuts))
        return jnp.repeat(jnp.exp(steps), dims[axis_at] // shards_of).reshape((-1,) + (1,) * (len(dims) - axis_at - 1))

    level = one(*cuts[0])
    for cut in cuts[1:]:
        level = level * one(*cut)
    return level


def split_up(amount, total, bound, slope):
    portions = [(1 << 20) // math.isqrt(standing ** slope) + 1 for standing in range(2, amount + 1)]
    spare, holding = total - bound - (amount - 1), [1] * (amount - 1)
    while spare > 0:
        candidates = [i for i in range(amount - 1) if holding[i] < bound]
        whole, remaining = sum([portions[i] for i in candidates]), spare
        for i in candidates:
            more = min(bound - holding[i], max(1, remaining * portions[i] // whole), spare)
            holding[i] = holding[i] + more
            spare = spare - more
    return np.array([bound] + holding)


def ragged_sizes(rng, amount, total, reach, lean):
    if amount == 2:
        one = jax.random.randint(rng, (), max(1, total - reach), min(reach, total - 1) + 1)
        return jnp.stack([one, total - one])
    sizes = jnp.asarray(split_up(amount, total, reach, lean), jnp.int32)
    pairs = (amount - 1) // 2
    giver, taker = sizes[1:1 + 2 * pairs:2], sizes[2:2 + 2 * pairs:2]
    margin = jnp.minimum(giver - 1, reach - taker)
    moved = jax.random.randint(jax.random.fold_in(rng, 1), (pairs,), 0, 1 << 20) % (margin + 1)
    sizes = sizes.at[1:1 + 2 * pairs:2].set(giver - moved).at[2:2 + 2 * pairs:2].set(taker + moved)
    return sizes[jax.random.permutation(jax.random.fold_in(rng, 2), amount)]


def bell_draw(key, dims, scale, most, split=(), kind=jnp.bfloat16):
    level = steps_of(key, dims, split, -0.22, 0.18) if split else 1.0
    array = jax.random.normal(key, dims, jnp.float32) * scale * level
    return jnp.minimum(jnp.maximum(array, -most), most).astype(kind)


def heavy_noise(key, extent, width, bound, shards, heavy, kind=jnp.bfloat16):
    array = width * jax.random.normal(key, extent, jnp.float32)
    if shards:
        array = array * steps_of(key, extent, shards, -0.22, 0.18)
    return jnp.clip(with_spikes(array, jax.random.fold_in(key, 3), *heavy), -bound, bound).astype(kind)


def setup_inputs(seed: int = 0) -> dict:
    splits = jax.random.split(jax.random.key(seed), 15)
    layer_input = bell_draw(splits[0], (BATCH, SEQ_LEN, D), 1.0, 6.0, ((0, 8), (1, 4)))
    segments = jax.vmap(lambda own: jnp.searchsorted(jnp.cumsum(ragged_sizes(own, 4, SEQ_LEN, SEQ_LEN // 2, 2)), jnp.arange(SEQ_LEN), side="right"))(jax.random.split(splits[1], BATCH)).reshape((BATCH, SEQ_LEN)).astype(jnp.int32)
    w_query = bell_draw(splits[2], (D, D), D ** -0.5, 0.125, ((0, 32),))
    w_key = bell_draw(splits[3], (D, D), D ** -0.5, 0.125, ((0, 32),))
    w_value = bell_draw(splits[4], (D, D), D ** -0.5, 0.125, ((0, 32),))
    w_output = bell_draw(splits[5], (D, D), D ** -0.5, 0.125, ((0, 32),))
    w_gate = bell_draw(splits[6], (D, FF), D ** -0.5, 0.125, ((0, 32),))
    w_up = bell_draw(splits[7], (D, FF), D ** -0.5, 0.125, ((0, 32),))
    w_down = bell_draw(splits[8], (FF, D), FF ** -0.5, 0.0625, ((1, 32),))
    query_gain = jnp.clip(1.0 + 0.18 * jax.random.normal(splits[9], (D,), jnp.float32), 0.1, 1.9)
    key_gain = jnp.clip(1.0 + 0.18 * jax.random.normal(splits[10], (D,), jnp.float32), 0.1, 1.9)
    attn_gain = jnp.clip(1.0 + 0.18 * jax.random.normal(splits[11], (D,), jnp.float32), 0.1, 1.9)
    ff_gain = jnp.clip(1.0 + 0.18 * jax.random.normal(splits[12], (D,), jnp.float32), 0.1, 1.9)
    cotangent = heavy_noise(splits[13], (BATCH, SEQ_LEN, D), 1.0, 6.0, ((0, 8), (1, 4)), (0, 2, 8, 2.0))
    return dict(layer_input=layer_input, segments=segments, w_query=w_query, w_key=w_key, w_value=w_value, w_output=w_output, w_gate=w_gate, w_up=w_up, w_down=w_down, query_gain=query_gain, key_gain=key_gain, attn_gain=attn_gain, ff_gain=ff_gain, cotangent=cotangent)


EPSILON = 1e-06
ROPE_BASE = 500000.0
MASKED = -1e+30

@jax.custom_vjp
def low(v):
    return lax.optimization_barrier(v.astype(jnp.bfloat16)).astype(jnp.float32)

@jax.custom_vjp
def low_back(v):
    return v

def low_keep(v):
    return (low(v), None)

def low_pass(kept, grad):
    return (grad,)

def back_keep(v):
    return (v, None)

def back_low(kept, grad):
    return (low(grad),)
low.defvjp(low_keep, low_pass)
low_back.defvjp(back_keep, back_low)

def matmul_high(left, right):
    return jnp.dot(left, right, precision=lax.Precision.HIGHEST, preferred_element_type=jnp.float32)

def rms_norm(values, gain_vec):
    factor = lax.rsqrt(lax.optimization_barrier(jnp.mean(values * values, axis=-1, keepdims=True)) + EPSILON)
    return values * factor * gain_vec

def rope_tables(positions):
    half_dim = HD // 2
    frequency = jnp.power(jnp.float32(ROPE_BASE), -jnp.arange(half_dim, dtype=jnp.float32) * (2.0 / HD))
    angles = positions[:, None] * frequency[None, :]
    angles = jnp.concatenate([angles, angles], axis=-1)
    return (jnp.cos(angles), jnp.sin(angles))

def rotate(values, cosine_table, sine_table):
    shaped = values.reshape(values.shape[:-1] + (values.shape[-1] // HD, HD))
    first_half = shaped[..., :HD // 2]
    second = shaped[..., HD // 2:]
    turned = jnp.concatenate([-second, first_half], axis=-1)
    rotated = shaped * cosine_table[:, None, :] + turned * sine_table[:, None, :]
    return rotated.reshape(values.shape)

def attend_row(query_row, key_row, value_row, segment_row):
    block_rows = min(512, SEQ_LEN)
    block_count = SEQ_LEN // block_rows
    score_scale = HD ** (-0.5)
    query_blocks = query_row.reshape(block_count, block_rows, H, HD)
    block_starts = jnp.arange(block_count, dtype=jnp.int32) * block_rows

    def one_block(block_args):
        query_block, row_start = block_args
        query_pos = row_start + jnp.arange(block_rows, dtype=jnp.int32)
        query_seg = lax.dynamic_slice_in_dim(segment_row, row_start, block_rows)
        key_pos = jnp.arange(SEQ_LEN, dtype=jnp.int32)
        allowed = (key_pos[None, :] <= query_pos[:, None]) & (segment_row[None, :] == query_seg[:, None])
        scores = jnp.einsum('qhd,khd->hqk', query_block, key_row, precision=lax.Precision.HIGHEST) * score_scale
        scores = low_back(scores)
        probs_full = jax.nn.softmax(jnp.where(allowed[None], scores, MASKED), axis=-1)
        probs_low = low(probs_full)
        return jnp.einsum('hqk,khd->qhd', probs_low, value_row, precision=lax.Precision.HIGHEST)
    outputs = lax.map(jax.checkpoint(one_block), (query_blocks, block_starts))
    return outputs.reshape(SEQ_LEN, H, HD)

def layer(layer_in, parameters, segment_rows, cosine_table, sine_table):
    wq_full, wk_full, wv_full, wo_full, wg_full, wu_full, wd_full, q_gain, k_gain, a_gain, f_gain = parameters
    q_proj = low_back(matmul_high(layer_in, wq_full))
    k_proj = low_back(matmul_high(layer_in, wk_full))
    q_sent = low_back(low(rotate(rms_norm(q_proj, q_gain), cosine_table, sine_table)))
    k_sent = low_back(low(rotate(rms_norm(k_proj, k_gain), cosine_table, sine_table)))
    v_sent = low_back(low(matmul_high(layer_in, wv_full)))
    row_count = layer_in.shape[0]
    head_shape = (row_count, SEQ_LEN, H, HD)
    attended = jax.vmap(attend_row)(q_sent.reshape(head_shape), k_sent.reshape(head_shape), v_sent.reshape(head_shape), segment_rows)
    mixed_sent = low_back(low(attended.reshape(row_count, SEQ_LEN, D)))
    attn_out = low_back(matmul_high(mixed_sent, wo_full))
    residual = layer_in + rms_norm(attn_out, a_gain)
    residual_low = low(residual)
    gate_act = low_back(matmul_high(residual_low, wg_full))
    up_act = low_back(matmul_high(residual_low, wu_full))
    hidden = low(jax.nn.silu(gate_act) * up_act)
    ff_out = low_back(matmul_high(hidden, wd_full))
    return residual + rms_norm(ff_out, f_gain)

def reference(layer_input, segments, w_query, w_key, w_value, w_output, w_gate, w_up, w_down, query_gain, key_gain, attn_gain, ff_gain, cotangent):
    row_group = math.gcd(BATCH, max(1, 4096 // SEQ_LEN))
    group_count = BATCH // row_group
    parameters = (w_query.astype(jnp.float32), w_key.astype(jnp.float32), w_value.astype(jnp.float32), w_output.astype(jnp.float32), w_gate.astype(jnp.float32), w_up.astype(jnp.float32), w_down.astype(jnp.float32), query_gain.astype(jnp.float32), key_gain.astype(jnp.float32), attn_gain.astype(jnp.float32), ff_gain.astype(jnp.float32))
    positions = jnp.arange(SEQ_LEN, dtype=jnp.float32)
    cosine_table, sine_table = rope_tables(positions)
    inputs_grouped = layer_input.astype(jnp.float32).reshape(group_count, row_group, SEQ_LEN, D)
    segments_grouped = segments.reshape(group_count, row_group, SEQ_LEN)
    cotangent_grouped = cotangent.astype(jnp.float32).reshape(group_count, row_group, SEQ_LEN, D)

    def step(totals, step_item):
        inputs_now, segments_now, cotangent_now = step_item

        def forward(layer_in, params_in):
            return layer(layer_in, params_in, segments_now, cosine_table, sine_table)
        output_now, backward = jax.vjp(forward, inputs_now, parameters)
        grad_input, grad_params = backward(cotangent_now)
        totals = tuple((total_now + grad_now for total_now, grad_now in zip(totals, grad_params)))
        return (totals, (output_now.astype(jnp.bfloat16), grad_input.astype(jnp.bfloat16)))
    initial = tuple((jnp.zeros(param.shape, jnp.float32) for param in parameters))
    totals, (outputs, grad_inputs) = lax.scan(step, initial, (inputs_grouped, segments_grouped, cotangent_grouped))
    activation = outputs.reshape(BATCH, SEQ_LEN, D)
    input_grad = grad_inputs.reshape(BATCH, SEQ_LEN, D)
    return (activation, input_grad, totals[0], totals[1], totals[2], totals[3], totals[4], totals[5], totals[6], totals[7], totals[8], totals[9], totals[10])
```

```python
import jax
import jax.numpy as jnp
from jax import lax
from jax.sharding import PartitionSpec as P

HD = 128
EPSILON = 1e-06
ROPE_BASE = 500000.0
MASKED = -1e30
BF = jnp.bfloat16
F32 = jnp.float32


def project(left, weight):
    return jnp.dot(left, weight, preferred_element_type=F32)


def back_project(grad_in, weight):
    return lax.dot_general(
        grad_in, weight, (((grad_in.ndim - 1,), (1,)), ((), ())), preferred_element_type=F32
    )


def rows_product(left, right):
    return lax.dot_general(left, right, (((0,), (0,)), ((), ())), preferred_element_type=F32)


def inv_rms(values):
    return lax.rsqrt(jnp.mean(values * values, axis=-1, keepdims=True) + EPSILON)


def rms_back(normed, factor, gain, grad):
    scaled = grad * gain
    inner = jnp.mean(scaled * normed, axis=-1, keepdims=True)
    return (scaled - normed * inner) * factor


def rope_tables(positions):
    half_dim = HD // 2
    frequency = jnp.power(F32(ROPE_BASE), -jnp.arange(half_dim, dtype=F32) * (2.0 / HD))
    angles = positions[:, None] * frequency[None, :]
    angles = jnp.concatenate([angles, angles], axis=-1)
    return (jnp.cos(angles), jnp.sin(angles))


def rotate(values, cosine, sine):
    shaped = values.reshape(values.shape[:-1] + (values.shape[-1] // HD, HD))
    first = shaped[..., : HD // 2]
    second = shaped[..., HD // 2 :]
    turned = jnp.concatenate([-second, first], axis=-1)
    return (shaped * cosine[:, None, :] + turned * sine[:, None, :]).reshape(values.shape)


def shift(values, count, step):
    return lax.ppermute(values, "seq", [((i + step) % count, i) for i in range(count)])


def gather_cyclic(values, count):
    if count != 4:
        return [values] + [shift(values, count, p) for p in range(1, count)]
    me = lax.axis_index("seq")
    far = lax.ppermute(values, "seq", [(i ^ 2, i) for i in range(4)])
    after = lax.ppermute(values, "seq", [(i + 1, i) for i in range(3)])
    before = lax.ppermute(values, "seq", [(i, i + 1) for i in range(3)])
    ends = lax.ppermute(far, "seq", [(2, 3), (1, 0)])
    return [values, jnp.where(me == 3, ends, after), far, jnp.where(me == 0, ends, before)]


def scatter_cyclic(parts, count):
    low = [part.astype(BF) for part in parts]
    if count != 4:
        total = parts[0]
        for p in range(1, count):
            got = lax.ppermute(low[p], "seq", [(i, (i + p) % count) for i in range(count)])
            total = total + got.astype(F32)
        return total
    me = lax.axis_index("seq")
    ends = lax.ppermute(jnp.where(me == 0, low[3], low[1]), "seq", [(0, 1), (3, 2)])
    after = lax.ppermute(low[1], "seq", [(i, i + 1) for i in range(3)])
    before = lax.ppermute(low[3], "seq", [(i + 1, i) for i in range(3)])
    far_sum = (parts[2] + ends.astype(F32)).astype(BF)
    far = lax.ppermute(far_sum, "seq", [(i, i ^ 2) for i in range(4)])
    return parts[0] + after.astype(F32) + before.astype(F32) + far.astype(F32)


def sum_stats(stats, count):
    total = stats
    for p in range(1, count):
        total = total + jnp.roll(shift(stats, count, p), p, axis=1)
    return total


def sum_everywhere(values, dp_count, seq_count):
    for name, count in (("seq", seq_count), ("dp", dp_count)):
        if count & (count - 1):
            values = lax.psum(values, name)
            continue
        bit = 1
        while bit < count:
            values = values + lax.ppermute(values, name, [(i, i ^ bit) for i in range(count)])
            bit *= 2
    return values


def swap_blocks(values):
    return lax.all_to_all(values, "seq", split_axis=0, concat_axis=0, tiled=True)


def gather_dp(values):
    return lax.all_gather(values, "dp", axis=0, tiled=True)


def scatter_dp(values):
    return lax.psum_scatter(values, "dp", scatter_dimension=0, tiled=True)


def attend(query, key, value, segments, positions, heads):
    length = query.shape[0]
    block_rows = min(512, length)
    blocks = length // block_rows
    scale = HD ** (-0.5)
    key_heads = key.reshape(length, heads, HD)
    value_heads = value.reshape(length, heads, HD)
    split = lambda v: v.reshape((blocks, block_rows) + v.shape[1:])

    def one_block(item):
        q, seg, pos = item
        scores = jnp.einsum("qhd,khd->hqk", q, key_heads, preferred_element_type=F32) * scale
        allowed = (positions[None, :] <= pos[:, None]) & (segments[None, :] == seg[:, None])
        scores = jnp.where(allowed[None], scores, MASKED)
        top = jnp.max(scores, axis=-1, keepdims=True)
        exps = jnp.exp(scores - top)
        total = jnp.sum(exps, axis=-1, keepdims=True)
        probs = exps / total
        mixed = jnp.einsum("hqk,khd->qhd", probs.astype(BF), value_heads, preferred_element_type=F32)
        return (mixed.astype(BF), (top + jnp.log(total))[..., 0])

    items = (split(query.reshape(length, heads, HD)), split(segments), split(positions))
    mixed, logs = lax.map(one_block, items)
    return (mixed.reshape(length, heads * HD), logs)


def attend_back(query, key, value, grad_mixed, logs, segments, positions, heads):
    length = query.shape[0]
    block_rows = min(512, length)
    blocks = length // block_rows
    scale = HD ** (-0.5)
    key_heads = key.reshape(length, heads, HD)
    value_heads = value.reshape(length, heads, HD)
    split = lambda v: v.reshape((blocks, block_rows) + v.shape[1:])

    def one_block(totals, item):
        grad_keys, grad_values = totals
        q, grad, log_total, seg, pos = item
        scores = jnp.einsum("qhd,khd->hqk", q, key_heads, preferred_element_type=F32) * scale
        allowed = (positions[None, :] <= pos[:, None]) & (segments[None, :] == seg[:, None])
        scores = jnp.where(allowed[None], scores, MASKED)
        probs = jnp.exp(scores - log_total[..., None])
        grad_probs = jnp.einsum("qhd,khd->hqk", grad, value_heads, preferred_element_type=F32)
        grad_values = grad_values + jnp.einsum(
            "hqk,qhd->khd", probs.astype(BF), grad, preferred_element_type=F32
        )
        inner = jnp.sum(probs * grad_probs, axis=-1, keepdims=True)
        grad_scores = (probs * (grad_probs - inner)).astype(BF)
        grad_q = jnp.einsum("hqk,khd->qhd", grad_scores, key_heads, preferred_element_type=F32) * scale
        grad_keys = grad_keys + scale * jnp.einsum(
            "hqk,qhd->khd", grad_scores, q, preferred_element_type=F32
        )
        return ((grad_keys, grad_values), grad_q.astype(BF))

    zeros = jnp.zeros((length, heads, HD), F32)
    by_head = lambda v: split(v.reshape(length, heads, HD))
    items = (by_head(query), by_head(grad_mixed), logs, split(segments), split(positions))
    (grad_keys, grad_values), grad_q = lax.scan(one_block, (zeros, zeros), items)
    flat = lambda v: v.reshape(length, heads * HD).astype(BF)
    return (flat(grad_q), flat(grad_keys), flat(grad_values))


def build(dp_count, seq_count):
    def shards(
        layer_input,
        segments,
        w_query,
        w_key,
        w_value,
        w_output,
        w_gate,
        w_up,
        w_down,
        query_gain,
        key_gain,
        attn_gain,
        ff_gain,
        cotangent,
    ):
        n = seq_count
        tokens, width = layer_input.shape[1:]
        shard_rows = w_query.shape[0]
        part = width // n
        ff_width = w_gate.shape[1]
        ff_part = ff_width // n
        heads = part // HD
        length = n * tokens
        me = lax.axis_index("seq")
        dp_me = lax.axis_index("dp")
        x_own = layer_input[0]
        cot = cotangent[0].astype(F32)

        by_part = lambda w: w.reshape(shard_rows, n, -1).transpose(1, 0, 2)
        qkv_blocks = jnp.concatenate([by_part(w_query), by_part(w_key), by_part(w_value)], axis=2)
        w_qkv = gather_dp(swap_blocks(qkv_blocks).reshape(n * shard_rows, 3 * part))
        devices = dp_count * n
        to_heads = [(b, (b % dp_count) * n + b // dp_count) for b in range(devices)]
        from_heads = [(dst, src) for src, dst in to_heads]
        w_out = gather_dp(lax.ppermute(w_output, ("dp", "seq"), to_heads))
        w_gate_part, w_up_part, w_down_part = (
            gather_dp(swap_blocks(by_part(w)).reshape(n * shard_rows, ff_part))
            for w in (w_gate, w_up, w_down.T)
        )

        x_all = jnp.concatenate(gather_cyclic(x_own, n), axis=0)
        natural = jnp.arange(length, dtype=jnp.int32)
        positions = (natural + me * tokens) % length
        seg_row = segments[0]
        seg_cyclic = lax.dynamic_slice_in_dim(
            jnp.concatenate([seg_row, seg_row]), me * tokens, length, 0
        )
        cosine, sine = rope_tables(positions.astype(F32))
        own_gain = lambda g: lax.dynamic_slice_in_dim(g, me * part, part, 0)
        q_gain = own_gain(query_gain)
        k_gain = own_gain(key_gain)

        qkv = project(x_all, w_qkv)
        q_proj, k_proj, v_proj = (qkv[:, j * part : (j + 1) * part] for j in range(3))
        squares = jnp.stack([jnp.sum(q_proj * q_proj, axis=-1), jnp.sum(k_proj * k_proj, axis=-1)])
        squares = sum_stats(squares.reshape(2, n, tokens), n).reshape(2, length, 1)
        factors = lax.rsqrt(squares / width + EPSILON)
        q_low = rotate(q_proj * factors[0] * q_gain, cosine, sine).astype(BF)
        k_low = rotate(k_proj * factors[1] * k_gain, cosine, sine).astype(BF)
        v_low = v_proj.astype(BF)
        mixed, logs = attend(q_low, k_low, v_low, seg_cyclic, positions, heads)

        chunks = lambda v: [v[p * tokens : (p + 1) * tokens] for p in range(n)]
        attn_out = scatter_cyclic(chunks(project(mixed, w_out)), n)
        attn_factor = inv_rms(attn_out)
        attn_normed = attn_out * attn_factor
        residual = x_own.astype(F32) + attn_normed * attn_gain
        residual_all = jnp.concatenate(gather_cyclic(residual.astype(BF), n), axis=0)

        gate_act = project(residual_all, w_gate_part)
        up_act = project(residual_all, w_up_part)
        hidden = (jax.nn.silu(gate_act) * up_act).astype(BF)
        ff_out = scatter_cyclic(chunks(back_project(hidden, w_down_part)), n)
        ff_factor = inv_rms(ff_out)
        ff_normed = ff_out * ff_factor
        activation = (residual + ff_normed * ff_gain).astype(BF)
        grad_ff_gain = jnp.sum(cot * ff_normed, axis=0)
        d_ff = rms_back(ff_normed, ff_factor, ff_gain, cot).astype(BF)
        d_ff_all = jnp.concatenate(gather_cyclic(d_ff, n), axis=0)

        d_hidden = project(d_ff_all, w_down_part)
        sig = 1.0 / (1.0 + jnp.exp(-gate_act))
        d_gate = (d_hidden * up_act * sig * (1.0 + gate_act * (1.0 - sig))).astype(BF)
        d_up = (d_hidden * gate_act * sig).astype(BF)
        d_res = back_project(d_gate, w_gate_part) + back_project(d_up, w_up_part)
        d_res = cot + scatter_cyclic(chunks(d_res), n)

        def back_to_rows(grad):
            return swap_blocks(scatter_dp(grad.astype(BF)).reshape(n, shard_rows, -1))

        joined = lambda g: g.transpose(1, 0, 2).reshape(shard_rows, -1).astype(F32)
        grad_down = joined(back_to_rows(rows_product(d_ff_all, hidden))).T
        grad_gate = joined(back_to_rows(rows_product(residual_all, d_gate)))
        grad_up = joined(back_to_rows(rows_product(residual_all, d_up)))

        grad_attn_gain = jnp.sum(d_res * attn_normed, axis=0)
        d_attn = rms_back(attn_normed, attn_factor, attn_gain, d_res).astype(BF)
        d_attn_all = jnp.concatenate(gather_cyclic(d_attn, n), axis=0)
        d_mixed = back_project(d_attn_all, w_out).astype(BF)
        out_rows = scatter_dp(rows_product(mixed, d_attn_all).astype(BF))
        grad_output = lax.ppermute(out_rows, ("dp", "seq"), from_heads).astype(F32)
        d_q, d_k, d_v = attend_back(
            q_low, k_low, v_low, d_mixed, logs, seg_cyclic, positions, heads
        )

        back_q = rotate(d_q.astype(F32), cosine, -sine)
        back_k = rotate(d_k.astype(F32), cosine, -sine)
        q_normed = q_proj * factors[0]
        k_normed = k_proj * factors[1]
        grad_q_gain = jnp.sum(back_q * q_normed, axis=0)
        grad_k_gain = jnp.sum(back_k * k_normed, axis=0)
        inner = jnp.stack(
            [
                jnp.sum(back_q * q_gain * q_normed, axis=-1),
                jnp.sum(back_k * k_gain * k_normed, axis=-1),
            ]
        )
        inner = sum_stats(inner.reshape(2, n, tokens), n).reshape(2, length, 1) / width
        d_q_proj = ((back_q * q_gain - q_normed * inner[0]) * factors[0]).astype(BF)
        d_k_proj = ((back_k * k_gain - k_normed * inner[1]) * factors[1]).astype(BF)
        d_qkv = jnp.concatenate([d_q_proj, d_k_proj, d_v], axis=1)
        input_grad = d_res + scatter_cyclic(chunks(back_project(d_qkv, w_qkv)), n)
        qkv_rows = back_to_rows(rows_product(x_all, d_qkv))
        grad_query, grad_key, grad_value = (
            joined(qkv_rows[:, :, j * part : (j + 1) * part]) for j in range(3)
        )

        spread = lambda g: lax.dynamic_update_slice(jnp.zeros(width, F32), g, (me * part,))
        gains = jnp.stack([spread(grad_q_gain), spread(grad_k_gain), grad_attn_gain, grad_ff_gain])
        gains = sum_everywhere(gains, dp_count, n)
        share = width // devices
        gains = lax.dynamic_slice_in_dim(gains, (dp_me * n + me) * share, share, 1)
        return (
            activation[None],
            input_grad.astype(BF)[None],
            grad_query,
            grad_key,
            grad_value,
            grad_output,
            grad_gate,
            grad_up,
            grad_down,
            gains[0],
            gains[1],
            gains[2],
            gains[3],
        )

    return shards


def solution(mesh):
    both = P(("dp", "seq"), None)
    tokens = P("dp", "seq", None)
    columns = P(None, ("dp", "seq"))
    gain = P(("dp", "seq"))
    return jax.shard_map(
        build(mesh.shape["dp"], mesh.shape["seq"]),
        mesh=mesh,
        in_specs=(tokens, P("dp", None)) + (both,) * 6 + (columns,) + (P(),) * 4 + (tokens,),
        out_specs=(tokens, tokens) + (both,) * 6 + (columns,) + (gain,) * 4,
        check_vma=False,
    )
```

```python
import functools

import jax
import jax.numpy as jnp
from jax import lax
from jax.experimental import pallas as pl
from jax.experimental.pallas import tpu as pltpu
from jax.sharding import PartitionSpec as P

HD = 128
EPSILON = 1e-06
ROPE_BASE = 500000.0
MASKED = -1e30
LOG2E = 1.4426950408889634
BF = jnp.bfloat16
F32 = jnp.float32


def project(left, weight):
    return jnp.dot(left, weight, preferred_element_type=F32)


def back_project(grad_in, weight):
    return lax.dot_general(
        grad_in, weight, (((grad_in.ndim - 1,), (1,)), ((), ())), preferred_element_type=F32
    )


def rows_product(left, right):
    return lax.dot_general(left, right, (((0,), (0,)), ((), ())), preferred_element_type=F32)


def inv_rms(values):
    return lax.rsqrt(jnp.mean(values * values, axis=-1, keepdims=True) + EPSILON)


def rms_back(normed, factor, gain, grad):
    scaled = grad * gain
    inner = jnp.mean(scaled * normed, axis=-1, keepdims=True)
    return (scaled - normed * inner) * factor


def rope_tables(positions):
    half_dim = HD // 2
    frequency = jnp.power(F32(ROPE_BASE), -jnp.arange(half_dim, dtype=F32) * (2.0 / HD))
    angles = positions[:, None] * frequency[None, :]
    cosine, sine = jnp.cos(angles), jnp.sin(angles)
    return (jnp.concatenate([cosine, cosine], axis=-1), jnp.concatenate([-sine, sine], axis=-1))


def shift(values, count, step):
    return lax.ppermute(values, "seq", [((i + step) % count, i) for i in range(count)])


def gather_cyclic(values, count):
    if count != 4:
        return [values] + [shift(values, count, p) for p in range(1, count)]
    me = lax.axis_index("seq")
    far = lax.ppermute(values, "seq", [(i ^ 2, i) for i in range(4)])
    after = lax.ppermute(values, "seq", [(i + 1, i) for i in range(3)])
    before = lax.ppermute(values, "seq", [(i, i + 1) for i in range(3)])
    ends = lax.ppermute(far, "seq", [(2, 3), (1, 0)])
    return [values, jnp.where(me == 3, ends, after), far, jnp.where(me == 0, ends, before)]


def scatter_start(after, before, count):
    me = lax.axis_index("seq")
    ends = lax.ppermute(jnp.where(me == 0, before, after), "seq", [(0, 1), (count - 1, count - 2)])
    step = [(i, i + 1) for i in range(count - 1)]
    after = lax.ppermute(after, "seq", step)
    before = lax.ppermute(before, "seq", [(j, i) for i, j in step])
    return [ends, after, before]


def scatter_far(far, ends, count):
    far_sum = (far + ends.astype(F32)).astype(BF)
    return lax.ppermute(far_sum, "seq", [(i, i ^ 2) for i in range(count)])


def scatter_end(own, got):
    for part in got:
        own = own + part.astype(F32)
    return own


def sum_stats(stats, count):
    total = stats
    for p in range(1, count):
        total = total + jnp.roll(shift(stats, count, p), p, axis=1)
    return total


def sum_everywhere(values, dp_count, seq_count):
    for name, count in (("dp", dp_count), ("seq", seq_count)):
        if count & (count - 1):
            values = lax.psum(values, name)
            continue
        bit = 1
        while bit < count:
            values = values + lax.ppermute(values, name, [(i, i ^ bit) for i in range(count)])
            bit *= 2
    return values


def swap_blocks(values):
    return lax.all_to_all(values, "seq", split_axis=0, concat_axis=0, tiled=True)


def send_columns(values, me, count):
    part = values.shape[1] // count
    columns = lambda p: lax.dynamic_slice_in_dim(values, (me + p) % count * part, part, 1)
    return [columns(0)] + [
        lax.ppermute(columns(p), "seq", [(i, (i + p) % count) for i in range(count)])
        for p in range(1, count)
    ]


def place_blocks(blocks, me, first, width, total=None):
    count = len(blocks)
    rows = blocks[0].shape[0]
    if total is None:
        total = jnp.zeros((count * rows, width), blocks[0].dtype)
    for p, block in enumerate(blocks):
        total = lax.dynamic_update_slice(total, block, ((me - p) % count * rows, first))
    return total


def send_rows(values, me, count):
    size = values.shape[0] // count
    rows = lambda p: lax.dynamic_slice_in_dim(values, (me + p) % count * size, size, 0)
    return [rows(0)] + [
        lax.ppermute(rows(p), "seq", [(i, (i + p) % count) for i in range(count)])
        for p in range(1, count)
    ]


def join_columns(blocks, me):
    count = len(blocks)
    rows, part = blocks[0].shape
    total = jnp.zeros((rows, count * part), F32)
    for p, block in enumerate(blocks):
        total = lax.dynamic_update_slice(total, block.astype(F32), (0, (me - p) % count * part))
    return total


def gather_dp(values):
    return lax.all_gather(values, "dp", axis=0, tiled=True)


def scatter_dp(values):
    return lax.psum_scatter(values, "dp", scatter_dimension=0, tiled=True)


def softmax_window(q, k_ref, seg_q, seg_row_ref, valid_from, place, tokens, count, span):
    parts = []
    for w in range(span):
        at = ((place - w) % count) * tokens
        scores = lax.dot_general(
            q, k_ref[at : at + tokens, :], (((1,), (1,)), ((), ())), preferred_element_type=F32
        )
        seg = seg_q if w == 0 else jnp.where(valid_from >= w, seg_q, -1)
        allowed = seg == seg_row_ref[:, at : at + tokens]
        if w == 0:
            rows = lax.broadcasted_iota(jnp.int32, (tokens, tokens), 0)
            cols = lax.broadcasted_iota(jnp.int32, (tokens, tokens), 1)
            allowed = allowed & (cols <= rows)
        parts.append(jnp.where(allowed, scores, MASKED))
    top = parts[0]
    for part in parts[1:]:
        top = jnp.maximum(top, part)
    top = jnp.max(top, axis=-1, keepdims=True)
    exps = [jnp.exp2((part - top) * (HD**-0.5 * LOG2E)) for part in parts]
    total = exps[0]
    for part in exps[1:]:
        total = total + part
    inverse = 1.0 / jnp.sum(total, axis=-1, keepdims=True)
    return [part * inverse for part in exps]


def turn(values, cosine, sine):
    return values * cosine + pltpu.roll(values, HD // 2, 1) * sine


def attend_kernel(
    tokens, count, span,
    me_ref, q_ref, k_ref, v_ref, f_ref, qg_ref, kg_ref, cos_ref, sin_ref, segc_ref, segr_ref,
    o_ref, qb_ref, kb_ref, vb_ref,
):
    cosine, sine = cos_ref[...], sin_ref[...]
    factors = f_ref[...]
    qb_ref[...] = turn(q_ref[...] * factors[:, 0:1] * qg_ref[...], cosine, sine).astype(BF)
    kb_ref[...] = turn(k_ref[...] * factors[:, 1:2] * kg_ref[...], cosine, sine).astype(BF)
    vb_ref[...] = v_ref[...].astype(BF)
    for place in range(count):
        rows = slice(place * tokens, (place + 1) * tokens)
        chunk = (me_ref[0] + place) % count
        probs = softmax_window(
            qb_ref[rows, :], kb_ref, segc_ref[rows, :], segr_ref, chunk, place, tokens, count, span
        )
        mixed = None
        for w in range(span):
            at = ((place - w) % count) * tokens
            part = jnp.dot(probs[w].astype(BF), vb_ref[at : at + tokens, :], preferred_element_type=F32)
            mixed = part if mixed is None else mixed + part
        o_ref[rows, :] = mixed.astype(BF)


def attend_back_kernel(
    tokens, count, span, me_ref, *refs
):
    grads_in = refs[:count]
    (q_ref, k_ref, v_ref, qp_ref, kp_ref, f_ref, qg_ref, kg_ref, cos_ref, sin_ref, segc_ref, segr_ref,
     dq_ref, dk_ref, dv_ref, inner_ref, gain_ref, dk_sum, dv_sum) = refs[count:]
    scale = HD**-0.5
    dk_sum[...] = jnp.zeros_like(dk_sum)
    dv_sum[...] = jnp.zeros_like(dv_sum)
    for place in range(count):
        rows = slice(place * tokens, (place + 1) * tokens)
        chunk = (me_ref[0] + place) % count
        q = q_ref[rows, :]
        grad = grads_in[place][...]
        probs = softmax_window(
            q, k_ref, segc_ref[rows, :], segr_ref, chunk, place, tokens, count, span
        )
        grads = []
        inner = None
        for w in range(span):
            at = ((place - w) % count) * tokens
            part = nt_dot(grad, v_ref[at : at + tokens, :])
            grads.append(part)
            inner = probs[w] * part if inner is None else inner + probs[w] * part
            dv_sum[at : at + tokens, :] += lax.dot_general(
                probs[w].astype(BF), grad, (((0,), (0,)), ((), ())), preferred_element_type=F32
            )
        inner = jnp.sum(inner, axis=-1, keepdims=True)
        dq = None
        for w in range(span):
            at = ((place - w) % count) * tokens
            ds = (probs[w] * (grads[w] - inner)).astype(BF)
            part = jnp.dot(ds, k_ref[at : at + tokens, :], preferred_element_type=F32)
            dq = part if dq is None else dq + part
            dk_sum[at : at + tokens, :] += lax.dot_general(
                ds, q, (((0,), (0,)), ((), ())), preferred_element_type=F32
            )
        dq_ref[rows, :] = dq
    ones = jnp.ones((8, HD), F32)
    first = pl.program_id(0) == 0
    sides = ((dq_ref, dq_ref, qp_ref, qg_ref), (dk_sum, dk_ref, kp_ref, kg_ref))
    for j, (raw_ref, out_ref, proj_ref, g_ref) in enumerate(sides):
        raw = (raw_ref[...] * scale).astype(BF).astype(F32)
        back = turn(raw, cos_ref[...], -sin_ref[...])
        normed = proj_ref[...] * f_ref[:, j : j + 1]
        gain_ref[j] = jnp.broadcast_to(jnp.sum(back * normed, axis=0, keepdims=True), (8, HD))
        back = back * g_ref[...]
        out_ref[...] = back
        sums = lax.dot_general(
            ones, back * normed, (((1,), (1,)), ((), ())),
            precision=lax.Precision.HIGHEST, preferred_element_type=F32,
        )
        inner_ref[j] = jnp.where(first, sums, inner_ref[j] + sums)
    dv_ref[...] = dv_sum[...].astype(BF)


def attend_specs(length, heads):
    head = lambda j: pl.BlockSpec((length, HD), lambda h, me: (0, j * heads + h))
    whole = lambda *shape: pl.BlockSpec(shape, lambda h, me: (0, 0))
    gain = pl.BlockSpec((1, HD), lambda h, me: (0, h))
    return head, whole, gain


def attend(me, qkv, factors, q_gain, k_gain, tables, seg, count):
    length = qkv.shape[0]
    part = qkv.shape[1] // 3
    heads = part // HD
    tokens = length // count
    span = min(count, (length // 2 - 1 + tokens - 1) // tokens + 1)
    head, whole, gain = attend_specs(length, heads)
    low = jax.ShapeDtypeStruct((length, part), BF)
    return pl.pallas_call(
        functools.partial(attend_kernel, tokens, count, span),
        grid_spec=pltpu.PrefetchScalarGridSpec(
            num_scalar_prefetch=1,
            grid=(heads,),
            in_specs=[head(0), head(1), head(2), whole(length, 2), gain, gain]
            + [whole(length, HD)] * 2
            + [whole(length, 1), whole(1, length)],
            out_specs=[head(0)] * 4,
        ),
        out_shape=[low] * 4,
        compiler_params=params(),
        cost_estimate=cost(4 * length * length * part, 16 << 20, length * length * heads),
        name="attend",
    )(me, qkv, qkv, qkv, factors, q_gain[None], k_gain[None], *tables, seg[:, None], seg[None])


def attend_back(me, pieces, query, key, value, qkv, factors, q_gain, k_gain, tables, seg, count):
    length, part = query.shape
    heads = part // HD
    tokens = length // count
    span = min(count, (length // 2 - 1 + tokens - 1) // tokens + 1)
    head, whole, gain = attend_specs(length, heads)
    return pl.pallas_call(
        functools.partial(attend_back_kernel, tokens, count, span),
        grid_spec=pltpu.PrefetchScalarGridSpec(
            num_scalar_prefetch=1,
            grid=(heads,),
            in_specs=[pl.BlockSpec((tokens, HD), lambda h, me: (0, h))] * count
            + [head(0)] * 3
            + [head(0), head(1), whole(length, 2), gain, gain]
            + [whole(length, HD)] * 2
            + [whole(length, 1), whole(1, length)],
            out_specs=[head(0)] * 3
            + [
                pl.BlockSpec((2, 8, length), lambda h, me: (0, 0, 0)),
                pl.BlockSpec((2, 8, HD), lambda h, me: (0, 0, h)),
            ],
            scratch_shapes=[pltpu.VMEM((length, HD), F32)] * 2,
        ),
        out_shape=[jax.ShapeDtypeStruct((length, part), t) for t in (F32, F32, BF)]
        + [jax.ShapeDtypeStruct((2, 8, m), F32) for m in (length, part)],
        compiler_params=params(),
        cost_estimate=cost(10 * length * length * part, 24 << 20, length * length * heads),
        name="attend_back",
    )(me, *pieces, query, key, value, qkv, qkv, factors, q_gain[None], k_gain[None], *tables,
      seg[:, None], seg[None])


def mixed_back_kernel(me_ref, d_ref, w_ref, *refs):
    for p, out in enumerate(refs):

        @pl.when(pl.program_id(0) == p)
        def _(out=out):
            out[...] = nt_dot(d_ref[...], w_ref[...]).astype(BF)


def mixed_back(me, d_attn, w_first, count):
    tokens, width = d_attn.shape
    part = width // count
    piece = pl.BlockSpec((tokens, part), lambda p, me: (0, 0))
    return pl.pallas_call(
        mixed_back_kernel,
        grid_spec=pltpu.PrefetchScalarGridSpec(
            num_scalar_prefetch=1,
            grid=(count,),
            in_specs=[
                pl.BlockSpec((tokens, width), lambda p, me: (0, 0)),
                pl.BlockSpec((part, width), lambda p, me: ((me[0] + p) % count, 0)),
            ],
            out_specs=[piece] * count,
        ),
        out_shape=[jax.ShapeDtypeStruct((tokens, part), BF)] * count,
        compiler_params=params(),
        cost_estimate=cost(2 * tokens * width * width, 10 << 20),
        name="mixed_back",
    )(me, d_attn, w_first)


def input_back_kernel(part, order, q_ref, k_ref, v_ref, qp_ref, kp_ref, in_ref, f_ref, w_ref, d_ref, *outs):
    for j, (grad, proj) in enumerate(((q_ref, qp_ref), (k_ref, kp_ref))):
        factor = f_ref[:, j : j + 1]
        normed = proj[...] * factor
        low = ((grad[...] - normed * in_ref[:, j : j + 1]) * factor).astype(BF)
        d_ref[:, j * part : (j + 1) * part] = low
    d_ref[:, 2 * part :] = v_ref[...]
    total = nt_dot(d_ref[...], w_ref[...])
    for step, out in enumerate(outs):

        @pl.when(pl.program_id(0) == step)
        def _(out=out):
            out[...] = total.astype(out.dtype)


def input_back(d_query, d_key, d_v, qkv, inner, factors, w_qkv, count):
    length, part = d_query.shape
    width = w_qkv.shape[0]
    tokens = length // count
    place = lambda t: jnp.where(t == 0, 1, jnp.where(t == 1, 3, jnp.where(t == 2, 2, 0)))
    rows = lambda columns, at=0: pl.BlockSpec((tokens, columns), lambda t: (place(t), at))
    kinds = (BF, BF, F32, F32)
    return pl.pallas_call(
        functools.partial(input_back_kernel, part, None),
        grid=(count,),
        in_specs=[rows(part)] * 3
        + [rows(part), rows(part, 1), rows(2), rows(2)]
        + [once((width, 3 * part), lambda t: (0, 0))],
        out_specs=[rows(3 * part)] + [pl.BlockSpec((tokens, width), lambda t: (0, 0))] * count,
        out_shape=[jax.ShapeDtypeStruct((length, 3 * part), BF)]
        + [jax.ShapeDtypeStruct((tokens, width), kind) for kind in kinds],
        compiler_params=params(),
        cost_estimate=cost(6 * length * width * part, 24 << 20),
        name="input_back",
    )(d_query, d_key, d_v, qkv, qkv, inner, factors, w_qkv)


def cost(flops, moved, exps=0):
    return pl.CostEstimate(flops=flops, bytes_accessed=moved, transcendentals=exps)


def params():
    return pltpu.CompilerParams(vmem_limit_bytes=56 << 20)


def once(shape, index):
    return pl.BlockSpec(shape, index, pipeline_mode=pl.Buffered(1))


def nt_dot(left, right):
    return lax.dot_general(left, right, (((1,), (1,)), ((), ())), preferred_element_type=F32)


def qkv_kernel(count, part, me_ref, *refs):
    chunks, (w_ref, x_ref, qkv_ref, sq_ref) = refs[:-4], refs[-4:]
    ones = jnp.ones((8, part), F32)
    for q in range(count):

        @pl.when(pl.program_id(0) == q)
        def _(q=q):
            x = chunks[q][...]
            x_ref[...] = x
            qkv = jnp.dot(x, w_ref[...], preferred_element_type=F32)
            qkv_ref[...] = qkv
            for j in range(2):
                values = qkv[:, j * part : (j + 1) * part]
                sq_ref[j] = lax.dot_general(
                    ones, values * values, (((1,), (1,)), ((), ())),
                    precision=lax.Precision.HIGHEST, preferred_element_type=F32,
                )


def qkv_project(me, chunks, w_qkv):
    count = len(chunks)
    tokens, width = chunks[0].shape
    columns = w_qkv.shape[1]
    length = count * tokens
    return pl.pallas_call(
        functools.partial(qkv_kernel, count, columns // 3),
        grid_spec=pltpu.PrefetchScalarGridSpec(
            num_scalar_prefetch=1,
            grid=(count,),
            in_specs=[once((tokens, width), lambda q, me: (0, 0))] * count
            + [once((width, columns), lambda q, me: (0, 0))],
            out_specs=[
                pl.BlockSpec((tokens, width), lambda q, me: (q, 0)),
                pl.BlockSpec((tokens, columns), lambda q, me: (q, 0)),
                pl.BlockSpec((2, 8, tokens), lambda q, me: (0, 0, q)),
            ],
        ),
        out_shape=[
            jax.ShapeDtypeStruct((length, width), BF),
            jax.ShapeDtypeStruct((length, columns), F32),
            jax.ShapeDtypeStruct((2, 8, length), F32),
        ],
        compiler_params=params(),
        cost_estimate=cost(2 * length * width * columns, 20 << 20),
        name="qkv_project",
    )(me, *chunks, w_qkv)


FF_TILE = 512


def ff_finish(step, product, acc, outs):
    @pl.when(step == 0)
    def _():
        acc[...] = product

    @pl.when(step > 0)
    def _():
        acc[...] += product

    @pl.when(step == pl.num_programs(0) - 1)
    def _():
        tokens = acc.shape[0] // len(outs)
        for j, out in enumerate(outs):
            out[...] = acc[j * tokens : (j + 1) * tokens].astype(out.dtype)


def ff_kernel(saved, h_ref, wg_ref, wu_ref, wd_ref, *refs):
    gate_ref, up_ref, hid_ref = refs[saved : saved + 3]
    h = h_ref[...]
    gate = jnp.dot(h, wg_ref[...], preferred_element_type=F32)
    up = jnp.dot(h, wu_ref[...], preferred_element_type=F32)
    hidden = (gate * (1.0 / (1.0 + jnp.exp(-gate))) * up).astype(BF)
    gate_ref[...] = gate
    up_ref[...] = up
    hid_ref[...] = hidden
    ff_finish(pl.program_id(0), nt_dot(hidden, wd_ref[...]), refs[-1], refs[saved + 3 : -1])


def ff_back_kernel(saved, d_ref, wg_ref, wu_ref, wd_ref, gate_ref, up_ref, *refs):
    dgu_ref = refs[saved]
    tile = wg_ref.shape[1]
    d_hidden = jnp.dot(d_ref[...], wd_ref[...], preferred_element_type=F32)
    gate = gate_ref[...]
    sig = 1.0 / (1.0 + jnp.exp(-gate))
    d_gate = (d_hidden * up_ref[...] * sig * (1.0 + gate * (1.0 - sig))).astype(BF)
    d_up = (d_hidden * gate * sig).astype(BF)
    dgu_ref[:, :tile] = d_gate
    dgu_ref[:, tile:] = d_up
    product = nt_dot(d_gate, wg_ref[...]) + nt_dot(d_up, wu_ref[...])
    ff_finish(pl.program_id(0), product, refs[-1], refs[saved + 1 : -1])


def ff_specs(width, tile, gate_at, down_at):
    return [
        pl.BlockSpec((width, tile), lambda t: (0, gate_at // tile + t)),
        pl.BlockSpec((width, tile), lambda t: (0, t)),
        pl.BlockSpec((width, tile), lambda t: (0, down_at // tile + t)),
    ]


def ff_forward(residual_all, w_first, w_second, place, kinds, saved=()):
    length, width = residual_all.shape
    tokens = length // 4
    rows = len(kinds) * tokens
    ff_part = w_second.shape[1] // 2
    tile = min(FF_TILE, ff_part)
    block = pl.BlockSpec((rows, tile), lambda t: (place // len(kinds), t))
    whole = pl.BlockSpec((tokens, width), lambda t: (0, 0))
    shape = lambda kind: jax.ShapeDtypeStruct((length, ff_part), kind)
    return pl.pallas_call(
        functools.partial(ff_kernel, len(saved)),
        grid=(ff_part // tile,),
        in_specs=[once((rows, width), lambda t: (place // len(kinds), 0))]
        + ff_specs(width, tile, w_first.shape[1] - ff_part, ff_part)
        + [pl.BlockSpec(memory_space=pl.ANY)] * len(saved),
        out_specs=[block] * 3 + [whole] * len(kinds),
        out_shape=[shape(F32), shape(F32), shape(BF)]
        + [jax.ShapeDtypeStruct((tokens, width), kind) for kind in kinds],
        scratch_shapes=[pltpu.VMEM((rows, width), F32)],
        input_output_aliases={4 + j: j for j in range(len(saved))},
        compiler_params=params(),
        cost_estimate=cost(6 * rows * width * ff_part, 40 << 20, rows * ff_part),
        name="ff_forward",
    )(residual_all, w_first, w_second, w_second, *saved)


def ff_backward(d_ff, w_first, w_second, gate, up, place, kinds, saved=()):
    rows, width = d_ff.shape
    length = gate.shape[0]
    tokens = length // 4
    ff_part = w_second.shape[1] // 2
    tile = min(FF_TILE, ff_part)
    block = pl.BlockSpec((rows, tile), lambda t: (place // len(kinds), t))
    whole = pl.BlockSpec((tokens, width), lambda t: (0, 0))
    return pl.pallas_call(
        functools.partial(ff_back_kernel, len(saved)),
        grid=(ff_part // tile,),
        in_specs=[once((rows, width), lambda t: (0, 0))]
        + ff_specs(width, tile, w_first.shape[1] - ff_part, ff_part)
        + [block, block]
        + [pl.BlockSpec(memory_space=pl.ANY)] * len(saved),
        out_specs=[pl.BlockSpec((rows, 2 * tile), lambda t: (place // len(kinds), t))]
        + [whole] * len(kinds),
        out_shape=[jax.ShapeDtypeStruct((length, 2 * ff_part), BF)]
        + [jax.ShapeDtypeStruct((tokens, width), kind) for kind in kinds],
        scratch_shapes=[pltpu.VMEM((rows, width), F32)],
        input_output_aliases={6 + j: j for j in range(len(saved))},
        compiler_params=params(),
        cost_estimate=cost(6 * rows * width * ff_part, 40 << 20, rows * ff_part),
        name="ff_backward",
    )(d_ff, w_first, w_second, w_second, gate, up, *saved)


def out_kernel(count, part, *refs):
    me_ref, pieces, (w_ref, x_ref, g_ref, res_ref, own_ref) = refs[0], refs[1:-5], refs[-5:]
    total = None
    for p, piece in enumerate(pieces):
        rows = pl.ds(pl.multiple_of((me_ref[0] + p) % count * part, part), part)
        product = jnp.dot(piece[...], w_ref[rows, :], preferred_element_type=F32)
        total = product if total is None else total + product
    normed = total * inv_rms(total)
    res_ref[...] = (x_ref[...].astype(F32) + normed * g_ref[...]).astype(BF)

    @pl.when(pl.program_id(0) == 0)
    def _():
        own_ref[...] = total


def ff_place(q):
    return jnp.where(q == 0, 3, jnp.where(q == 3, 1, jnp.where(q == 2, 2, 0)))


def out_project(me, pieces, w_out, x_all, gain, count):
    length, width = x_all.shape
    tokens = length // count
    part = pieces[0].shape[1]
    rolled = lambda p: pl.BlockSpec((tokens, part), lambda q, me: ((q + count - p) % count, 0))
    chunk = pl.BlockSpec((tokens, width), lambda q, me: (q, 0))
    moved = pl.BlockSpec((tokens, width), lambda q, me: (ff_place(q), 0))
    return pl.pallas_call(
        functools.partial(out_kernel, count, part),
        grid_spec=pltpu.PrefetchScalarGridSpec(
            num_scalar_prefetch=1,
            grid=(count,),
            in_specs=[rolled(p) for p in range(count)]
            + [pl.BlockSpec((width, width), lambda q, me: (0, 0), pipeline_mode=pl.Buffered(1))]
            + [chunk, pl.BlockSpec((1, width), lambda q, me: (0, 0))],
            out_specs=[moved, pl.BlockSpec((tokens, width), lambda q, me: (0, 0))],
        ),
        out_shape=[
            jax.ShapeDtypeStruct((length, width), BF),
            jax.ShapeDtypeStruct((tokens, width), F32),
        ],
        compiler_params=params(),
        cost_estimate=cost(2 * length * width * width, 22 << 20),
        name="out_project",
    )(me, *pieces, w_out, x_all, gain[None])


def roll_blocks(values, first):
    n = values.shape[0]
    return lax.dynamic_slice_in_dim(jnp.concatenate([values, values]), first, n, 0)


def columns_to_parts(values, me, count):
    part = values.shape[1] // count
    columns = lambda p: lax.dynamic_slice_in_dim(values, (me + p) % count * part, part, 1)
    got = [columns(0)] + [
        lax.ppermute(columns(p), "seq", [(i, (i + p) % count) for i in range(count)])
        for p in range(1, count)
    ]
    return jnp.concatenate([got[(count - q) % count] for q in range(count)], axis=0)


def build(dp_count, seq_count):
    assert seq_count == 4

    def shards(
        layer_input,
        segments,
        w_query,
        w_key,
        w_value,
        w_output,
        w_gate,
        w_up,
        w_down,
        query_gain,
        key_gain,
        attn_gain,
        ff_gain,
        cotangent,
    ):
        n = seq_count
        tokens, width = layer_input.shape[1:]
        shard_rows = w_query.shape[0]
        part = width // n
        ff_part = w_gate.shape[1] // n
        length = n * tokens
        devices = dp_count * n
        me = lax.axis_index("seq")
        me_ref = me[None].astype(jnp.int32)
        cot = cotangent[0]
        chunks = lambda v: [v[p * tokens : (p + 1) * tokens] for p in range(n)]
        by_part = lambda w: w.reshape(shard_rows, n, -1).transpose(1, 0, 2)
        rows_of = lambda blocks: blocks.reshape(n * shard_rows, -1)

        fence = lax.optimization_barrier
        qkv_blocks = jnp.concatenate([by_part(w) for w in (w_query, w_key, w_value)], axis=2)
        qkv_blocks = swap_blocks(qkv_blocks)
        w_qkv = gather_dp(rows_of(qkv_blocks))
        qkv_blocks, w_output, w_gate, w_down_t = fence((qkv_blocks, w_output, w_gate, w_down.T))
        out_blocks = gather_cyclic(w_output, n)
        gate_blocks = send_columns(w_gate, me, n)
        out_blocks, gate_blocks, x_own = fence((out_blocks, gate_blocks, layer_input[0]))
        out_blocks = out_blocks[:1] + out_blocks[:0:-1]
        w_first = place_blocks(out_blocks, me, 0, width + ff_part)
        w_first = gather_dp(place_blocks(gate_blocks, me, width, width + ff_part, w_first))
        x_chunks, w_up = fence((gather_cyclic(x_own, n), w_up))
        up_blocks = send_columns(w_up, me, n)
        x_all, qkv, squares = qkv_project(me_ref, x_chunks, w_qkv)
        squares, up_blocks = fence((squares, up_blocks))

        natural = jnp.arange(length, dtype=jnp.int32)
        positions = (natural + me * tokens) % length
        seg_row = segments[0]
        seg = lax.dynamic_slice_in_dim(
            jnp.concatenate([seg_row, seg_row]), me * tokens, length, 0
        )
        tables = rope_tables(positions.astype(F32))
        own_gain = lambda g: lax.dynamic_slice_in_dim(g, me * part, part, 0)
        q_gain = own_gain(query_gain)
        k_gain = own_gain(key_gain)

        squares = sum_stats(squares[:, 0].reshape(2, n, tokens), n).reshape(2, length)
        squares, w_down_t = fence((squares, w_down_t))
        down_blocks = send_columns(w_down_t, me, n)
        factors = lax.rsqrt(squares / width + EPSILON).T
        mixed, q_low, k_low, v_low = attend(me_ref, qkv, factors, q_gain, k_gain, tables, seg, n)

        mixed, down_blocks = fence((mixed, down_blocks))
        w_second = place_blocks(up_blocks, me, 0, 2 * ff_part)
        w_second = gather_dp(place_blocks(down_blocks, me, ff_part, 2 * ff_part, w_second))
        pieces = gather_cyclic(mixed, n)
        residual_all, attn_out = out_project(me_ref, pieces, w_first, x_all, attn_gain, n)
        attn_factor = inv_rms(attn_out)
        attn_normed = attn_out * attn_factor
        residual = x_own.astype(F32) + attn_normed * attn_gain

        *saved, after, before, far = ff_forward(
            residual_all, w_first, w_second, 0, (BF, BF, F32)
        )
        sent = scatter_start(after, before, n)
        residual_late, first_sent = fence((residual_all, sent[0]))
        gate, up, hidden, own = ff_forward(residual_late, w_first, w_second, 3, (F32,), saved)
        ff_out = scatter_end(own, sent[1:] + [scatter_far(far, first_sent, n)])
        ff_factor = inv_rms(ff_out)
        ff_normed = ff_out * ff_factor
        activation = (residual + ff_normed * ff_gain).astype(BF)
        grad_ff_gain = jnp.sum(cot.astype(F32) * ff_normed, axis=0)
        d_ff = rms_back(ff_normed, ff_factor, ff_gain, cot.astype(F32)).astype(BF)
        d_ffs = gather_cyclic(d_ff, n)
        d_both, own = ff_backward(d_ffs[0], w_first, w_second, gate, up, 3, (F32,))
        d_ffs, d_both = fence((d_ffs, d_both))
        d_ff_near = jnp.concatenate([d_ffs[1], d_ffs[3]], axis=0)
        d_both, after, before = ff_backward(
            d_ff_near, w_first, w_second, gate, up, 0, (BF, BF), (d_both,)
        )
        after, before, d_ffs, hidden = fence((after, before, d_ffs, hidden))
        sent = scatter_start(after, before, n)
        d_ff_all = jnp.concatenate([d_ff_near, d_ffs[2], d_ffs[0]], axis=0)
        down_grad = rows_product(d_ff_all, hidden).astype(BF)
        down_rows = scatter_dp(down_grad)
        d_ff_far, down_grad = fence((d_ffs[2], down_grad))
        d_both, far = ff_backward(d_ff_far, w_first, w_second, gate, up, 2, (F32,), (d_both,))
        d_both, far, sent[0] = fence((d_both, far, sent[0]))
        sent[0] = scatter_far(far, sent[0], n)
        joined = lambda g: g.transpose(1, 0, 2).reshape(shard_rows, -1).astype(F32)
        gate_up_grad = rows_product(residual_all, d_both).astype(BF)
        gate_up_grad, sent = fence((gate_up_grad, sent))
        gate_up_rows = scatter_dp(gate_up_grad)
        d_res = cot.astype(F32) + scatter_end(own, sent)

        grad_attn_gain = jnp.sum(d_res * attn_normed, axis=0)
        d_attn = rms_back(attn_normed, attn_factor, attn_gain, d_res).astype(BF)
        d_pieces = mixed_back(me_ref, d_attn, w_first, n)
        d_mixed = [d_pieces[0]] + [None] * (n - 1)
        for p in range(1, n):
            d_mixed[n - p] = lax.ppermute(
                d_pieces[p], "seq", [(i, (i + p) % n) for i in range(n)]
            )
        d_mixed, d_attn, down_rows = fence((d_mixed, d_attn, down_rows))
        d_attn_part = columns_to_parts(d_attn, me, n)
        d_query, d_key, d_v, inner, gain_sums = attend_back(
            me_ref, d_mixed, q_low, k_low, v_low, qkv, factors, q_gain, k_gain, tables, seg, n
        )
        inner, d_attn_part = fence((inner, d_attn_part))
        inner = sum_stats(inner[:, 0].reshape(2, n, tokens), n).reshape(2, length)
        inner, down_rows = fence((inner, down_rows))
        down_back = send_rows(down_rows, me, n)
        d_qkv, after, before, far, own = input_back(
            d_query, d_key, d_v, qkv, (inner / width).T, factors, w_qkv, n
        )
        after, before, far, own, d_qkv, down_back = fence(
            (after, before, far, own, d_qkv, down_back)
        )
        sent = scatter_start(after, before, n)
        qkv_grad = rows_product(x_all, d_qkv).astype(BF)
        sent, qkv_grad = fence((sent, qkv_grad))
        sent[0] = scatter_far(far, sent[0], n)
        out_grads = [
            rows_product(piece, jnp.roll(d_attn_part, -p * tokens, axis=0)).astype(BF)
            for p, piece in enumerate(pieces)
        ]
        out_grad = roll_blocks(jnp.stack(out_grads), (n - me) % n).reshape(width, part)
        attn_grads = jnp.concatenate([qkv_grad, out_grad], axis=1)
        attn_rows = scatter_dp(attn_grads)
        input_grad = d_res + scatter_end(own, sent)
        spread = lambda g: lax.dynamic_update_slice(jnp.zeros(width, F32), g, (me * part,))
        gains = jnp.stack(
            [spread(gain_sums[0, 0]), spread(gain_sums[1, 0]), grad_attn_gain, grad_ff_gain]
        )
        input_grad, gate_up_rows, gains = fence((input_grad, gate_up_rows, gains))
        gate_up_back = send_rows(gate_up_rows, me, n)
        gains = sum_everywhere(gains, dp_count, n)
        attn_rows, input_grad, gate_up_back, down_back, gains = fence(
            (attn_rows, input_grad, gate_up_back, down_back, gains)
        )
        attn_back = swap_blocks(attn_rows.reshape(n, shard_rows, -1))
        by_tile = [b.reshape(shard_rows, -1, 2, min(FF_TILE, ff_part)) for b in gate_up_back]
        grad_gate, grad_up = (
            join_columns([b[:, :, j].reshape(shard_rows, ff_part) for b in by_tile], me)
            for j in range(2)
        )
        grad_down = join_columns(down_back, me).T
        grad_query, grad_key, grad_value, grad_output = (
            joined(attn_back[:, :, j * part : (j + 1) * part]) for j in range(4)
        )

        share = width // devices
        gains = lax.dynamic_slice_in_dim(
            gains, (lax.axis_index("dp") * n + me) * share, share, 1
        )
        return (
            activation[None],
            input_grad.astype(BF)[None],
            grad_query,
            grad_key,
            grad_value,
            grad_output,
            grad_gate,
            grad_up,
            grad_down,
            gains[0],
            gains[1],
            gains[2],
            gains[3],
        )

    return shards


def solution(mesh):
    both = P(("dp", "seq"), None)
    tokens = P("dp", "seq", None)
    columns = P(None, ("dp", "seq"))
    gain = P(("dp", "seq"))
    return jax.shard_map(
        build(mesh.shape["dp"], mesh.shape["seq"]),
        mesh=mesh,
        in_specs=(tokens, P("dp", None)) + (both,) * 6 + (columns,) + (P(),) * 4 + (tokens,),
        out_specs=(tokens, tokens) + (both,) * 6 + (columns,) + (gain,) * 4,
        check_vma=False,
    )
```

```python
import functools

import jax
import jax.numpy as jnp
from jax import lax
from jax.experimental import pallas as pl
from jax.experimental.pallas import tpu as pltpu
from jax.sharding import PartitionSpec as P

HD = 128
EPSILON = 1e-06
ROPE_BASE = 500000.0
MASKED = -1e30
LOG2E = 1.4426950408889634
BF = jnp.bfloat16
F32 = jnp.float32


def inv_rms(values):
    return lax.rsqrt(jnp.mean(values * values, axis=-1, keepdims=True) + EPSILON)


def rms_back(normed, factor, gain, grad):
    scaled = grad * gain
    inner = jnp.mean(scaled * normed, axis=-1, keepdims=True)
    return (scaled - normed * inner) * factor


def rope_tables(positions):
    half_dim = HD // 2
    frequency = jnp.power(F32(ROPE_BASE), -jnp.arange(half_dim, dtype=F32) * (2.0 / HD))
    angles = positions[:, None] * frequency[None, :]
    cosine, sine = jnp.cos(angles), jnp.sin(angles)
    return (jnp.concatenate([cosine, cosine], axis=-1), jnp.concatenate([-sine, sine], axis=-1))


def shift(values, count, step):
    return lax.ppermute(values, "seq", [((i + step) % count, i) for i in range(count)])


def gather_cyclic(values, count):
    if count != 4:
        return [values] + [shift(values, count, p) for p in range(1, count)]
    me = lax.axis_index("seq")
    far = lax.ppermute(values, "seq", [(i ^ 2, i) for i in range(4)])
    after = lax.ppermute(values, "seq", [(i + 1, i) for i in range(3)])
    before = lax.ppermute(values, "seq", [(i, i + 1) for i in range(3)])
    ends = lax.ppermute(far, "seq", [(2, 3), (1, 0)])
    return [values, jnp.where(me == 3, ends, after), far, jnp.where(me == 0, ends, before)]


def scatter_start(ends, after, before, count):
    ends = lax.ppermute(ends, "seq", [(0, 1), (count - 1, count - 2)])
    step = [(i, i + 1) for i in range(count - 1)]
    after = lax.ppermute(after, "seq", step)
    before = lax.ppermute(before, "seq", [(j, i) for i, j in step])
    return [ends, after, before]


def scatter_far(far, ends, count):
    far_sum = (far + ends.astype(F32)).astype(BF)
    return lax.ppermute(far_sum, "seq", [(i, i ^ 2) for i in range(count)])


def scatter_end(own, got):
    for part in got:
        own = own + part.astype(F32)
    return own


def sum_stats(stats, count):
    total = stats
    for p in range(1, count):
        total = total + jnp.roll(shift(stats, count, p), p, axis=1)
    return total


def sum_everywhere(values, dp_count, seq_count):
    for name, count in (("dp", dp_count), ("seq", seq_count)):
        if count & (count - 1):
            values = lax.psum(values, name)
            continue
        bit = 1
        while bit < count:
            values = values + lax.ppermute(values, name, [(i, i ^ bit) for i in range(count)])
            bit *= 2
    return values


def swap_blocks(values):
    return lax.all_to_all(values, "seq", split_axis=0, concat_axis=0, tiled=True)


def send_columns(values, me, count):
    part = values.shape[1] // count
    columns = lambda p: lax.dynamic_slice_in_dim(values, (me + p) % count * part, part, 1)
    return [columns(0)] + [
        lax.ppermute(columns(p), "seq", [(i, (i + p) % count) for i in range(count)])
        for p in range(1, count)
    ]


def place_blocks(blocks, me, first, width, total=None):
    count = len(blocks)
    rows = blocks[0].shape[0]
    if total is None:
        total = jnp.zeros((count * rows, width), blocks[0].dtype)
    for p, block in enumerate(blocks):
        total = lax.dynamic_update_slice(total, block, ((me - p) % count * rows, first))
    return total


def send_rows(values, me, count):
    size = values.shape[0] // count
    rows = lambda p: lax.dynamic_slice_in_dim(values, (me + p) % count * size, size, 0)
    return [rows(0)] + [
        lax.ppermute(rows(p), "seq", [(i, (i + p) % count) for i in range(count)])
        for p in range(1, count)
    ]


def join_columns(blocks, me):
    count = len(blocks)
    rows, part = blocks[0].shape
    total = jnp.zeros((rows, count * part), F32)
    for p, block in enumerate(blocks):
        total = lax.dynamic_update_slice(total, block.astype(F32), (0, (me - p) % count * part))
    return total


def gather_dp(values):
    return lax.all_gather(values, "dp", axis=0, tiled=True)


def scatter_dp(values):
    return lax.psum_scatter(values, "dp", scatter_dimension=0, tiled=True)


def softmax_window(q, k_ref, seg_q, seg_row_ref, valid_from, place, tokens, count, span):
    parts = []
    for w in range(span):
        at = ((place - w) % count) * tokens
        scores = lax.dot_general(
            q, k_ref[at : at + tokens, :], (((1,), (1,)), ((), ())), preferred_element_type=F32
        )
        seg = seg_q if w == 0 else jnp.where(valid_from >= w, seg_q, -1)
        allowed = seg == seg_row_ref[:, at : at + tokens]
        if w == 0:
            rows = lax.broadcasted_iota(jnp.int32, (tokens, tokens), 0)
            cols = lax.broadcasted_iota(jnp.int32, (tokens, tokens), 1)
            allowed = allowed & (cols <= rows)
        parts.append(jnp.where(allowed, scores, MASKED))
    top = parts[0]
    for part in parts[1:]:
        top = jnp.maximum(top, part)
    top = jnp.max(top, axis=-1, keepdims=True)
    exps = [jnp.exp2((part - top) * (HD**-0.5 * LOG2E)) for part in parts]
    total = exps[0]
    for part in exps[1:]:
        total = total + part
    inverse = 1.0 / jnp.sum(total, axis=-1, keepdims=True)
    return [part * inverse for part in exps]


def turn(values, cosine, sine):
    return values * cosine + pltpu.roll(values, HD // 2, 1) * sine


def attend_kernel(
    tokens, count, span,
    me_ref, q_ref, k_ref, v_ref, f_ref, qg_ref, kg_ref, cos_ref, sin_ref, segc_ref, segr_ref,
    o_ref, qb_ref, kb_ref, vb_ref,
):
    cosine, sine = cos_ref[...], sin_ref[...]
    factors = f_ref[...]
    qb_ref[...] = turn(q_ref[...] * factors[:, 0:1] * qg_ref[...], cosine, sine).astype(BF)
    kb_ref[...] = turn(k_ref[...] * factors[:, 1:2] * kg_ref[...], cosine, sine).astype(BF)
    vb_ref[...] = v_ref[...].astype(BF)
    for place in range(count):
        rows = slice(place * tokens, (place + 1) * tokens)
        chunk = (me_ref[0] + place) % count
        probs = softmax_window(
            qb_ref[rows, :], kb_ref, segc_ref[rows, :], segr_ref, chunk, place, tokens, count, span
        )
        mixed = None
        for w in range(span):
            at = ((place - w) % count) * tokens
            part = jnp.dot(probs[w].astype(BF), vb_ref[at : at + tokens, :], preferred_element_type=F32)
            mixed = part if mixed is None else mixed + part
        o_ref[rows, :] = mixed.astype(BF)


def attend_back_kernel(
    tokens, count, span, me_ref, *refs
):
    grads_in = refs[:count]
    (q_ref, k_ref, v_ref, qp_ref, kp_ref, f_ref, qg_ref, kg_ref, cos_ref, sin_ref, segc_ref, segr_ref,
     dq_ref, dk_ref, dv_ref, inner_ref, gain_ref, dk_sum, dv_sum) = refs[count:]
    scale = HD**-0.5
    dk_sum[...] = jnp.zeros_like(dk_sum)
    dv_sum[...] = jnp.zeros_like(dv_sum)
    for place in range(count):
        rows = slice(place * tokens, (place + 1) * tokens)
        chunk = (me_ref[0] + place) % count
        q = q_ref[rows, :]
        grad = grads_in[place][...]
        probs = softmax_window(
            q, k_ref, segc_ref[rows, :], segr_ref, chunk, place, tokens, count, span
        )
        grads = []
        inner = None
        for w in range(span):
            at = ((place - w) % count) * tokens
            part = nt_dot(grad, v_ref[at : at + tokens, :])
            grads.append(part)
            inner = probs[w] * part if inner is None else inner + probs[w] * part
            dv_sum[at : at + tokens, :] += lax.dot_general(
                probs[w].astype(BF), grad, (((0,), (0,)), ((), ())), preferred_element_type=F32
            )
        inner = jnp.sum(inner, axis=-1, keepdims=True)
        dq = None
        for w in range(span):
            at = ((place - w) % count) * tokens
            ds = (probs[w] * (grads[w] - inner)).astype(BF)
            part = jnp.dot(ds, k_ref[at : at + tokens, :], preferred_element_type=F32)
            dq = part if dq is None else dq + part
            dk_sum[at : at + tokens, :] += lax.dot_general(
                ds, q, (((0,), (0,)), ((), ())), preferred_element_type=F32
            )
        dq_ref[rows, :] = dq
    ones = jnp.ones((8, HD), F32)
    first = pl.program_id(0) == 0
    sides = ((dq_ref, dq_ref, qp_ref, qg_ref), (dk_sum, dk_ref, kp_ref, kg_ref))
    for j, (raw_ref, out_ref, proj_ref, g_ref) in enumerate(sides):
        raw = (raw_ref[...] * scale).astype(BF).astype(F32)
        back = turn(raw, cos_ref[...], -sin_ref[...])
        normed = proj_ref[...] * f_ref[:, j : j + 1]
        gain_ref[j] = jnp.broadcast_to(jnp.sum(back * normed, axis=0, keepdims=True), (8, HD))
        back = back * g_ref[...]
        out_ref[...] = back
        sums = lax.dot_general(
            ones, back * normed, (((1,), (1,)), ((), ())),
            precision=lax.Precision.HIGHEST, preferred_element_type=F32,
        )
        inner_ref[j] = jnp.where(first, sums, inner_ref[j] + sums)
    dv_ref[...] = dv_sum[...].astype(BF)


def attend_specs(length, heads):
    head = lambda j: pl.BlockSpec((length, HD), lambda h, me: (0, j * heads + h))
    whole = lambda *shape: pl.BlockSpec(shape, lambda h, me: (0, 0))
    gain = pl.BlockSpec((1, HD), lambda h, me: (0, h))
    return head, whole, gain


def attend(me, qkv, factors, q_gain, k_gain, tables, seg, count):
    length = qkv.shape[0]
    part = qkv.shape[1] // 3
    heads = part // HD
    tokens = length // count
    span = min(count, (length // 2 - 1 + tokens - 1) // tokens + 1)
    head, whole, gain = attend_specs(length, heads)
    low = jax.ShapeDtypeStruct((length, part), BF)
    return pl.pallas_call(
        functools.partial(attend_kernel, tokens, count, span),
        grid_spec=pltpu.PrefetchScalarGridSpec(
            num_scalar_prefetch=1,
            grid=(heads,),
            in_specs=[head(0), head(1), head(2), whole(length, 2), gain, gain]
            + [whole(length, HD)] * 2
            + [whole(length, 1), whole(1, length)],
            out_specs=[head(0)] * 4,
        ),
        out_shape=[low] * 4,
        compiler_params=params(),
        cost_estimate=cost(4 * length * length * part, 16 << 20, length * length * heads),
        name="attend",
    )(me, qkv, qkv, qkv, factors, q_gain[None], k_gain[None], *tables, seg[:, None], seg[None])


def attend_back(me, pieces, query, key, value, qkv, factors, q_gain, k_gain, tables, seg, count):
    length, part = query.shape
    heads = part // HD
    tokens = length // count
    span = min(count, (length // 2 - 1 + tokens - 1) // tokens + 1)
    head, whole, gain = attend_specs(length, heads)
    return pl.pallas_call(
        functools.partial(attend_back_kernel, tokens, count, span),
        grid_spec=pltpu.PrefetchScalarGridSpec(
            num_scalar_prefetch=1,
            grid=(heads,),
            in_specs=[pl.BlockSpec((tokens, HD), lambda h, me: (0, h))] * count
            + [head(0)] * 3
            + [head(0), head(1), whole(length, 2), gain, gain]
            + [whole(length, HD)] * 2
            + [whole(length, 1), whole(1, length)],
            out_specs=[head(0)] * 3
            + [
                pl.BlockSpec((2, 8, length), lambda h, me: (0, 0, 0)),
                pl.BlockSpec((2, 8, HD), lambda h, me: (0, 0, h)),
            ],
            scratch_shapes=[pltpu.VMEM((length, HD), F32)] * 2,
        ),
        out_shape=[jax.ShapeDtypeStruct((length, part), t) for t in (F32, F32, BF)]
        + [jax.ShapeDtypeStruct((2, 8, m), F32) for m in (length, part)],
        compiler_params=params(),
        cost_estimate=cost(10 * length * length * part, 24 << 20, length * length * heads),
        name="attend_back",
    )(me, *pieces, query, key, value, qkv, qkv, factors, q_gain[None], k_gain[None], *tables,
      seg[:, None], seg[None])


def mixed_back_kernel(me_ref, d_ref, w_ref, *refs):
    for p, out in enumerate(refs):

        @pl.when(pl.program_id(0) == p)
        def _(out=out):
            out[...] = nt_dot(d_ref[...], w_ref[...]).astype(BF)


def mixed_back(me, d_attn, w_first, count):
    tokens, width = d_attn.shape
    part = width // count
    piece = pl.BlockSpec((tokens, part), lambda p, me: (0, 0))
    return pl.pallas_call(
        mixed_back_kernel,
        grid_spec=pltpu.PrefetchScalarGridSpec(
            num_scalar_prefetch=1,
            grid=(count,),
            in_specs=[
                pl.BlockSpec((tokens, width), lambda p, me: (0, 0)),
                pl.BlockSpec((part, width), lambda p, me: ((me[0] + p) % count, 0)),
            ],
            out_specs=[piece] * count,
        ),
        out_shape=[jax.ShapeDtypeStruct((tokens, part), BF)] * count,
        compiler_params=params(),
        cost_estimate=cost(2 * tokens * width * width, 10 << 20),
        name="mixed_back",
    )(me, d_attn, w_first)


def input_back_kernel(
    part, me_ref, q_ref, k_ref, v_ref, qp_ref, kp_ref, in_ref, f_ref, w_ref, d_ref, ends_ref, *outs
):
    for j, (grad, proj) in enumerate(((q_ref, qp_ref), (k_ref, kp_ref))):
        factor = f_ref[:, j : j + 1]
        normed = proj[...] * factor
        low = ((grad[...] - normed * in_ref[:, j : j + 1]) * factor).astype(BF)
        d_ref[:, j * part : (j + 1) * part] = low
    d_ref[:, 2 * part :] = v_ref[...]
    total = nt_dot(d_ref[...], w_ref[...])
    for step, out in enumerate(outs):

        @pl.when(pl.program_id(0) == step)
        def _(out=out):
            out[...] = total.astype(out.dtype)

    @pl.when((pl.program_id(0) == 0) | ((pl.program_id(0) == 1) & (me_ref[0] == 0)))
    def _():
        ends_ref[...] = total.astype(BF)


def input_back(me, d_query, d_key, d_v, qkv, inner, factors, w_qkv, count):
    length, part = d_query.shape
    width = w_qkv.shape[0]
    tokens = length // count
    place = lambda t: jnp.where(t == 0, 1, jnp.where(t == 1, 3, jnp.where(t == 2, 2, 0)))
    rows = lambda columns, at=0: pl.BlockSpec((tokens, columns), lambda t, me: (place(t), at))
    kinds = (BF, BF, BF, F32, F32)
    return pl.pallas_call(
        functools.partial(input_back_kernel, part),
        grid_spec=pltpu.PrefetchScalarGridSpec(
            num_scalar_prefetch=1,
            grid=(count,),
            in_specs=[rows(part)] * 3
            + [rows(part), rows(part, 1), rows(2), rows(2)]
            + [once((width, 3 * part), lambda t, me: (0, 0))],
            out_specs=[rows(3 * part)]
            + [pl.BlockSpec((tokens, width), lambda t, me: (0, 0))] * len(kinds),
        ),
        out_shape=[jax.ShapeDtypeStruct((length, 3 * part), BF)]
        + [jax.ShapeDtypeStruct((tokens, width), kind) for kind in kinds],
        compiler_params=params(),
        cost_estimate=cost(6 * length * width * part, 24 << 20),
        name="input_back",
    )(me, d_query, d_key, d_v, qkv, qkv, inner, factors, w_qkv)


def tn_dot(left, right):
    return lax.dot_general(left, right, (((0,), (0,)), ((), ())), preferred_element_type=F32)


def weight_grad_kernel(lefts, right_ref, out_ref):
    total, at = None, 0
    for left in lefts:
        rows = left.shape[0]
        product = tn_dot(left[...], right_ref[at : at + rows, :])
        total = product if total is None else total + product
        at += rows
    out_ref[...] = total.astype(BF)


def weight_grad(lefts, right):
    width = lefts[0].shape[1]
    length, columns = right.shape
    tile, wide = 256, min(columns, 2048)
    return pl.pallas_call(
        lambda *refs: weight_grad_kernel(refs[:-2], *refs[-2:]),
        grid=(columns // wide, width // tile),
        in_specs=[pl.BlockSpec((left.shape[0], tile), lambda j, i: (0, i)) for left in lefts]
        + [pl.BlockSpec((length, wide), lambda j, i: (0, j))],
        out_specs=pl.BlockSpec((tile, wide), lambda j, i: (i, j)),
        out_shape=jax.ShapeDtypeStruct((width, columns), BF),
        compiler_params=params(),
        cost_estimate=cost(2 * length * width * columns, 2 * (length + width) * columns),
        name="weight_grad",
    )(*lefts, right)


def attn_grad_kernel(count, me_ref, x_ref, d_ref, *refs):
    pieces, parts, out_ref = refs[:count], refs[count : 2 * count], refs[-1]
    columns = d_ref.shape[1]
    out_ref[:, :columns] = tn_dot(x_ref[...], d_ref[...]).astype(BF)
    source = (pl.program_id(0) // (pl.num_programs(0) // count) + count - me_ref[0]) % count
    for p, piece in enumerate(pieces):

        @pl.when(source == p)
        def _(p=p, piece=piece):
            total, tokens = None, parts[0].shape[0]
            for q in range(count):
                rows = slice(q * tokens, (q + 1) * tokens)
                product = tn_dot(piece[rows, :], parts[(q + p) % count][...])
                total = product if total is None else total + product
            out_ref[:, columns:] = total.astype(BF)


def attn_grad(me, x_all, d_qkv, pieces, d_parts):
    count = len(pieces)
    length, width = x_all.shape
    columns, part = d_qkv.shape[1], d_parts[0].shape[1]
    tile = min(256, part)
    per_part = part // tile
    return pl.pallas_call(
        functools.partial(attn_grad_kernel, count),
        grid_spec=pltpu.PrefetchScalarGridSpec(
            num_scalar_prefetch=1,
            grid=(width // tile,),
            in_specs=[
                pl.BlockSpec((length, tile), lambda i, me: (0, i)),
                once((length, columns), lambda i, me: (0, 0)),
            ]
            + [pl.BlockSpec((length, tile), lambda i, me: (0, i % per_part))] * count
            + [once((length // count, part), lambda i, me: (0, 0))] * count,
            out_specs=pl.BlockSpec((tile, columns + part), lambda i, me: (i, 0)),
        ),
        out_shape=jax.ShapeDtypeStruct((width, columns + part), BF),
        compiler_params=params(),
        cost_estimate=cost(2 * length * width * (columns + part), 20 << 20),
        name="attn_grad",
    )(me, x_all, d_qkv, *pieces, *d_parts)


def cost(flops, moved, exps=0):
    return pl.CostEstimate(flops=flops, bytes_accessed=moved, transcendentals=exps)


def params():
    return pltpu.CompilerParams(vmem_limit_bytes=56 << 20)


def once(shape, index):
    return pl.BlockSpec(shape, index, pipeline_mode=pl.Buffered(1))


def nt_dot(left, right):
    return lax.dot_general(left, right, (((1,), (1,)), ((), ())), preferred_element_type=F32)


def qkv_kernel(count, part, me_ref, *refs):
    chunks, (w_ref, x_ref, qkv_ref, sq_ref) = refs[:-4], refs[-4:]
    ones = jnp.ones((8, part), F32)
    for q in range(count):

        @pl.when(pl.program_id(0) == q)
        def _(q=q):
            x = chunks[q][...]
            x_ref[...] = x
            qkv = jnp.dot(x, w_ref[...], preferred_element_type=F32)
            qkv_ref[...] = qkv
            for j in range(2):
                values = qkv[:, j * part : (j + 1) * part]
                sq_ref[j] = lax.dot_general(
                    ones, values * values, (((1,), (1,)), ((), ())),
                    precision=lax.Precision.HIGHEST, preferred_element_type=F32,
                )


def qkv_project(me, chunks, w_qkv):
    count = len(chunks)
    tokens, width = chunks[0].shape
    columns = w_qkv.shape[1]
    length = count * tokens
    return pl.pallas_call(
        functools.partial(qkv_kernel, count, columns // 3),
        grid_spec=pltpu.PrefetchScalarGridSpec(
            num_scalar_prefetch=1,
            grid=(count,),
            in_specs=[once((tokens, width), lambda q, me: (0, 0))] * count
            + [once((width, columns), lambda q, me: (0, 0))],
            out_specs=[
                pl.BlockSpec((tokens, width), lambda q, me: (q, 0)),
                pl.BlockSpec((tokens, columns), lambda q, me: (q, 0)),
                pl.BlockSpec((2, 8, tokens), lambda q, me: (0, 0, q)),
            ],
        ),
        out_shape=[
            jax.ShapeDtypeStruct((length, width), BF),
            jax.ShapeDtypeStruct((length, columns), F32),
            jax.ShapeDtypeStruct((2, 8, length), F32),
        ],
        compiler_params=params(),
        cost_estimate=cost(2 * length * width * columns, 20 << 20),
        name="qkv_project",
    )(me, *chunks, w_qkv)


FF_TILE = 512


def ff_finish(step, product, acc, me_ref, outs):
    @pl.when(step == 0)
    def _():
        acc[...] = product

    @pl.when(step > 0)
    def _():
        acc[...] += product

    @pl.when(step == pl.num_programs(0) - 1)
    def _():
        tokens = outs[0].shape[0]
        for j, out in enumerate(outs[:2]):
            out[...] = acc[j * tokens : (j + 1) * tokens].astype(out.dtype)
        if len(outs) == 3:
            at = pl.multiple_of(jnp.where(me_ref[0] == 0, tokens, 0), tokens)
            outs[2][...] = acc[pl.ds(at, tokens), :].astype(BF)


def ff_kernel(saved, me_ref, h_ref, wg_ref, wu_ref, wd_ref, *refs):
    gate_ref, up_ref, hid_ref = refs[saved : saved + 3]
    h = h_ref[...]
    gate = jnp.dot(h, wg_ref[...], preferred_element_type=F32)
    up = jnp.dot(h, wu_ref[...], preferred_element_type=F32)
    hidden = (gate * (1.0 / (1.0 + jnp.exp(-gate))) * up).astype(BF)
    gate_ref[...] = gate
    up_ref[...] = up
    hid_ref[...] = hidden
    product = nt_dot(hidden, wd_ref[...])
    ff_finish(pl.program_id(0), product, refs[-1], me_ref, refs[saved + 3 : -1])


def ff_back_kernel(saved, groups, me_ref, *refs):
    d_refs, (wg_ref, wu_ref, wd_ref, gate_ref, up_ref) = refs[:groups], refs[groups : groups + 5]
    refs = refs[groups + 5 :]
    dgu_ref = refs[saved]
    tile = wg_ref.shape[1]
    d_ff = d_refs[0][...] if groups == 1 else jnp.concatenate([d[...] for d in d_refs], axis=0)
    d_hidden = jnp.dot(d_ff, wd_ref[...], preferred_element_type=F32)
    gate = gate_ref[...]
    sig = 1.0 / (1.0 + jnp.exp(-gate))
    d_gate = (d_hidden * up_ref[...] * sig * (1.0 + gate * (1.0 - sig))).astype(BF)
    d_up = (d_hidden * gate * sig).astype(BF)
    dgu_ref[:, :tile] = d_gate
    dgu_ref[:, tile:] = d_up
    product = nt_dot(d_gate, wg_ref[...]) + nt_dot(d_up, wu_ref[...])
    ff_finish(pl.program_id(0), product, refs[-1], me_ref, refs[saved + 1 : -1])


def ff_specs(width, tile, gate_at, down_at):
    return [
        pl.BlockSpec((width, tile), lambda t: (0, gate_at // tile + t)),
        pl.BlockSpec((width, tile), lambda t: (0, t)),
        pl.BlockSpec((width, tile), lambda t: (0, down_at // tile + t)),
    ]


def ff_forward(me, residual_all, w_first, w_second, place, kinds, saved=()):
    length, width = residual_all.shape
    tokens = length // 4
    group = min(len(kinds), 2)
    rows = group * tokens
    ff_part = w_second.shape[1] // 2
    tile = min(FF_TILE, ff_part)
    block = pl.BlockSpec((rows, tile), lambda t: (place // group, t))
    whole = pl.BlockSpec((tokens, width), lambda t: (0, 0))
    shape = lambda kind: jax.ShapeDtypeStruct((length, ff_part), kind)
    return pl.pallas_call(
        functools.partial(ff_kernel, len(saved)),
        grid=(ff_part // tile,),
        in_specs=[pl.BlockSpec(memory_space=pltpu.SMEM)]
        + [once((rows, width), lambda t: (place // group, 0))]
        + ff_specs(width, tile, w_first.shape[1] - ff_part, ff_part)
        + [pl.BlockSpec(memory_space=pl.ANY)] * len(saved),
        out_specs=[block] * 3 + [whole] * len(kinds),
        out_shape=[shape(F32), shape(F32), shape(BF)]
        + [jax.ShapeDtypeStruct((tokens, width), kind) for kind in kinds],
        scratch_shapes=[pltpu.VMEM((rows, width), F32)],
        input_output_aliases={5 + j: j for j in range(len(saved))},
        compiler_params=params(),
        cost_estimate=cost(6 * rows * width * ff_part, 40 << 20, rows * ff_part),
        name="ff_forward",
    )(me, residual_all, w_first, w_second, w_second, *saved)


def ff_backward(me, d_ffs, w_first, w_second, gate, up, place, kinds, saved=()):
    tokens, width = d_ffs[0].shape
    group = len(d_ffs)
    rows = group * tokens
    length = gate.shape[0]
    ff_part = w_second.shape[1] // 2
    tile = min(FF_TILE, ff_part)
    block = pl.BlockSpec((rows, tile), lambda t: (place // group, t))
    whole = pl.BlockSpec((tokens, width), lambda t: (0, 0))
    return pl.pallas_call(
        functools.partial(ff_back_kernel, len(saved), group),
        grid=(ff_part // tile,),
        in_specs=[pl.BlockSpec(memory_space=pltpu.SMEM)]
        + [once((tokens, width), lambda t: (0, 0))] * group
        + ff_specs(width, tile, w_first.shape[1] - ff_part, ff_part)
        + [block, block]
        + [pl.BlockSpec(memory_space=pl.ANY)] * len(saved),
        out_specs=[pl.BlockSpec((rows, 2 * tile), lambda t: (place // group, t))]
        + [whole] * len(kinds),
        out_shape=[jax.ShapeDtypeStruct((length, 2 * ff_part), BF)]
        + [jax.ShapeDtypeStruct((tokens, width), kind) for kind in kinds],
        scratch_shapes=[pltpu.VMEM((rows, width), F32)],
        input_output_aliases={6 + group + j: j for j in range(len(saved))},
        compiler_params=params(),
        cost_estimate=cost(6 * rows * width * ff_part, 40 << 20, rows * ff_part),
        name="ff_backward",
    )(me, *d_ffs, w_first, w_second, w_second, gate, up, *saved)


def out_kernel(count, part, *refs):
    me_ref, pieces, (w_ref, x_ref, g_ref, res_ref, own_ref) = refs[0], refs[1:-5], refs[-5:]
    total = None
    for p, piece in enumerate(pieces):
        rows = pl.ds(pl.multiple_of((me_ref[0] + p) % count * part, part), part)
        product = jnp.dot(piece[...], w_ref[rows, :], preferred_element_type=F32)
        total = product if total is None else total + product
    normed = total * inv_rms(total)
    res_ref[...] = (x_ref[...].astype(F32) + normed * g_ref[...]).astype(BF)

    @pl.when(pl.program_id(0) == 0)
    def _():
        own_ref[...] = total


def ff_place(q):
    return jnp.where(q == 0, 3, jnp.where(q == 3, 1, jnp.where(q == 2, 2, 0)))


def out_project(me, pieces, w_out, x_all, gain, count):
    length, width = x_all.shape
    tokens = length // count
    part = pieces[0].shape[1]
    rolled = lambda p: pl.BlockSpec((tokens, part), lambda q, me: ((q + count - p) % count, 0))
    chunk = pl.BlockSpec((tokens, width), lambda q, me: (q, 0))
    moved = pl.BlockSpec((tokens, width), lambda q, me: (ff_place(q), 0))
    return pl.pallas_call(
        functools.partial(out_kernel, count, part),
        grid_spec=pltpu.PrefetchScalarGridSpec(
            num_scalar_prefetch=1,
            grid=(count,),
            in_specs=[rolled(p) for p in range(count)]
            + [pl.BlockSpec((width, width), lambda q, me: (0, 0), pipeline_mode=pl.Buffered(1))]
            + [chunk, pl.BlockSpec((1, width), lambda q, me: (0, 0))],
            out_specs=[moved, pl.BlockSpec((tokens, width), lambda q, me: (0, 0))],
        ),
        out_shape=[
            jax.ShapeDtypeStruct((length, width), BF),
            jax.ShapeDtypeStruct((tokens, width), F32),
        ],
        compiler_params=params(),
        cost_estimate=cost(2 * length * width * width, 22 << 20),
        name="out_project",
    )(me, *pieces, w_out, x_all, gain[None])


def columns_to_parts(values, me, count):
    part = values.shape[1] // count
    columns = lambda p: lax.dynamic_slice_in_dim(values, (me + p) % count * part, part, 1)
    got = [columns(0)] + [
        lax.ppermute(columns(p), "seq", [(i, (i + p) % count) for i in range(count)])
        for p in range(1, count)
    ]
    return [got[(count - q) % count] for q in range(count)]


def build(dp_count, seq_count):
    assert seq_count == 4

    def shards(
        layer_input,
        segments,
        w_query,
        w_key,
        w_value,
        w_output,
        w_gate,
        w_up,
        w_down,
        query_gain,
        key_gain,
        attn_gain,
        ff_gain,
        cotangent,
    ):
        n = seq_count
        tokens, width = layer_input.shape[1:]
        shard_rows = w_query.shape[0]
        part = width // n
        ff_part = w_gate.shape[1] // n
        length = n * tokens
        devices = dp_count * n
        me = lax.axis_index("seq")
        me_ref = me[None].astype(jnp.int32)
        cot = cotangent[0]
        by_part = lambda w: w.reshape(shard_rows, n, -1).transpose(1, 0, 2)
        rows_of = lambda blocks: blocks.reshape(n * shard_rows, -1)

        fence = lax.optimization_barrier
        qkv_blocks = jnp.concatenate([by_part(w) for w in (w_query, w_key, w_value)], axis=2)
        qkv_blocks = swap_blocks(qkv_blocks)
        w_qkv = gather_dp(rows_of(qkv_blocks))
        qkv_blocks, w_output, w_gate, w_down_t = fence((qkv_blocks, w_output, w_gate, w_down.T))
        out_blocks = gather_cyclic(w_output, n)
        gate_blocks = send_columns(w_gate, me, n)
        out_blocks, gate_blocks, x_own = fence((out_blocks, gate_blocks, layer_input[0]))
        out_blocks = out_blocks[:1] + out_blocks[:0:-1]
        w_first = place_blocks(out_blocks, me, 0, width + ff_part)
        w_first = gather_dp(place_blocks(gate_blocks, me, width, width + ff_part, w_first))
        x_chunks, w_up = fence((gather_cyclic(x_own, n), w_up))
        up_blocks = send_columns(w_up, me, n)
        x_all, qkv, squares = qkv_project(me_ref, x_chunks, w_qkv)
        squares, up_blocks = fence((squares, up_blocks))

        natural = jnp.arange(length, dtype=jnp.int32)
        positions = (natural + me * tokens) % length
        seg_row = segments[0]
        seg = lax.dynamic_slice_in_dim(
            jnp.concatenate([seg_row, seg_row]), me * tokens, length, 0
        )
        tables = rope_tables(positions.astype(F32))
        own_gain = lambda g: lax.dynamic_slice_in_dim(g, me * part, part, 0)
        q_gain = own_gain(query_gain)
        k_gain = own_gain(key_gain)

        squares = sum_stats(squares[:, 0].reshape(2, n, tokens), n).reshape(2, length)
        squares, w_down_t = fence((squares, w_down_t))
        down_blocks = send_columns(w_down_t, me, n)
        factors = lax.rsqrt(squares / width + EPSILON).T
        mixed, q_low, k_low, v_low = attend(me_ref, qkv, factors, q_gain, k_gain, tables, seg, n)

        mixed, down_blocks = fence((mixed, down_blocks))
        w_second = place_blocks(up_blocks, me, 0, 2 * ff_part)
        w_second = gather_dp(place_blocks(down_blocks, me, ff_part, 2 * ff_part, w_second))
        pieces = gather_cyclic(mixed, n)
        residual_all, attn_out = out_project(me_ref, pieces, w_first, x_all, attn_gain, n)
        attn_factor = inv_rms(attn_out)
        attn_normed = attn_out * attn_factor
        residual = x_own.astype(F32) + attn_normed * attn_gain

        *saved, after, before, ends = ff_forward(
            me_ref, residual_all, w_first, w_second, 0, (BF, BF, BF)
        )
        sent = scatter_start(ends, after, before, n)
        *saved, far = ff_forward(me_ref, residual_all, w_first, w_second, 2, (F32,), saved)
        far, sent[0], residual_late = fence((far, sent[0], residual_all))
        sent[0] = scatter_far(far, sent[0], n)
        gate, up, hidden, own = ff_forward(
            me_ref, residual_late, w_first, w_second, 3, (F32,), saved
        )
        ff_out = scatter_end(own, sent)
        ff_factor = inv_rms(ff_out)
        ff_normed = ff_out * ff_factor
        activation = (residual + ff_normed * ff_gain).astype(BF)
        grad_ff_gain = jnp.sum(cot.astype(F32) * ff_normed, axis=0)
        d_ff = rms_back(ff_normed, ff_factor, ff_gain, cot.astype(F32)).astype(BF)
        d_ffs = gather_cyclic(d_ff, n)
        d_both, own = ff_backward(me_ref, d_ffs[:1], w_first, w_second, gate, up, 3, (F32,))
        d_ffs, d_both = fence((d_ffs, d_both))
        d_both, after, before, ends = ff_backward(
            me_ref, d_ffs[1::2], w_first, w_second, gate, up, 0, (BF, BF, BF), (d_both,)
        )
        after, before, ends, d_ffs, hidden = fence((after, before, ends, d_ffs, hidden))
        sent = scatter_start(ends, after, before, n)
        down_grad = weight_grad([d_ffs[1], d_ffs[3], d_ffs[2], d_ffs[0]], hidden)
        down_rows = scatter_dp(down_grad)
        d_ff_far, down_grad = fence((d_ffs[2], down_grad))
        d_both, far = ff_backward(
            me_ref, [d_ff_far], w_first, w_second, gate, up, 2, (F32,), (d_both,)
        )
        d_both, far, sent[0] = fence((d_both, far, sent[0]))
        sent[0] = scatter_far(far, sent[0], n)
        joined = lambda g: g.transpose(1, 0, 2).reshape(shard_rows, -1).astype(F32)
        gate_up_grad = weight_grad([residual_all], d_both)
        gate_up_grad, sent = fence((gate_up_grad, sent))
        gate_up_rows = scatter_dp(gate_up_grad)
        d_res = cot.astype(F32) + scatter_end(own, sent)

        grad_attn_gain = jnp.sum(d_res * attn_normed, axis=0)
        d_attn = rms_back(attn_normed, attn_factor, attn_gain, d_res).astype(BF)
        d_pieces = mixed_back(me_ref, d_attn, w_first, n)
        d_mixed = [d_pieces[0]] + [None] * (n - 1)
        for p in range(1, n):
            d_mixed[n - p] = lax.ppermute(
                d_pieces[p], "seq", [(i, (i + p) % n) for i in range(n)]
            )
        d_mixed, d_attn, down_rows = fence((d_mixed, d_attn, down_rows))
        d_attn_part = columns_to_parts(d_attn, me, n)
        d_query, d_key, d_v, inner, gain_sums = attend_back(
            me_ref, d_mixed, q_low, k_low, v_low, qkv, factors, q_gain, k_gain, tables, seg, n
        )
        inner, d_attn_part = fence((inner, d_attn_part))
        inner = sum_stats(inner[:, 0].reshape(2, n, tokens), n).reshape(2, length)
        inner, down_rows = fence((inner, down_rows))
        down_back = send_rows(down_rows, me, n)
        d_qkv, ends, after, before, far, own = input_back(
            me_ref, d_query, d_key, d_v, qkv, (inner / width).T, factors, w_qkv, n
        )
        ends, after, before, far, own, d_qkv, down_back = fence(
            (ends, after, before, far, own, d_qkv, down_back)
        )
        sent = scatter_start(ends, after, before, n)
        attn_grads = attn_grad(me_ref, x_all, d_qkv, pieces, d_attn_part)
        sent, attn_grads = fence((sent, attn_grads))
        sent[0] = scatter_far(far, sent[0], n)
        attn_rows = scatter_dp(attn_grads)
        input_grad = d_res + scatter_end(own, sent)
        spread = lambda g: lax.dynamic_update_slice(jnp.zeros(width, F32), g, (me * part,))
        gains = jnp.stack(
            [spread(gain_sums[0, 0]), spread(gain_sums[1, 0]), grad_attn_gain, grad_ff_gain]
        )
        input_grad, gate_up_rows, gains = fence((input_grad, gate_up_rows, gains))
        gate_up_back = send_rows(gate_up_rows, me, n)
        gains = sum_everywhere(gains, dp_count, n)
        attn_rows, input_grad, gate_up_back, down_back, gains = fence(
            (attn_rows, input_grad, gate_up_back, down_back, gains)
        )
        attn_back = swap_blocks(attn_rows.reshape(n, shard_rows, -1))
        by_tile = [b.reshape(shard_rows, -1, 2, min(FF_TILE, ff_part)) for b in gate_up_back]
        grad_gate, grad_up = (
            join_columns([b[:, :, j].reshape(shard_rows, ff_part) for b in by_tile], me)
            for j in range(2)
        )
        grad_down = join_columns(down_back, me).T
        attn_back, grad_gate, grad_up, grad_down = fence(
            (attn_back, grad_gate, grad_up, grad_down)
        )
        grad_query, grad_key, grad_value, grad_output = (
            joined(attn_back[:, :, j * part : (j + 1) * part]) for j in range(4)
        )

        share = width // devices
        gains = lax.dynamic_slice_in_dim(
            gains, (lax.axis_index("dp") * n + me) * share, share, 1
        )
        return (
            activation[None],
            input_grad.astype(BF)[None],
            grad_query,
            grad_key,
            grad_value,
            grad_output,
            grad_gate,
            grad_up,
            grad_down,
            gains[0],
            gains[1],
            gains[2],
            gains[3],
        )

    return shards


def solution(mesh):
    both = P(("dp", "seq"), None)
    tokens = P("dp", "seq", None)
    columns = P(None, ("dp", "seq"))
    gain = P(("dp", "seq"))
    return jax.shard_map(
        build(mesh.shape["dp"], mesh.shape["seq"]),
        mesh=mesh,
        in_specs=(tokens, P("dp", None)) + (both,) * 6 + (columns,) + (P(),) * 4 + (tokens,),
        out_specs=(tokens, tokens) + (both,) * 6 + (columns,) + (gain,) * 4,
        check_vma=False,
    )
```

```python
import functools

import jax
import jax.numpy as jnp
from jax import lax
from jax.experimental import pallas as pl
from jax.experimental.pallas import tpu as pltpu
from jax.sharding import PartitionSpec as P

HD = 128
EPSILON = 1e-06
ROPE_BASE = 500000.0
MASKED = -1e30
LOG2E = 1.4426950408889634
BF = jnp.bfloat16
F32 = jnp.float32


def inv_rms(values):
    return lax.rsqrt(jnp.mean(values * values, axis=-1, keepdims=True) + EPSILON)


def rms_back(normed, factor, gain, grad):
    scaled = grad * gain
    inner = jnp.mean(scaled * normed, axis=-1, keepdims=True)
    return (scaled - normed * inner) * factor


def rope_tables(positions):
    half_dim = HD // 2
    frequency = jnp.power(F32(ROPE_BASE), -jnp.arange(half_dim, dtype=F32) * (2.0 / HD))
    angles = positions[:, None] * frequency[None, :]
    cosine, sine = jnp.cos(angles), jnp.sin(angles)
    return (jnp.concatenate([cosine, cosine], axis=-1), jnp.concatenate([-sine, sine], axis=-1))


def shift(values, count, step):
    return lax.ppermute(values, "seq", [((i + step) % count, i) for i in range(count)])


def gather_cyclic(values, count):
    if count != 4:
        return [values] + [shift(values, count, p) for p in range(1, count)]
    me = lax.axis_index("seq")
    far = lax.ppermute(values, "seq", [(i ^ 2, i) for i in range(4)])
    after = lax.ppermute(values, "seq", [(i + 1, i) for i in range(3)])
    before = lax.ppermute(values, "seq", [(i, i + 1) for i in range(3)])
    ends = lax.ppermute(far, "seq", [(2, 3), (1, 0)])
    return [values, jnp.where(me == 3, ends, after), far, jnp.where(me == 0, ends, before)]


def scatter_start(ends, after, before, count):
    ends = lax.ppermute(ends, "seq", [(0, 1), (count - 1, count - 2)])
    step = [(i, i + 1) for i in range(count - 1)]
    after = lax.ppermute(after, "seq", step)
    before = lax.ppermute(before, "seq", [(j, i) for i, j in step])
    return [ends, after, before]


def scatter_far(far, ends, count):
    far_sum = (far + ends.astype(F32)).astype(BF)
    return lax.ppermute(far_sum, "seq", [(i, i ^ 2) for i in range(count)])


def scatter_end(own, got):
    for part in got:
        own = own + part.astype(F32)
    return own


def sum_stats(stats, count):
    total = stats
    for p in range(1, count):
        total = total + jnp.roll(shift(stats, count, p), p, axis=1)
    return total


def sum_everywhere(values, dp_count, seq_count):
    for name, count in (("dp", dp_count), ("seq", seq_count)):
        if count & (count - 1):
            values = lax.psum(values, name)
            continue
        bit = 1
        while bit < count:
            values = values + lax.ppermute(values, name, [(i, i ^ bit) for i in range(count)])
            bit *= 2
    return values


def swap_blocks(values):
    return lax.all_to_all(values, "seq", split_axis=0, concat_axis=0, tiled=True)


def send_columns(values, me, count):
    part = values.shape[1] // count
    columns = lambda p: lax.dynamic_slice_in_dim(values, (me + p) % count * part, part, 1)
    return [columns(0)] + [
        lax.ppermute(columns(p), "seq", [(i, (i + p) % count) for i in range(count)])
        for p in range(1, count)
    ]


def place_blocks(blocks, me, first, width, total=None):
    count = len(blocks)
    rows = blocks[0].shape[0]
    if total is None:
        total = jnp.zeros((count * rows, width), blocks[0].dtype)
    for p, block in enumerate(blocks):
        total = lax.dynamic_update_slice(total, block, ((me - p) % count * rows, first))
    return total


def row_blocks(values, me, count):
    size = values.shape[0] // count
    return [
        lax.dynamic_slice_in_dim(values, (me + p) % count * size, size, 0) for p in range(count)
    ]


def send_blocks(blocks):
    count = len(blocks)
    return blocks[:1] + [
        lax.ppermute(blocks[p], "seq", [(i, (i + p) % count) for i in range(count)])
        for p in range(1, count)
    ]


def join_kernel(sides, me_ref, *refs):
    blocks, outs = refs[:-sides], refs[-sides:]
    for p, block in enumerate(blocks):

        @pl.when(pl.program_id(0) == p)
        def _(block=block):
            for j, out in enumerate(outs):
                tile = min(FF_TILE, out.shape[1])
                for at in range(0, out.shape[1], tile):
                    first = at * sides + j * tile
                    out[:, at : at + tile] = block[:, first : first + tile].astype(F32)


def join_columns(me, blocks, sides):
    count = len(blocks)
    rows, columns = blocks[0].shape
    part = columns // sides
    out = pl.BlockSpec((rows, part), lambda p, me: (0, (me[0] + count - p) % count))
    return pl.pallas_call(
        functools.partial(join_kernel, sides),
        grid_spec=pltpu.PrefetchScalarGridSpec(
            num_scalar_prefetch=1,
            grid=(count,),
            in_specs=[once((rows, columns), lambda p, me: (0, 0))] * count,
            out_specs=[out] * sides,
        ),
        out_shape=[jax.ShapeDtypeStruct((rows, count * part), F32)] * sides,
        compiler_params=params(),
        cost_estimate=cost(0, 0),
        name="join_columns",
    )(me, *blocks)


def gather_dp(values):
    return lax.all_gather(values, "dp", axis=0, tiled=True)


def scatter_dp(values):
    return lax.psum_scatter(values, "dp", scatter_dimension=0, tiled=True)


def softmax_window(q, k_ref, seg_q, seg_row_ref, valid_from, place, tokens, count, span):
    parts = []
    for w in range(span):
        at = ((place - w) % count) * tokens
        scores = lax.dot_general(
            q, k_ref[at : at + tokens, :], (((1,), (1,)), ((), ())), preferred_element_type=F32
        )
        seg = seg_q if w == 0 else jnp.where(valid_from >= w, seg_q, -1)
        allowed = seg == seg_row_ref[:, at : at + tokens]
        if w == 0:
            rows = lax.broadcasted_iota(jnp.int32, (tokens, tokens), 0)
            cols = lax.broadcasted_iota(jnp.int32, (tokens, tokens), 1)
            allowed = allowed & (cols <= rows)
        parts.append(jnp.where(allowed, scores, MASKED))
    top = parts[0]
    for part in parts[1:]:
        top = jnp.maximum(top, part)
    top = jnp.max(top, axis=-1, keepdims=True)
    exps = [jnp.exp2((part - top) * (HD**-0.5 * LOG2E)) for part in parts]
    total = exps[0]
    for part in exps[1:]:
        total = total + part
    inverse = 1.0 / jnp.sum(total, axis=-1, keepdims=True)
    return [part * inverse for part in exps]


def turn(values, cosine, sine):
    return values * cosine + pltpu.roll(values, HD // 2, 1) * sine


def attend_kernel(
    tokens, count, span,
    me_ref, q_ref, k_ref, v_ref, f_ref, qg_ref, kg_ref, cos_ref, sin_ref, segc_ref, segr_ref,
    o_ref, qb_ref, kb_ref, vb_ref,
):
    cosine, sine = cos_ref[...], sin_ref[...]
    factors = f_ref[...]
    qb_ref[...] = turn(q_ref[...] * factors[:, 0:1] * qg_ref[...], cosine, sine).astype(BF)
    kb_ref[...] = turn(k_ref[...] * factors[:, 1:2] * kg_ref[...], cosine, sine).astype(BF)
    vb_ref[...] = v_ref[...].astype(BF)
    for place in range(count):
        rows = slice(place * tokens, (place + 1) * tokens)
        chunk = (me_ref[0] + place) % count
        probs = softmax_window(
            qb_ref[rows, :], kb_ref, segc_ref[rows, :], segr_ref, chunk, place, tokens, count, span
        )
        mixed = None
        for w in range(span):
            at = ((place - w) % count) * tokens
            part = jnp.dot(probs[w].astype(BF), vb_ref[at : at + tokens, :], preferred_element_type=F32)
            mixed = part if mixed is None else mixed + part
        o_ref[rows, :] = mixed.astype(BF)


def attend_back_kernel(
    tokens, count, span, me_ref, *refs
):
    grads_in = refs[:count]
    (q_ref, k_ref, v_ref, qp_ref, kp_ref, f_ref, qg_ref, kg_ref, cos_ref, sin_ref, segc_ref, segr_ref,
     dq_ref, dk_ref, dv_ref, inner_ref, gain_ref, dk_sum, dv_sum) = refs[count:]
    scale = HD**-0.5
    dk_sum[...] = jnp.zeros_like(dk_sum)
    dv_sum[...] = jnp.zeros_like(dv_sum)
    for place in range(count):
        rows = slice(place * tokens, (place + 1) * tokens)
        chunk = (me_ref[0] + place) % count
        q = q_ref[rows, :]
        grad = grads_in[place][...]
        probs = softmax_window(
            q, k_ref, segc_ref[rows, :], segr_ref, chunk, place, tokens, count, span
        )
        grads = []
        inner = None
        for w in range(span):
            at = ((place - w) % count) * tokens
            part = nt_dot(grad, v_ref[at : at + tokens, :])
            grads.append(part)
            inner = probs[w] * part if inner is None else inner + probs[w] * part
            dv_sum[at : at + tokens, :] += lax.dot_general(
                probs[w].astype(BF), grad, (((0,), (0,)), ((), ())), preferred_element_type=F32
            )
        inner = jnp.sum(inner, axis=-1, keepdims=True)
        dq = None
        for w in range(span):
            at = ((place - w) % count) * tokens
            ds = (probs[w] * (grads[w] - inner)).astype(BF)
            part = jnp.dot(ds, k_ref[at : at + tokens, :], preferred_element_type=F32)
            dq = part if dq is None else dq + part
            dk_sum[at : at + tokens, :] += lax.dot_general(
                ds, q, (((0,), (0,)), ((), ())), preferred_element_type=F32
            )
        dq_ref[rows, :] = dq
    ones = jnp.ones((8, HD), F32)
    first = pl.program_id(0) == 0
    sides = ((dq_ref, dq_ref, qp_ref, qg_ref), (dk_sum, dk_ref, kp_ref, kg_ref))
    for j, (raw_ref, out_ref, proj_ref, g_ref) in enumerate(sides):
        raw = (raw_ref[...] * scale).astype(BF).astype(F32)
        back = turn(raw, cos_ref[...], -sin_ref[...])
        normed = proj_ref[...] * f_ref[:, j : j + 1]
        gain_ref[j] = jnp.broadcast_to(jnp.sum(back * normed, axis=0, keepdims=True), (8, HD))
        back = back * g_ref[...]
        out_ref[...] = back
        sums = lax.dot_general(
            ones, back * normed, (((1,), (1,)), ((), ())),
            precision=lax.Precision.HIGHEST, preferred_element_type=F32,
        )
        inner_ref[j] = jnp.where(first, sums, inner_ref[j] + sums)
    dv_ref[...] = dv_sum[...].astype(BF)


def attend_specs(length, heads):
    head = lambda j: pl.BlockSpec((length, HD), lambda h, me: (0, j * heads + h))
    whole = lambda *shape: pl.BlockSpec(shape, lambda h, me: (0, 0))
    gain = pl.BlockSpec((1, HD), lambda h, me: (0, h))
    return head, whole, gain


def attend(me, qkv, factors, q_gain, k_gain, tables, seg, count):
    length = qkv.shape[0]
    part = qkv.shape[1] // 3
    heads = part // HD
    tokens = length // count
    span = min(count, (length // 2 - 1 + tokens - 1) // tokens + 1)
    head, whole, gain = attend_specs(length, heads)
    low = jax.ShapeDtypeStruct((length, part), BF)
    return pl.pallas_call(
        functools.partial(attend_kernel, tokens, count, span),
        grid_spec=pltpu.PrefetchScalarGridSpec(
            num_scalar_prefetch=1,
            grid=(heads,),
            in_specs=[head(0), head(1), head(2), whole(length, 2), gain, gain]
            + [whole(length, HD)] * 2
            + [whole(length, 1), whole(1, length)],
            out_specs=[head(0)] * 4,
        ),
        out_shape=[low] * 4,
        compiler_params=params(),
        cost_estimate=cost(0, 0),
        name="attend",
    )(me, qkv, qkv, qkv, factors, q_gain[None], k_gain[None], *tables, seg[:, None], seg[None])


def attend_back(me, pieces, query, key, value, qkv, factors, q_gain, k_gain, tables, seg, count):
    length, part = query.shape
    heads = part // HD
    tokens = length // count
    span = min(count, (length // 2 - 1 + tokens - 1) // tokens + 1)
    head, whole, gain = attend_specs(length, heads)
    return pl.pallas_call(
        functools.partial(attend_back_kernel, tokens, count, span),
        grid_spec=pltpu.PrefetchScalarGridSpec(
            num_scalar_prefetch=1,
            grid=(heads,),
            in_specs=[pl.BlockSpec((tokens, HD), lambda h, me: (0, h))] * count
            + [head(0)] * 3
            + [head(0), head(1), whole(length, 2), gain, gain]
            + [whole(length, HD)] * 2
            + [whole(length, 1), whole(1, length)],
            out_specs=[head(0)] * 3
            + [
                pl.BlockSpec((2, 8, length), lambda h, me: (0, 0, 0)),
                pl.BlockSpec((2, 8, HD), lambda h, me: (0, 0, h)),
            ],
            scratch_shapes=[pltpu.VMEM((length, HD), F32)] * 2,
        ),
        out_shape=[jax.ShapeDtypeStruct((length, part), t) for t in (F32, F32, BF)]
        + [jax.ShapeDtypeStruct((2, 8, m), F32) for m in (length, part)],
        compiler_params=params(),
        cost_estimate=cost(0, 0),
        name="attend_back",
    )(me, *pieces, query, key, value, qkv, qkv, factors, q_gain[None], k_gain[None], *tables,
      seg[:, None], seg[None])


def residual_back_kernel(
    me_ref, own_ref, a_ref, b_ref, c_ref, cot_ref, attn_ref, gain_ref, w_ref, res_ref, d_ref, sum_ref, *outs
):
    step = pl.program_id(0)

    @pl.when(step == 0)
    def _():
        grad = cot_ref[...].astype(F32) + own_ref[...]
        for ref in (a_ref, b_ref, c_ref):
            grad = grad + ref[...].astype(F32)
        res_ref[...] = grad
        attn = attn_ref[...]
        factor = inv_rms(attn)
        normed = attn * factor
        sums = jnp.sum(grad * normed, axis=0, keepdims=True)
        sum_ref[...] = jnp.broadcast_to(sums, sum_ref.shape)
        d_ref[...] = rms_back(normed, factor, gain_ref[...], grad).astype(BF)

    piece = nt_dot(d_ref[...], w_ref[...]).astype(BF)
    for p, out in enumerate(outs):

        @pl.when(step == p)
        def _(out=out):
            out[...] = piece


def residual_back(me, own, got, cot, attn_out, gain, w_first, count):
    tokens, width = own.shape
    part = width // count
    piece = pl.BlockSpec((tokens, part), lambda p, me: (0, 0))
    full = once((tokens, width), lambda p, me: (0, 0))
    whole = lambda rows: pl.BlockSpec((rows, width), lambda p, me: (0, 0))
    return pl.pallas_call(
        residual_back_kernel,
        grid_spec=pltpu.PrefetchScalarGridSpec(
            num_scalar_prefetch=1,
            grid=(count,),
            in_specs=[full] * 6
            + [whole(1), pl.BlockSpec((part, width), lambda p, me: ((me[0] + p) % count, 0))],
            out_specs=[whole(tokens), whole(tokens), whole(8)] + [piece] * count,
        ),
        out_shape=[
            jax.ShapeDtypeStruct((tokens, width), F32),
            jax.ShapeDtypeStruct((tokens, width), BF),
            jax.ShapeDtypeStruct((8, width), F32),
        ]
        + [jax.ShapeDtypeStruct((tokens, part), BF)] * count,
        compiler_params=params(),
        cost_estimate=cost(LATE_COST, 0),
        name="residual_back",
    )(me, own, *got, cot, attn_out, gain[None], w_first)


def input_back_kernel(
    part, me_ref, q_ref, k_ref, v_ref, qp_ref, kp_ref, in_ref, f_ref, w_ref, d_ref, ends_ref, *outs
):
    for j, (grad, proj) in enumerate(((q_ref, qp_ref), (k_ref, kp_ref))):
        factor = f_ref[:, j : j + 1]
        normed = proj[...] * factor
        low = ((grad[...] - normed * in_ref[:, j : j + 1]) * factor).astype(BF)
        d_ref[:, j * part : (j + 1) * part] = low
    d_ref[:, 2 * part :] = v_ref[...]
    total = nt_dot(d_ref[...], w_ref[...])
    step = pl.program_id(0)
    for j, out in enumerate(outs):

        @pl.when(step == j)
        def _(out=out):
            out[...] = total.astype(out.dtype)

    @pl.when((step == 0) | ((step == 1) & (me_ref[0] == 0)))
    def _():
        ends_ref[...] = total.astype(BF)


def input_back(me, d_query, d_key, d_v, qkv, inner, factors, w_qkv):
    length, part = d_query.shape
    width = w_qkv.shape[0]
    tokens = length // 4
    place = lambda t: jnp.where(t == 0, 1, jnp.where(t == 1, 3, jnp.where(t == 2, 2, 0)))
    rows = lambda columns, at=0: pl.BlockSpec((tokens, columns), lambda t, me: (place(t), at))
    kinds = (BF, BF, BF, BF, F32)
    return pl.pallas_call(
        functools.partial(input_back_kernel, part),
        grid_spec=pltpu.PrefetchScalarGridSpec(
            num_scalar_prefetch=1,
            grid=(4,),
            in_specs=[rows(part)] * 3
            + [rows(part), rows(part, 1), rows(2), rows(2)]
            + [once((width, 3 * part), lambda t, me: (0, 0))],
            out_specs=[rows(3 * part)]
            + [pl.BlockSpec((tokens, width), lambda t, me: (0, 0))] * len(kinds),
        ),
        out_shape=[jax.ShapeDtypeStruct((length, 3 * part), BF)]
        + [jax.ShapeDtypeStruct((tokens, width), kind) for kind in kinds],
        compiler_params=params(),
        cost_estimate=cost(0, 0),
        name="input_back",
    )(me, d_query, d_key, d_v, qkv, qkv, inner, factors, w_qkv)


def add_up_kernel(*refs):
    total = refs[0][...]
    for ref in refs[1:-1]:
        total = total + ref[...].astype(F32)
    refs[-1][...] = total.astype(BF)


def add_up(parts):
    tokens, width = parts[0].shape
    tile = tokens // 4
    block = pl.BlockSpec((tile, width), lambda i: (i, 0))
    return pl.pallas_call(
        add_up_kernel,
        grid=(4,),
        in_specs=[block] * len(parts),
        out_specs=block,
        out_shape=jax.ShapeDtypeStruct((tokens, width), BF),
        compiler_params=params(),
        cost_estimate=cost(LATE_COST, 0),
        name="add_up",
    )(*parts)


def tn_dot(left, right):
    return lax.dot_general(left, right, (((0,), (0,)), ((), ())), preferred_element_type=F32)


def weight_grad_kernel(lefts, right_ref, out_ref):
    total, at = None, 0
    for left in lefts:
        rows = left.shape[0]
        product = tn_dot(left[...], right_ref[at : at + rows, :])
        total = product if total is None else total + product
        at += rows
    out_ref[...] = total.astype(BF)


def weight_grad(lefts, right):
    width = lefts[0].shape[1]
    length, columns = right.shape
    tile, wide = 256, min(columns, 2048)
    return pl.pallas_call(
        lambda *refs: weight_grad_kernel(refs[:-2], *refs[-2:]),
        grid=(columns // wide, width // tile),
        in_specs=[pl.BlockSpec((left.shape[0], tile), lambda j, i: (0, i)) for left in lefts]
        + [pl.BlockSpec((length, wide), lambda j, i: (0, j))],
        out_specs=pl.BlockSpec((tile, wide), lambda j, i: (i, j)),
        out_shape=jax.ShapeDtypeStruct((width, columns), BF),
        compiler_params=params(),
        cost_estimate=cost(0, 0),
        name="weight_grad",
    )(*lefts, right)


def attn_grad_kernel(count, me_ref, x_ref, d_ref, *refs):
    pieces, parts, out_ref = refs[:count], refs[count : 2 * count], refs[-1]
    columns = d_ref.shape[1]
    out_ref[:, :columns] = tn_dot(x_ref[...], d_ref[...]).astype(BF)
    source = (pl.program_id(0) // (pl.num_programs(0) // count) + count - me_ref[0]) % count
    for p, piece in enumerate(pieces):

        @pl.when(source == p)
        def _(p=p, piece=piece):
            total, tokens = None, parts[0].shape[0]
            for q in range(count):
                rows = slice(q * tokens, (q + 1) * tokens)
                product = tn_dot(piece[rows, :], parts[(q + p) % count][...])
                total = product if total is None else total + product
            out_ref[:, columns:] = total.astype(BF)


def attn_grad(me, x_all, d_qkv, pieces, d_parts):
    count = len(pieces)
    length, width = x_all.shape
    columns, part = d_qkv.shape[1], d_parts[0].shape[1]
    tile = min(256, part)
    per_part = part // tile
    return pl.pallas_call(
        functools.partial(attn_grad_kernel, count),
        grid_spec=pltpu.PrefetchScalarGridSpec(
            num_scalar_prefetch=1,
            grid=(width // tile,),
            in_specs=[
                pl.BlockSpec((length, tile), lambda i, me: (0, i)),
                once((length, columns), lambda i, me: (0, 0)),
            ]
            + [pl.BlockSpec((length, tile), lambda i, me: (0, i % per_part))] * count
            + [once((length // count, part), lambda i, me: (0, 0))] * count,
            out_specs=pl.BlockSpec((tile, columns + part), lambda i, me: (i, 0)),
        ),
        out_shape=jax.ShapeDtypeStruct((width, columns + part), BF),
        compiler_params=params(),
        cost_estimate=cost(SIDE_COST, 0),
        name="attn_grad",
    )(me, x_all, d_qkv, *pieces, *d_parts)


def cost(flops, moved, exps=0):
    return pl.CostEstimate(flops=flops, bytes_accessed=moved, transcendentals=exps)


def params():
    return pltpu.CompilerParams(vmem_limit_bytes=56 << 20)


def once(shape, index):
    return pl.BlockSpec(shape, index, pipeline_mode=pl.Buffered(1))


def nt_dot(left, right):
    return lax.dot_general(left, right, (((1,), (1,)), ((), ())), preferred_element_type=F32)


def qkv_kernel(count, part, me_ref, *refs):
    chunks, (w_ref, x_ref, qkv_ref, sq_ref) = refs[:-4], refs[-4:]
    for q in range(count):

        @pl.when(pl.program_id(0) == q)
        def _(q=q):
            x_ref[...] = chunks[q][...]

    qkv = jnp.dot(x_ref[...], w_ref[...], preferred_element_type=F32)
    qkv_ref[...] = qkv
    ones = jnp.ones((8, part), F32)
    for j in range(2):
        values = qkv[:, j * part : (j + 1) * part]
        sq_ref[j] = lax.dot_general(
            ones, values * values, (((1,), (1,)), ((), ())),
            precision=lax.Precision.HIGHEST, preferred_element_type=F32,
        )


def qkv_project(me, chunks, w_qkv):
    count = len(chunks)
    tokens, width = chunks[0].shape
    columns = w_qkv.shape[1]
    length = count * tokens
    return pl.pallas_call(
        functools.partial(qkv_kernel, count, columns // 3),
        grid_spec=pltpu.PrefetchScalarGridSpec(
            num_scalar_prefetch=1,
            grid=(count,),
            in_specs=[once((tokens, width), lambda q, me: (0, 0))] * count
            + [once((width, columns), lambda q, me: (0, 0))],
            out_specs=[
                pl.BlockSpec((tokens, width), lambda q, me: (q, 0)),
                pl.BlockSpec((tokens, columns), lambda q, me: (q, 0)),
                pl.BlockSpec((2, 8, tokens), lambda q, me: (0, 0, q)),
            ],
        ),
        out_shape=[
            jax.ShapeDtypeStruct((length, width), BF),
            jax.ShapeDtypeStruct((length, columns), F32),
            jax.ShapeDtypeStruct((2, 8, length), F32),
        ],
        compiler_params=params(),
        cost_estimate=cost(0, 0),
        name="qkv_project",
    )(me, *chunks, w_qkv)


FF_TILE = 512
LATE_COST = 10**12
SIDE_COST = 10**11


def ff_finish(step, product, acc, me_ref, outs):
    @pl.when(step == 0)
    def _():
        acc[...] = product

    @pl.when(step > 0)
    def _():
        acc[...] += product

    @pl.when(step == pl.num_programs(0) - 1)
    def _():
        tokens = outs[0].shape[0]
        for j, out in enumerate(outs[:2]):
            out[...] = acc[j * tokens : (j + 1) * tokens].astype(out.dtype)
        if len(outs) == 3:
            at = pl.multiple_of(jnp.where(me_ref[0] == 0, tokens, 0), tokens)
            outs[2][...] = acc[pl.ds(at, tokens), :].astype(BF)


def ff_kernel(saved, me_ref, h_ref, wg_ref, wu_ref, wd_ref, *refs):
    gate_ref, up_ref, hid_ref = refs[saved : saved + 3]
    h = h_ref[...]
    gate = jnp.dot(h, wg_ref[...], preferred_element_type=F32)
    up = jnp.dot(h, wu_ref[...], preferred_element_type=F32)
    hidden = (gate * (1.0 / (1.0 + jnp.exp(-gate))) * up).astype(BF)
    gate_ref[...] = gate
    up_ref[...] = up
    hid_ref[...] = hidden
    product = nt_dot(hidden, wd_ref[...])
    ff_finish(pl.program_id(0), product, refs[-1], me_ref, refs[saved + 3 : -1])


def ff_back_kernel(saved, groups, me_ref, *refs):
    d_refs, (wg_ref, wu_ref, wd_ref, gate_ref, up_ref) = refs[:groups], refs[groups : groups + 5]
    refs = refs[groups + 5 :]
    dgu_ref = refs[saved]
    tile = wg_ref.shape[1]
    d_ff = d_refs[0][...] if groups == 1 else jnp.concatenate([d[...] for d in d_refs], axis=0)
    d_hidden = jnp.dot(d_ff, wd_ref[...], preferred_element_type=F32)
    gate = gate_ref[...]
    sig = 1.0 / (1.0 + jnp.exp(-gate))
    d_gate = (d_hidden * up_ref[...] * sig * (1.0 + gate * (1.0 - sig))).astype(BF)
    d_up = (d_hidden * gate * sig).astype(BF)
    dgu_ref[:, :tile] = d_gate
    dgu_ref[:, tile:] = d_up
    product = nt_dot(d_gate, wg_ref[...]) + nt_dot(d_up, wu_ref[...])
    ff_finish(pl.program_id(0), product, refs[-1], me_ref, refs[saved + 1 : -1])


def ff_specs(width, tile, gate_at, down_at):
    return [
        pl.BlockSpec((width, tile), lambda t: (0, gate_at // tile + t)),
        pl.BlockSpec((width, tile), lambda t: (0, t)),
        pl.BlockSpec((width, tile), lambda t: (0, down_at // tile + t)),
    ]


def ff_forward(me, residual_all, w_first, w_second, place, kinds, saved=()):
    length, width = residual_all.shape
    tokens = length // 4
    group = min(len(kinds), 2)
    rows = group * tokens
    ff_part = w_second.shape[1] // 2
    tile = min(FF_TILE, ff_part)
    block = pl.BlockSpec((rows, tile), lambda t: (place // group, t))
    whole = pl.BlockSpec((tokens, width), lambda t: (0, 0))
    shape = lambda kind: jax.ShapeDtypeStruct((length, ff_part), kind)
    return pl.pallas_call(
        functools.partial(ff_kernel, len(saved)),
        grid=(ff_part // tile,),
        in_specs=[pl.BlockSpec(memory_space=pltpu.SMEM)]
        + [once((rows, width), lambda t: (place // group, 0))]
        + ff_specs(width, tile, w_first.shape[1] - ff_part, ff_part)
        + [pl.BlockSpec(memory_space=pl.ANY)] * len(saved),
        out_specs=[block] * 3 + [whole] * len(kinds),
        out_shape=[shape(F32), shape(F32), shape(BF)]
        + [jax.ShapeDtypeStruct((tokens, width), kind) for kind in kinds],
        scratch_shapes=[pltpu.VMEM((rows, width), F32)],
        input_output_aliases={5 + j: j for j in range(len(saved))},
        compiler_params=params(),
        cost_estimate=cost(0, 0),
        name="ff_forward",
    )(me, residual_all, w_first, w_second, w_second, *saved)


def ff_backward(me, d_ffs, w_first, w_second, gate, up, place, kinds, saved=()):
    tokens, width = d_ffs[0].shape
    group = len(d_ffs)
    rows = group * tokens
    length = gate.shape[0]
    ff_part = w_second.shape[1] // 2
    tile = min(FF_TILE, ff_part)
    block = pl.BlockSpec((rows, tile), lambda t: (place // group, t))
    whole = pl.BlockSpec((tokens, width), lambda t: (0, 0))
    return pl.pallas_call(
        functools.partial(ff_back_kernel, len(saved), group),
        grid=(ff_part // tile,),
        in_specs=[pl.BlockSpec(memory_space=pltpu.SMEM)]
        + [once((tokens, width), lambda t: (0, 0))] * group
        + ff_specs(width, tile, w_first.shape[1] - ff_part, ff_part)
        + [block, block]
        + [pl.BlockSpec(memory_space=pl.ANY)] * len(saved),
        out_specs=[pl.BlockSpec((rows, 2 * tile), lambda t: (place // group, t))]
        + [whole] * len(kinds),
        out_shape=[jax.ShapeDtypeStruct((length, 2 * ff_part), BF)]
        + [jax.ShapeDtypeStruct((tokens, width), kind) for kind in kinds],
        scratch_shapes=[pltpu.VMEM((rows, width), F32)],
        input_output_aliases={6 + group + j: j for j in range(len(saved))},
        compiler_params=params(),
        cost_estimate=cost(SIDE_COST, 0),
        name="ff_backward",
    )(me, *d_ffs, w_first, w_second, w_second, gate, up, *saved)


def out_kernel(count, part, *refs):
    me_ref, pieces, (w_ref, x_ref, g_ref, res_ref, own_ref) = refs[0], refs[1:-5], refs[-5:]
    total = None
    for p, piece in enumerate(pieces):
        rows = pl.ds(pl.multiple_of((me_ref[0] + p) % count * part, part), part)
        product = jnp.dot(piece[...], w_ref[rows, :], preferred_element_type=F32)
        total = product if total is None else total + product
    normed = total * inv_rms(total)
    res_ref[...] = (x_ref[...].astype(F32) + normed * g_ref[...]).astype(BF)

    @pl.when(pl.program_id(0) == 0)
    def _():
        own_ref[...] = total


def ff_place(q):
    return jnp.where(q == 0, 3, jnp.where(q == 3, 1, jnp.where(q == 2, 2, 0)))


def out_project(me, pieces, w_out, x_all, gain, count):
    length, width = x_all.shape
    tokens = length // count
    part = pieces[0].shape[1]
    rolled = lambda p: pl.BlockSpec((tokens, part), lambda q, me: ((q + count - p) % count, 0))
    chunk = pl.BlockSpec((tokens, width), lambda q, me: (q, 0))
    moved = pl.BlockSpec((tokens, width), lambda q, me: (ff_place(q), 0))
    return pl.pallas_call(
        functools.partial(out_kernel, count, part),
        grid_spec=pltpu.PrefetchScalarGridSpec(
            num_scalar_prefetch=1,
            grid=(count,),
            in_specs=[rolled(p) for p in range(count)]
            + [pl.BlockSpec((width, width), lambda q, me: (0, 0), pipeline_mode=pl.Buffered(1))]
            + [chunk, pl.BlockSpec((1, width), lambda q, me: (0, 0))],
            out_specs=[moved, pl.BlockSpec((tokens, width), lambda q, me: (0, 0))],
        ),
        out_shape=[
            jax.ShapeDtypeStruct((length, width), BF),
            jax.ShapeDtypeStruct((tokens, width), F32),
        ],
        compiler_params=params(),
        cost_estimate=cost(0, 0),
        name="out_project",
    )(me, *pieces, w_out, x_all, gain[None])


def columns_to_parts(values, me, count):
    part = values.shape[1] // count
    columns = lambda p: lax.dynamic_slice_in_dim(values, (me + p) % count * part, part, 1)
    got = [columns(0)] + [
        lax.ppermute(columns(p), "seq", [(i, (i + p) % count) for i in range(count)])
        for p in range(1, count)
    ]
    return [got[(count - q) % count] for q in range(count)]


def build(dp_count, seq_count):
    assert seq_count == 4

    def shards(
        layer_input,
        segments,
        w_query,
        w_key,
        w_value,
        w_output,
        w_gate,
        w_up,
        w_down,
        query_gain,
        key_gain,
        attn_gain,
        ff_gain,
        cotangent,
    ):
        n = seq_count
        tokens, width = layer_input.shape[1:]
        shard_rows = w_query.shape[0]
        part = width // n
        ff_part = w_gate.shape[1] // n
        length = n * tokens
        devices = dp_count * n
        me = lax.axis_index("seq")
        me_ref = me[None].astype(jnp.int32)
        cot = cotangent[0]
        by_part = lambda w: w.reshape(shard_rows, n, -1).transpose(1, 0, 2)
        rows_of = lambda blocks: blocks.reshape(n * shard_rows, -1)

        fence = lax.optimization_barrier
        qkv_blocks = jnp.concatenate([by_part(w) for w in (w_query, w_key, w_value)], axis=2)
        qkv_blocks = swap_blocks(qkv_blocks)
        w_qkv = gather_dp(rows_of(qkv_blocks))
        qkv_blocks, w_output, w_gate, w_down_t = fence((qkv_blocks, w_output, w_gate, w_down.T))
        out_blocks = gather_cyclic(w_output, n)
        gate_blocks = send_columns(w_gate, me, n)
        out_blocks, gate_blocks, x_own = fence((out_blocks, gate_blocks, layer_input[0]))
        out_blocks = out_blocks[:1] + out_blocks[:0:-1]
        w_first = place_blocks(out_blocks, me, 0, width + ff_part)
        w_first = gather_dp(place_blocks(gate_blocks, me, width, width + ff_part, w_first))
        x_chunks, w_up = fence((gather_cyclic(x_own, n), w_up))
        up_blocks = send_columns(w_up, me, n)
        x_all, qkv, squares = qkv_project(me_ref, x_chunks, w_qkv)
        squares, up_blocks = fence((squares, up_blocks))

        natural = jnp.arange(length, dtype=jnp.int32)
        positions = (natural + me * tokens) % length
        seg_row = segments[0]
        seg = lax.dynamic_slice_in_dim(
            jnp.concatenate([seg_row, seg_row]), me * tokens, length, 0
        )
        tables = rope_tables(positions.astype(F32))
        own_gain = lambda g: lax.dynamic_slice_in_dim(g, me * part, part, 0)
        q_gain = own_gain(query_gain)
        k_gain = own_gain(key_gain)

        squares = sum_stats(squares[:, 0].reshape(2, n, tokens), n).reshape(2, length)
        squares, w_down_t = fence((squares, w_down_t))
        down_blocks = send_columns(w_down_t, me, n)
        factors = lax.rsqrt(squares / width + EPSILON).T
        mixed, q_low, k_low, v_low = attend(me_ref, qkv, factors, q_gain, k_gain, tables, seg, n)

        mixed, down_blocks = fence((mixed, down_blocks))
        w_second = place_blocks(up_blocks, me, 0, 2 * ff_part)
        w_second = gather_dp(place_blocks(down_blocks, me, ff_part, 2 * ff_part, w_second))
        pieces = gather_cyclic(mixed, n)
        residual_all, attn_out = out_project(me_ref, pieces, w_first, x_all, attn_gain, n)
        attn_factor = inv_rms(attn_out)
        attn_normed = attn_out * attn_factor
        residual = x_own.astype(F32) + attn_normed * attn_gain

        *saved, after, before, ends = ff_forward(
            me_ref, residual_all, w_first, w_second, 0, (BF, BF, BF)
        )
        sent = scatter_start(ends, after, before, n)
        *saved, far = ff_forward(me_ref, residual_all, w_first, w_second, 2, (F32,), saved)
        far, sent[0], residual_late = fence((far, sent[0], residual_all))
        sent[0] = scatter_far(far, sent[0], n)
        gate, up, hidden, own = ff_forward(
            me_ref, residual_late, w_first, w_second, 3, (F32,), saved
        )
        ff_out = scatter_end(own, sent)
        ff_factor = inv_rms(ff_out)
        ff_normed = ff_out * ff_factor
        activation = (residual + ff_normed * ff_gain).astype(BF)
        grad_ff_gain = jnp.sum(cot.astype(F32) * ff_normed, axis=0)
        d_ff = rms_back(ff_normed, ff_factor, ff_gain, cot.astype(F32)).astype(BF)
        d_ffs = gather_cyclic(d_ff, n)
        d_both, own = ff_backward(me_ref, d_ffs[:1], w_first, w_second, gate, up, 3, (F32,))
        d_ffs, d_both = fence((d_ffs, d_both))
        d_both, after, before, ends = ff_backward(
            me_ref, d_ffs[1::2], w_first, w_second, gate, up, 0, (BF, BF, BF), (d_both,)
        )
        sent = scatter_start(ends, after, before, n)
        d_both, far = ff_backward(
            me_ref, d_ffs[2:3], w_first, w_second, gate, up, 2, (F32,), (d_both,)
        )
        d_both, far, sent[0], d_ffs, hidden = fence((d_both, far, sent[0], d_ffs, hidden))
        sent[0] = scatter_far(far, sent[0], n)
        joined = lambda g: g.transpose(1, 0, 2).reshape(shard_rows, -1).astype(F32)
        down_grad = weight_grad([d_ffs[1], d_ffs[3], d_ffs[2], d_ffs[0]], hidden)
        down_rows = scatter_dp(down_grad)
        down_grad, sent = fence((down_grad, sent))
        d_res, d_attn, grad_attn_gain, *d_pieces = residual_back(
            me_ref, own, sent, cot, attn_out, attn_gain, w_first, n
        )
        d_mixed = [d_pieces[0]] + [None] * (n - 1)
        for p in range(1, n):
            d_mixed[n - p] = lax.ppermute(
                d_pieces[p], "seq", [(i, (i + p) % n) for i in range(n)]
            )
        residual_all, d_both, _ = fence((residual_all, d_both, d_pieces[0]))
        gate_up_grad = weight_grad([residual_all], d_both)
        d_mixed, d_attn, gate_up_grad = fence((d_mixed, d_attn, gate_up_grad))
        gate_up_rows = scatter_dp(gate_up_grad)
        d_attn_part = columns_to_parts(d_attn, me, n)
        d_query, d_key, d_v, inner, gain_sums = attend_back(
            me_ref, d_mixed, q_low, k_low, v_low, qkv, factors, q_gain, k_gain, tables, seg, n
        )
        inner, d_attn_part = fence((inner, d_attn_part))
        inner = sum_stats(inner[:, 0].reshape(2, n, tokens), n).reshape(2, length)
        inner, down_rows = fence((inner, down_rows))
        down_back = send_blocks(row_blocks(down_rows, me, n))
        d_qkv, ends, after, before, far, own = input_back(
            me_ref, d_query, d_key, d_v, qkv, (inner / width).T, factors, w_qkv
        )
        d_qkv, ends, after, before, far, own, down_back = fence(
            (d_qkv, ends, after, before, far, own, down_back)
        )
        ends, *sent = scatter_start(ends, after, before, n)
        sent.append(lax.ppermute(far, "seq", [(0, 2), (3, 1)]))
        attn_grads = attn_grad(me_ref, x_all, d_qkv, pieces, d_attn_part)
        ends, attn_grads = fence((ends, attn_grads))
        attn_rows = scatter_dp(attn_grads)
        far = (far.astype(F32) + ends.astype(F32)).astype(BF)
        sent.append(lax.ppermute(far, "seq", [(1, 3), (2, 0)]))
        input_grad = add_up([d_res, own] + sent)
        spread = lambda g: lax.dynamic_update_slice(jnp.zeros(width, F32), g, (me * part,))
        gains = jnp.stack(
            [spread(gain_sums[0, 0]), spread(gain_sums[1, 0]), grad_attn_gain[0], grad_ff_gain]
        )
        input_grad, gate_up_rows, gains = fence((input_grad, gate_up_rows, gains))
        gate_up_back = send_blocks(row_blocks(gate_up_rows, me, n))
        gains = sum_everywhere(gains, dp_count, n)
        attn_rows, input_grad, gate_up_back, down_back, gains = fence(
            (attn_rows, input_grad, gate_up_back, down_back, gains)
        )
        attn_back = swap_blocks(attn_rows.reshape(n, shard_rows, -1))
        grad_gate, grad_up = join_columns(me_ref, gate_up_back, 2)
        grad_down = join_columns(me_ref, down_back, 1)[0].T
        attn_back, grad_gate, grad_up, grad_down = fence(
            (attn_back, grad_gate, grad_up, grad_down)
        )
        grad_query, grad_key, grad_value, grad_output = (
            joined(attn_back[:, :, j * part : (j + 1) * part]) for j in range(4)
        )

        share = width // devices
        gains = lax.dynamic_slice_in_dim(
            gains, (lax.axis_index("dp") * n + me) * share, share, 1
        )
        return (
            activation[None],
            input_grad[None],
            grad_query,
            grad_key,
            grad_value,
            grad_output,
            grad_gate,
            grad_up,
            grad_down,
            gains[0],
            gains[1],
            gains[2],
            gains[3],
        )

    return shards


def solution(mesh):
    both = P(("dp", "seq"), None)
    tokens = P("dp", "seq", None)
    columns = P(None, ("dp", "seq"))
    gain = P(("dp", "seq"))
    return jax.shard_map(
        build(mesh.shape["dp"], mesh.shape["seq"]),
        mesh=mesh,
        in_specs=(tokens, P("dp", None)) + (both,) * 6 + (columns,) + (P(),) * 4 + (tokens,),
        out_specs=(tokens, tokens) + (both,) * 6 + (columns,) + (gain,) * 4,
        check_vma=False,
    )
```

```python
import functools

import jax
import jax.numpy as jnp
from jax import lax
from jax.experimental import pallas as pl
from jax.experimental.pallas import tpu as pltpu
from jax.sharding import PartitionSpec as P

HD = 128
EPSILON = 1e-06
ROPE_BASE = 500000.0
MASKED = -1e30
LOG2E = 1.4426950408889634
BF = jnp.bfloat16
F32 = jnp.float32


def inv_rms(values):
    return lax.rsqrt(jnp.mean(values * values, axis=-1, keepdims=True) + EPSILON)


def rms_back(normed, factor, gain, grad):
    scaled = grad * gain
    inner = jnp.mean(scaled * normed, axis=-1, keepdims=True)
    return (scaled - normed * inner) * factor


def rope_tables(positions):
    half_dim = HD // 2
    frequency = jnp.power(F32(ROPE_BASE), -jnp.arange(half_dim, dtype=F32) * (2.0 / HD))
    angles = positions[:, None] * frequency[None, :]
    cosine, sine = jnp.cos(angles), jnp.sin(angles)
    return (jnp.concatenate([cosine, cosine], axis=-1), jnp.concatenate([-sine, sine], axis=-1))


def shift(values, count, step):
    return lax.ppermute(values, "seq", [((i + step) % count, i) for i in range(count)])


def gather_raw(values, count):
    far = lax.ppermute(values, "seq", [(i ^ 2, i) for i in range(count)])
    after = lax.ppermute(values, "seq", [(i + 1, i) for i in range(count - 1)])
    before = lax.ppermute(values, "seq", [(i, i + 1) for i in range(count - 1)])
    ends = lax.ppermute(far, "seq", [(2, 3), (1, 0)])
    return [values, after, far, before, ends]


def gather_cyclic(values, count):
    own, after, far, before, ends = gather_raw(values, count)
    me = lax.axis_index("seq")
    after = jnp.where(me == count - 1, ends, after)
    return [own, after, far, jnp.where(me == 0, ends, before)]


def scatter_start(ends, after, before, count):
    ends = lax.ppermute(ends, "seq", [(0, 1), (count - 1, count - 2)])
    step = [(i, i + 1) for i in range(count - 1)]
    after = lax.ppermute(after, "seq", step)
    before = lax.ppermute(before, "seq", [(j, i) for i, j in step])
    return [ends, after, before]


def scatter_far(far, ends, count):
    far_sum = (far + ends.astype(F32)).astype(BF)
    return lax.ppermute(far_sum, "seq", [(i, i ^ 2) for i in range(count)])


def scatter_end(own, got):
    for part in got:
        own = own + part.astype(F32)
    return own


def sum_stats(stats, count):
    total = stats
    for p in range(1, count):
        total = total + jnp.roll(shift(stats, count, p), p, axis=0)
    return total


def stat_columns(stats):
    return stats[:, :2].transpose(0, 2, 1).reshape(-1, 2)


def sum_everywhere(values, dp_count, seq_count):
    for name, count in (("dp", dp_count), ("seq", seq_count)):
        if count & (count - 1):
            values = lax.psum(values, name)
            continue
        bit = 1
        while bit < count:
            values = values + lax.ppermute(values, name, [(i, i ^ bit) for i in range(count)])
            bit *= 2
    return values


def swap_blocks(values):
    return lax.all_to_all(values, "seq", split_axis=0, concat_axis=0, tiled=True)


def part_columns(values, me, count):
    part = values.shape[1] // count
    return [
        lax.dynamic_slice_in_dim(values, (me + p) % count * part, part, 1) for p in range(count)
    ]


def place_blocks(blocks, me, first, width, total=None):
    count = len(blocks)
    rows = blocks[0].shape[0]
    if total is None:
        total = jnp.zeros((count * rows, width), blocks[0].dtype)
    for p, block in enumerate(blocks):
        total = lax.dynamic_update_slice(total, block, ((me - p) % count * rows, first))
    return total


def row_blocks(values, me, count):
    size = values.shape[0] // count
    return [
        lax.dynamic_slice_in_dim(values, (me + p) % count * size, size, 0) for p in range(count)
    ]


def send_blocks(blocks):
    count = len(blocks)
    return blocks[:1] + [
        lax.ppermute(blocks[p], "seq", [(i, (i + p) % count) for i in range(count)])
        for p in range(1, count)
    ]


def join_kernel(sides, me_ref, *refs):
    blocks, outs = refs[:-sides], refs[-sides:]
    for p, block in enumerate(blocks):

        @pl.when(pl.program_id(0) == p)
        def _(block=block):
            for j, out in enumerate(outs):
                tile = min(FF_TILE, out.shape[1])
                for at in range(0, out.shape[1], tile):
                    first = at * sides + j * tile
                    out[:, at : at + tile] = block[:, first : first + tile].astype(F32)


def join_columns(me, blocks, sides):
    count = len(blocks)
    rows, columns = blocks[0].shape
    part = columns // sides
    out = pl.BlockSpec((rows, part), lambda p, me: (0, (me[0] + count - p) % count))
    return pl.pallas_call(
        functools.partial(join_kernel, sides),
        grid_spec=pltpu.PrefetchScalarGridSpec(
            num_scalar_prefetch=1,
            grid=(count,),
            in_specs=[once((rows, columns), lambda p, me: (0, 0))] * count,
            out_specs=[out] * sides,
        ),
        out_shape=[jax.ShapeDtypeStruct((rows, count * part), F32)] * sides,
        compiler_params=params(),
        cost_estimate=cost(0, 0),
        name="join_columns",
    )(me, *blocks)


def gather_dp(values):
    return lax.all_gather(values, "dp", axis=0, tiled=True)


def scatter_dp(values):
    return lax.psum_scatter(values, "dp", scatter_dimension=0, tiled=True)


def softmax_window(q, k_ref, seg_q, seg_row_ref, valid_from, place, tokens, count, span):
    parts = []
    for w in range(span):
        at = ((place - w) % count) * tokens
        scores = lax.dot_general(
            q, k_ref[at : at + tokens, :], (((1,), (1,)), ((), ())), preferred_element_type=F32
        )
        seg = seg_q if w == 0 else jnp.where(valid_from >= w, seg_q, -1)
        allowed = seg == seg_row_ref[:, at : at + tokens]
        if w == 0:
            rows = lax.broadcasted_iota(jnp.int32, (tokens, tokens), 0)
            cols = lax.broadcasted_iota(jnp.int32, (tokens, tokens), 1)
            allowed = allowed & (cols <= rows)
        parts.append(jnp.where(allowed, scores, MASKED))
    top = parts[0]
    for part in parts[1:]:
        top = jnp.maximum(top, part)
    top = jnp.max(top, axis=-1, keepdims=True)
    exps = [jnp.exp2((part - top) * (HD**-0.5 * LOG2E)) for part in parts]
    total = exps[0]
    for part in exps[1:]:
        total = total + part
    inverse = 1.0 / jnp.sum(total, axis=-1, keepdims=True)
    return [part * inverse for part in exps]


def turn(values, cosine, sine):
    return values * cosine + pltpu.roll(values, HD // 2, 1) * sine


def attend_kernel(
    tokens, count, span,
    me_ref, q_ref, k_ref, v_ref, f_ref, qg_ref, kg_ref, cos_ref, sin_ref, segc_ref, segr_ref,
    o_ref, qb_ref, kb_ref, vb_ref,
):
    cosine, sine = cos_ref[...], sin_ref[...]
    factors = f_ref[...]
    qb_ref[...] = turn(q_ref[...] * factors[:, 0:1] * qg_ref[...], cosine, sine).astype(BF)
    kb_ref[...] = turn(k_ref[...] * factors[:, 1:2] * kg_ref[...], cosine, sine).astype(BF)
    vb_ref[...] = v_ref[...].astype(BF)
    for place in range(count):
        rows = slice(place * tokens, (place + 1) * tokens)
        chunk = (me_ref[0] + place) % count
        probs = softmax_window(
            qb_ref[rows, :], kb_ref, segc_ref[rows, :], segr_ref, chunk, place, tokens, count, span
        )
        mixed = None
        for w in range(span):
            at = ((place - w) % count) * tokens
            part = jnp.dot(probs[w].astype(BF), vb_ref[at : at + tokens, :], preferred_element_type=F32)
            mixed = part if mixed is None else mixed + part
        o_ref[rows, :] = mixed.astype(BF)


def attend_back_kernel(
    tokens, count, span, me_ref, *refs
):
    grads_in = refs[:count]
    (q_ref, k_ref, v_ref, qp_ref, kp_ref, f_ref, qg_ref, kg_ref, cos_ref, sin_ref, segc_ref, segr_ref,
     dq_ref, dk_ref, dv_ref, inner_ref, gain_ref, dk_sum, dv_sum) = refs[count:]
    scale = HD**-0.5
    dk_sum[...] = jnp.zeros_like(dk_sum)
    dv_sum[...] = jnp.zeros_like(dv_sum)
    for place in range(count):
        rows = slice(place * tokens, (place + 1) * tokens)
        chunk = (me_ref[0] + place) % count
        q = q_ref[rows, :]
        grad = grads_in[place][...]
        probs = softmax_window(
            q, k_ref, segc_ref[rows, :], segr_ref, chunk, place, tokens, count, span
        )
        grads = []
        inner = None
        for w in range(span):
            at = ((place - w) % count) * tokens
            part = nt_dot(grad, v_ref[at : at + tokens, :])
            grads.append(part)
            inner = probs[w] * part if inner is None else inner + probs[w] * part
            dv_sum[at : at + tokens, :] += lax.dot_general(
                probs[w].astype(BF), grad, (((0,), (0,)), ((), ())), preferred_element_type=F32
            )
        inner = jnp.sum(inner, axis=-1, keepdims=True)
        dq = None
        for w in range(span):
            at = ((place - w) % count) * tokens
            ds = (probs[w] * (grads[w] - inner)).astype(BF)
            part = jnp.dot(ds, k_ref[at : at + tokens, :], preferred_element_type=F32)
            dq = part if dq is None else dq + part
            dk_sum[at : at + tokens, :] += lax.dot_general(
                ds, q, (((0,), (0,)), ((), ())), preferred_element_type=F32
            )
        dq_ref[rows, :] = dq
    first = pl.program_id(0) == 0
    sums = []
    sides = ((dq_ref, dq_ref, qp_ref, qg_ref), (dk_sum, dk_ref, kp_ref, kg_ref))
    for j, (raw_ref, out_ref, proj_ref, g_ref) in enumerate(sides):
        raw = (raw_ref[...] * scale).astype(BF).astype(F32)
        back = turn(raw, cos_ref[...], -sin_ref[...])
        normed = proj_ref[...] * f_ref[:, j : j + 1]
        gain_ref[j] = jnp.broadcast_to(jnp.sum(back * normed, axis=0, keepdims=True), (8, HD))
        back = back * g_ref[...]
        out_ref[...] = back
        sums.append(feature_sums(back * normed))
    sums = two_rows(*sums)
    for place in range(count):
        part = sums[:, place * tokens : (place + 1) * tokens]
        inner_ref[place] = jnp.where(first, part, inner_ref[place] + part)
    dv_ref[...] = dv_sum[...].astype(BF)


def attend_specs(length, heads):
    head = lambda j: pl.BlockSpec((length, HD), lambda h, me: (0, j * heads + h))
    whole = lambda *shape: pl.BlockSpec(shape, lambda h, me: (0, 0))
    gain = pl.BlockSpec((1, HD), lambda h, me: (0, h))
    return head, whole, gain


def attend(me, qkv, factors, q_gain, k_gain, tables, seg, count):
    length = qkv.shape[0]
    part = qkv.shape[1] // 3
    heads = part // HD
    tokens = length // count
    span = min(count, (length // 2 - 1 + tokens - 1) // tokens + 1)
    head, whole, gain = attend_specs(length, heads)
    low = jax.ShapeDtypeStruct((length, part), BF)
    return pl.pallas_call(
        functools.partial(attend_kernel, tokens, count, span),
        grid_spec=pltpu.PrefetchScalarGridSpec(
            num_scalar_prefetch=1,
            grid=(heads,),
            in_specs=[head(0), head(1), head(2), whole(length, 2), gain, gain]
            + [whole(length, HD)] * 2
            + [whole(length, 1), whole(1, length)],
            out_specs=[head(0)] * 4,
        ),
        out_shape=[low] * 4,
        compiler_params=params(),
        cost_estimate=cost(0, 0),
        name="attend",
    )(me, qkv, qkv, qkv, factors, q_gain[None], k_gain[None], *tables, seg[:, None], seg[None])


def attend_back(me, pieces, query, key, value, qkv, factors, q_gain, k_gain, tables, seg, count):
    length, part = query.shape
    heads = part // HD
    tokens = length // count
    span = min(count, (length // 2 - 1 + tokens - 1) // tokens + 1)
    head, whole, gain = attend_specs(length, heads)
    return pl.pallas_call(
        functools.partial(attend_back_kernel, tokens, count, span),
        grid_spec=pltpu.PrefetchScalarGridSpec(
            num_scalar_prefetch=1,
            grid=(heads,),
            in_specs=[pl.BlockSpec((tokens, HD), lambda h, me: (0, h))] * count
            + [head(0)] * 3
            + [head(0), head(1), whole(length, 2), gain, gain]
            + [whole(length, HD)] * 2
            + [whole(length, 1), whole(1, length)],
            out_specs=[head(0)] * 3
            + [
                pl.BlockSpec((count, 8, tokens), lambda h, me: (0, 0, 0)),
                pl.BlockSpec((2, 8, HD), lambda h, me: (0, 0, h)),
            ],
            scratch_shapes=[pltpu.VMEM((length, HD), F32)] * 2,
        ),
        out_shape=[jax.ShapeDtypeStruct((length, part), t) for t in (F32, F32, BF)]
        + [jax.ShapeDtypeStruct(m, F32) for m in ((count, 8, tokens), (2, 8, part))],
        compiler_params=params(),
        cost_estimate=cost(0, 0),
        name="attend_back",
    )(me, *pieces, query, key, value, qkv, qkv, factors, q_gain[None], k_gain[None], *tables,
      seg[:, None], seg[None])


def residual_back_kernel(
    me_ref, own_ref, a_ref, b_ref, c_ref, cot_ref, attn_ref, gain_ref, w_ref, res_ref, d_ref, sum_ref, *outs
):
    step = pl.program_id(0)

    @pl.when(step == 0)
    def _():
        grad = cot_ref[...].astype(F32) + own_ref[...]
        for ref in (a_ref, b_ref, c_ref):
            grad = grad + ref[...].astype(F32)
        res_ref[...] = grad
        attn = attn_ref[...]
        factor = inv_rms(attn)
        normed = attn * factor
        sums = jnp.sum(grad * normed, axis=0, keepdims=True)
        sum_ref[...] = jnp.broadcast_to(sums, sum_ref.shape)
        d_ref[...] = rms_back(normed, factor, gain_ref[...], grad).astype(BF)

    piece = nt_dot(d_ref[...], w_ref[...]).astype(BF)
    for p, out in enumerate(outs):

        @pl.when(step == p)
        def _(out=out):
            out[...] = piece


def residual_back(me, own, got, cot, attn_out, gain, w_first, count):
    tokens, width = own.shape
    part = width // count
    piece = pl.BlockSpec((tokens, part), lambda p, me: (0, 0))
    full = once((tokens, width), lambda p, me: (0, 0))
    whole = lambda rows: pl.BlockSpec((rows, width), lambda p, me: (0, 0))
    return pl.pallas_call(
        residual_back_kernel,
        grid_spec=pltpu.PrefetchScalarGridSpec(
            num_scalar_prefetch=1,
            grid=(count,),
            in_specs=[full] * 6
            + [whole(1), pl.BlockSpec((part, width), lambda p, me: ((me[0] + p) % count, 0))],
            out_specs=[whole(tokens), whole(tokens), whole(8)] + [piece] * count,
        ),
        out_shape=[
            jax.ShapeDtypeStruct((tokens, width), F32),
            jax.ShapeDtypeStruct((tokens, width), BF),
            jax.ShapeDtypeStruct((8, width), F32),
        ]
        + [jax.ShapeDtypeStruct((tokens, part), BF)] * count,
        compiler_params=params(),
        cost_estimate=cost(LATE_COST, 0),
        name="residual_back",
    )(me, own, *got, cot, attn_out, gain[None], w_first)


def input_back_kernel(
    part, me_ref, q_ref, k_ref, v_ref, qp_ref, kp_ref, in_ref, f_ref, w_ref, d_ref, ends_ref, *outs
):
    for j, (grad, proj) in enumerate(((q_ref, qp_ref), (k_ref, kp_ref))):
        factor = f_ref[:, j : j + 1]
        normed = proj[...] * factor
        low = ((grad[...] - normed * in_ref[:, j : j + 1]) * factor).astype(BF)
        d_ref[:, j * part : (j + 1) * part] = low
    d_ref[:, 2 * part :] = v_ref[...]
    total = nt_dot(d_ref[...], w_ref[...])
    step = pl.program_id(0)
    for j, out in enumerate(outs):

        @pl.when(step == j)
        def _(out=out):
            out[...] = total.astype(out.dtype)

    @pl.when((step == 0) | ((step == 1) & (me_ref[0] == 0)))
    def _():
        ends_ref[...] = total.astype(BF)


def input_back(me, d_query, d_key, d_v, qkv, inner, factors, w_qkv):
    length, part = d_query.shape
    width = w_qkv.shape[0]
    tokens = length // 4
    place = lambda t: jnp.where(t == 0, 1, jnp.where(t == 1, 3, jnp.where(t == 2, 2, 0)))
    rows = lambda columns, at=0: pl.BlockSpec((tokens, columns), lambda t, me: (place(t), at))
    kinds = (BF, BF, BF, BF, F32)
    return pl.pallas_call(
        functools.partial(input_back_kernel, part),
        grid_spec=pltpu.PrefetchScalarGridSpec(
            num_scalar_prefetch=1,
            grid=(4,),
            in_specs=[rows(part)] * 3
            + [rows(part), rows(part, 1), rows(2), rows(2)]
            + [once((width, 3 * part), lambda t, me: (0, 0))],
            out_specs=[rows(3 * part)]
            + [pl.BlockSpec((tokens, width), lambda t, me: (0, 0))] * len(kinds),
        ),
        out_shape=[jax.ShapeDtypeStruct((length, 3 * part), BF)]
        + [jax.ShapeDtypeStruct((tokens, width), kind) for kind in kinds],
        compiler_params=params(),
        cost_estimate=cost(0, 0),
        name="input_back",
    )(me, d_query, d_key, d_v, qkv, qkv, inner, factors, w_qkv)


def add_up_kernel(*refs):
    total = refs[0][...]
    for ref in refs[1:-1]:
        total = total + ref[...].astype(F32)
    refs[-1][...] = total.astype(BF)


def add_up(parts):
    tokens, width = parts[0].shape
    tile = tokens // 4
    block = pl.BlockSpec((tile, width), lambda i: (i, 0))
    return pl.pallas_call(
        add_up_kernel,
        grid=(4,),
        in_specs=[block] * len(parts),
        out_specs=block,
        out_shape=jax.ShapeDtypeStruct((tokens, width), BF),
        compiler_params=params(),
        cost_estimate=cost(LATE_COST, 0),
        name="add_up",
    )(*parts)


def tn_dot(left, right):
    return lax.dot_general(left, right, (((0,), (0,)), ((), ())), preferred_element_type=F32)


def weight_grad_kernel(lefts, right_ref, out_ref):
    total, at = None, 0
    for left in lefts:
        rows = left.shape[0]
        product = tn_dot(left[...], right_ref[at : at + rows, :])
        total = product if total is None else total + product
        at += rows
    out_ref[...] = total.astype(BF)


def weight_grad(lefts, right):
    width = lefts[0].shape[1]
    length, columns = right.shape
    tile, wide = 256, min(columns, 2048)
    return pl.pallas_call(
        lambda *refs: weight_grad_kernel(refs[:-2], *refs[-2:]),
        grid=(columns // wide, width // tile),
        in_specs=[pl.BlockSpec((left.shape[0], tile), lambda j, i: (0, i)) for left in lefts]
        + [pl.BlockSpec((length, wide), lambda j, i: (0, j))],
        out_specs=pl.BlockSpec((tile, wide), lambda j, i: (i, j)),
        out_shape=jax.ShapeDtypeStruct((width, columns), BF),
        compiler_params=params(),
        cost_estimate=cost(0, 0),
        name="weight_grad",
    )(*lefts, right)


def attn_grad_kernel(count, me_ref, x_ref, d_ref, *refs):
    pieces, parts, out_ref = refs[:count], refs[count : 2 * count], refs[-1]
    columns = d_ref.shape[1]
    out_ref[:, :columns] = tn_dot(x_ref[...], d_ref[...]).astype(BF)
    source = (pl.program_id(0) // (pl.num_programs(0) // count) + count - me_ref[0]) % count
    for p, piece in enumerate(pieces):

        @pl.when(source == p)
        def _(p=p, piece=piece):
            total, tokens = None, parts[0].shape[0]
            for q in range(count):
                rows = slice(q * tokens, (q + 1) * tokens)
                product = tn_dot(piece[rows, :], parts[(q + p) % count][...])
                total = product if total is None else total + product
            out_ref[:, columns:] = total.astype(BF)


def attn_grad(me, x_all, d_qkv, pieces, d_parts):
    count = len(pieces)
    length, width = x_all.shape
    columns, part = d_qkv.shape[1], d_parts[0].shape[1]
    tile = min(256, part)
    per_part = part // tile
    return pl.pallas_call(
        functools.partial(attn_grad_kernel, count),
        grid_spec=pltpu.PrefetchScalarGridSpec(
            num_scalar_prefetch=1,
            grid=(width // tile,),
            in_specs=[
                pl.BlockSpec((length, tile), lambda i, me: (0, i)),
                once((length, columns), lambda i, me: (0, 0)),
            ]
            + [pl.BlockSpec((length, tile), lambda i, me: (0, i % per_part))] * count
            + [once((length // count, part), lambda i, me: (0, 0))] * count,
            out_specs=pl.BlockSpec((tile, columns + part), lambda i, me: (i, 0)),
        ),
        out_shape=jax.ShapeDtypeStruct((width, columns + part), BF),
        compiler_params=params(),
        cost_estimate=cost(SIDE_COST, 0),
        name="attn_grad",
    )(me, x_all, d_qkv, *pieces, *d_parts)


def cost(flops, moved, exps=0):
    return pl.CostEstimate(flops=flops, bytes_accessed=moved, transcendentals=exps)


def params():
    return pltpu.CompilerParams(vmem_limit_bytes=56 << 20)


def once(shape, index):
    return pl.BlockSpec(shape, index, pipeline_mode=pl.Buffered(1))


def nt_dot(left, right):
    return lax.dot_general(left, right, (((1,), (1,)), ((), ())), preferred_element_type=F32)


def feature_sums(values):
    ones = jnp.ones((8, values.shape[1]), BF)
    total = None
    for _ in range(3):
        term = values.astype(BF)
        values = values - term.astype(F32)
        total = nt_dot(ones, term) if total is None else total + nt_dot(ones, term)
    return total


def two_rows(first, second):
    return jnp.where(lax.broadcasted_iota(jnp.int32, first.shape, 0) == 0, first, second)


def qkv_kernel(part, saved, me_ref, *refs):
    chunks, w_ref, (x_ref, qkv_ref, sq_ref) = refs[: -4 - saved], refs[-4 - saved], refs[-3:]
    step, me = pl.program_id(0), me_ref[0]
    at_end = (step == 0) & (me == 3) | (step == 1) & (me == 0) if len(chunks) == 3 else step < 0
    for q in range(2):

        @pl.when((step == q) & jnp.logical_not(at_end))
        def _(q=q):
            x_ref[...] = chunks[q][...]

    @pl.when(at_end)
    def _():
        x_ref[...] = chunks[-1][...]

    qkv = jnp.dot(x_ref[...], w_ref[...], preferred_element_type=F32)
    qkv_ref[...] = qkv
    q, k = (qkv[:, j * part : (j + 1) * part] for j in range(2))
    sq_ref[0] = two_rows(feature_sums(q * q), feature_sums(k * k))


def qkv_project(me, first, chunks, w_qkv, saved=()):
    tokens, width = chunks[0].shape
    columns = w_qkv.shape[1]
    length = 4 * tokens
    place = lambda q: 2 * q + first
    return pl.pallas_call(
        functools.partial(qkv_kernel, columns // 3, len(saved)),
        grid_spec=pltpu.PrefetchScalarGridSpec(
            num_scalar_prefetch=1,
            grid=(2,),
            in_specs=[once((tokens, width), lambda q, me: (0, 0))] * len(chunks)
            + [once((width, columns), lambda q, me: (0, 0))]
            + [pl.BlockSpec(memory_space=pl.ANY)] * len(saved),
            out_specs=[
                pl.BlockSpec((tokens, width), lambda q, me: (place(q), 0)),
                pl.BlockSpec((tokens, columns), lambda q, me: (place(q), 0)),
                pl.BlockSpec((1, 8, tokens), lambda q, me: (place(q), 0, 0)),
            ],
        ),
        out_shape=[
            jax.ShapeDtypeStruct((length, width), BF),
            jax.ShapeDtypeStruct((length, columns), F32),
            jax.ShapeDtypeStruct((4, 8, tokens), F32),
        ],
        input_output_aliases={2 + len(chunks) + j: j for j in range(len(saved))},
        compiler_params=params(),
        cost_estimate=cost(0, 0),
        name="qkv_project",
    )(me, *chunks, w_qkv, *saved)


FF_TILE = 512
LATE_COST = 10**12
SIDE_COST = 10**11


def ff_finish(step, product, acc, me_ref, outs):
    @pl.when(step == 0)
    def _():
        acc[...] = product

    @pl.when(step > 0)
    def _():
        acc[...] += product

    @pl.when(step == pl.num_programs(0) - 1)
    def _():
        tokens = outs[0].shape[0]
        for j, out in enumerate(outs[:2]):
            out[...] = acc[j * tokens : (j + 1) * tokens].astype(out.dtype)
        if len(outs) == 3:
            at = pl.multiple_of(jnp.where(me_ref[0] == 0, tokens, 0), tokens)
            outs[2][...] = acc[pl.ds(at, tokens), :].astype(BF)


def ff_kernel(saved, me_ref, h_ref, wg_ref, wu_ref, wd_ref, *refs):
    gate_ref, up_ref, hid_ref = refs[saved : saved + 3]
    h = h_ref[...]
    gate = jnp.dot(h, wg_ref[...], preferred_element_type=F32)
    up = jnp.dot(h, wu_ref[...], preferred_element_type=F32)
    hidden = (gate * (1.0 / (1.0 + jnp.exp(-gate))) * up).astype(BF)
    gate_ref[...] = gate
    up_ref[...] = up
    hid_ref[...] = hidden
    product = nt_dot(hidden, wd_ref[...])
    ff_finish(pl.program_id(0), product, refs[-1], me_ref, refs[saved + 3 : -1])


def ff_back_kernel(saved, groups, me_ref, *refs):
    d_refs, (wg_ref, wu_ref, wd_ref, gate_ref, up_ref) = refs[:groups], refs[groups : groups + 5]
    refs = refs[groups + 5 :]
    dgu_ref = refs[saved]
    tile = wg_ref.shape[1]
    d_ff = d_refs[0][...] if groups == 1 else jnp.concatenate([d[...] for d in d_refs], axis=0)
    d_hidden = jnp.dot(d_ff, wd_ref[...], preferred_element_type=F32)
    gate = gate_ref[...]
    sig = 1.0 / (1.0 + jnp.exp(-gate))
    d_gate = (d_hidden * up_ref[...] * sig * (1.0 + gate * (1.0 - sig))).astype(BF)
    d_up = (d_hidden * gate * sig).astype(BF)
    dgu_ref[:, :tile] = d_gate
    dgu_ref[:, tile:] = d_up
    product = nt_dot(d_gate, wg_ref[...]) + nt_dot(d_up, wu_ref[...])
    ff_finish(pl.program_id(0), product, refs[-1], me_ref, refs[saved + 1 : -1])


def ff_specs(width, tile, gate_at, down_at):
    return [
        pl.BlockSpec((width, tile), lambda t: (0, gate_at // tile + t)),
        pl.BlockSpec((width, tile), lambda t: (0, t)),
        pl.BlockSpec((width, tile), lambda t: (0, down_at // tile + t)),
    ]


def ff_forward(me, residual_all, w_first, w_second, place, kinds, saved=()):
    length, width = residual_all.shape
    tokens = length // 4
    group = min(len(kinds), 2)
    rows = group * tokens
    ff_part = w_second.shape[1] // 2
    tile = min(FF_TILE, ff_part)
    block = pl.BlockSpec((rows, tile), lambda t: (place // group, t))
    whole = pl.BlockSpec((tokens, width), lambda t: (0, 0))
    shape = lambda kind: jax.ShapeDtypeStruct((length, ff_part), kind)
    return pl.pallas_call(
        functools.partial(ff_kernel, len(saved)),
        grid=(ff_part // tile,),
        in_specs=[pl.BlockSpec(memory_space=pltpu.SMEM)]
        + [once((rows, width), lambda t: (place // group, 0))]
        + ff_specs(width, tile, w_first.shape[1] - ff_part, ff_part)
        + [pl.BlockSpec(memory_space=pl.ANY)] * len(saved),
        out_specs=[block] * 3 + [whole] * len(kinds),
        out_shape=[shape(F32), shape(F32), shape(BF)]
        + [jax.ShapeDtypeStruct((tokens, width), kind) for kind in kinds],
        scratch_shapes=[pltpu.VMEM((rows, width), F32)],
        input_output_aliases={5 + j: j for j in range(len(saved))},
        compiler_params=params(),
        cost_estimate=cost(0, 0),
        name="ff_forward",
    )(me, residual_all, w_first, w_second, w_second, *saved)


def ff_backward(me, d_ffs, w_first, w_second, gate, up, place, kinds, saved=()):
    tokens, width = d_ffs[0].shape
    group = len(d_ffs)
    rows = group * tokens
    length = gate.shape[0]
    ff_part = w_second.shape[1] // 2
    tile = min(FF_TILE, ff_part)
    block = pl.BlockSpec((rows, tile), lambda t: (place // group, t))
    whole = pl.BlockSpec((tokens, width), lambda t: (0, 0))
    return pl.pallas_call(
        functools.partial(ff_back_kernel, len(saved), group),
        grid=(ff_part // tile,),
        in_specs=[pl.BlockSpec(memory_space=pltpu.SMEM)]
        + [once((tokens, width), lambda t: (0, 0))] * group
        + ff_specs(width, tile, w_first.shape[1] - ff_part, ff_part)
        + [block, block]
        + [pl.BlockSpec(memory_space=pl.ANY)] * len(saved),
        out_specs=[pl.BlockSpec((rows, 2 * tile), lambda t: (place // group, t))]
        + [whole] * len(kinds),
        out_shape=[jax.ShapeDtypeStruct((length, 2 * ff_part), BF)]
        + [jax.ShapeDtypeStruct((tokens, width), kind) for kind in kinds],
        scratch_shapes=[pltpu.VMEM((rows, width), F32)],
        input_output_aliases={6 + group + j: j for j in range(len(saved))},
        compiler_params=params(),
        cost_estimate=cost(SIDE_COST, 0),
        name="ff_backward",
    )(me, *d_ffs, w_first, w_second, w_second, gate, up, *saved)


def out_kernel(count, part, *refs):
    me_ref, pieces, (w_ref, x_ref, g_ref, res_ref, own_ref) = refs[0], refs[1:-5], refs[-5:]
    total = None
    for p, piece in enumerate(pieces):
        rows = pl.ds(pl.multiple_of((me_ref[0] + p) % count * part, part), part)
        product = jnp.dot(piece[...], w_ref[rows, :], preferred_element_type=F32)
        total = product if total is None else total + product
    normed = total * inv_rms(total)
    res_ref[...] = (x_ref[...].astype(F32) + normed * g_ref[...]).astype(BF)

    @pl.when(pl.program_id(0) == 0)
    def _():
        own_ref[...] = total


def ff_place(q):
    return jnp.where(q == 0, 3, jnp.where(q == 3, 1, jnp.where(q == 2, 2, 0)))


def out_project(me, pieces, w_out, x_all, gain, count):
    length, width = x_all.shape
    tokens = length // count
    part = pieces[0].shape[1]
    rolled = lambda p: pl.BlockSpec((tokens, part), lambda q, me: ((q + count - p) % count, 0))
    chunk = pl.BlockSpec((tokens, width), lambda q, me: (q, 0))
    moved = pl.BlockSpec((tokens, width), lambda q, me: (ff_place(q), 0))
    return pl.pallas_call(
        functools.partial(out_kernel, count, part),
        grid_spec=pltpu.PrefetchScalarGridSpec(
            num_scalar_prefetch=1,
            grid=(count,),
            in_specs=[rolled(p) for p in range(count)]
            + [pl.BlockSpec((width, width), lambda q, me: (0, 0), pipeline_mode=pl.Buffered(1))]
            + [chunk, pl.BlockSpec((1, width), lambda q, me: (0, 0))],
            out_specs=[moved, pl.BlockSpec((tokens, width), lambda q, me: (0, 0))],
        ),
        out_shape=[
            jax.ShapeDtypeStruct((length, width), BF),
            jax.ShapeDtypeStruct((tokens, width), F32),
        ],
        compiler_params=params(),
        cost_estimate=cost(0, 0),
        name="out_project",
    )(me, *pieces, w_out, x_all, gain[None])


def columns_to_parts(values, me, count):
    part = values.shape[1] // count
    columns = lambda p: lax.dynamic_slice_in_dim(values, (me + p) % count * part, part, 1)
    got = [columns(0)] + [
        lax.ppermute(columns(p), "seq", [(i, (i + p) % count) for i in range(count)])
        for p in range(1, count)
    ]
    return [got[(count - q) % count] for q in range(count)]


def build(dp_count, seq_count):
    assert seq_count == 4

    def shards(
        layer_input,
        segments,
        w_query,
        w_key,
        w_value,
        w_output,
        w_gate,
        w_up,
        w_down,
        query_gain,
        key_gain,
        attn_gain,
        ff_gain,
        cotangent,
    ):
        n = seq_count
        tokens, width = layer_input.shape[1:]
        shard_rows = w_query.shape[0]
        part = width // n
        ff_part = w_gate.shape[1] // n
        length = n * tokens
        devices = dp_count * n
        me = lax.axis_index("seq")
        me_ref = me[None].astype(jnp.int32)
        cot = cotangent[0]
        by_part = lambda w: w.reshape(shard_rows, n, -1).transpose(1, 0, 2)
        rows_of = lambda blocks: blocks.reshape(n * shard_rows, -1)

        fence = lax.optimization_barrier
        qkv_blocks = jnp.concatenate([by_part(w) for w in (w_query, w_key, w_value)], axis=2)
        qkv_blocks = swap_blocks(qkv_blocks)
        w_qkv = gather_dp(rows_of(qkv_blocks))
        natural = jnp.arange(length, dtype=jnp.int32)
        positions = (natural + me * tokens) % length
        seg_row = segments[0]
        seg = lax.dynamic_slice_in_dim(
            jnp.concatenate([seg_row, seg_row]), me * tokens, length, 0
        )
        tables = rope_tables(positions.astype(F32))
        own_gain = lambda g: lax.dynamic_slice_in_dim(g, me * part, part, 0)
        q_gain = own_gain(query_gain)
        k_gain = own_gain(key_gain)

        up_columns, down_columns = (part_columns(w, me, n) for w in (w_up, w_down.T))
        ready = (seg, tables, q_gain, k_gain, up_columns, down_columns)
        qkv_blocks, w_output, w_gate = fence((qkv_blocks, w_output, w_gate))
        out_blocks = gather_cyclic(w_output, n)
        gate_blocks = send_blocks(part_columns(w_gate, me, n))
        out_blocks, gate_blocks, x_own, ready = fence(
            (out_blocks, gate_blocks, layer_input[0], ready)
        )
        seg, tables, q_gain, k_gain, up_columns, down_columns = ready
        out_blocks = out_blocks[:1] + out_blocks[:0:-1]
        w_first = place_blocks(out_blocks, me, 0, width + ff_part)
        w_first = gather_dp(place_blocks(gate_blocks, me, width, width + ff_part, w_first))
        x_own, x_after, x_far, x_before, x_ends = gather_raw(x_own, n)
        saved = qkv_project(me_ref, 0, [x_own, x_far], w_qkv)
        x_sides, saved, up_columns = fence(([x_after, x_before, x_ends], saved, up_columns))
        up_blocks = send_blocks(up_columns)
        x_all, qkv, squares = qkv_project(me_ref, 1, x_sides, w_qkv, saved)
        squares, up_blocks = fence((squares, up_blocks))

        squares = sum_stats(squares, n)
        squares, down_columns = fence((squares, down_columns))
        down_blocks = send_blocks(down_columns)
        factors = lax.rsqrt(stat_columns(squares) / width + EPSILON)
        mixed, q_low, k_low, v_low = attend(me_ref, qkv, factors, q_gain, k_gain, tables, seg, n)

        mixed, down_blocks = fence((mixed, down_blocks))
        w_second = place_blocks(up_blocks, me, 0, 2 * ff_part)
        w_second = gather_dp(place_blocks(down_blocks, me, ff_part, 2 * ff_part, w_second))
        pieces = gather_cyclic(mixed, n)
        residual_all, attn_out = out_project(me_ref, pieces, w_first, x_all, attn_gain, n)
        attn_factor = inv_rms(attn_out)
        attn_normed = attn_out * attn_factor
        residual = x_own.astype(F32) + attn_normed * attn_gain

        *saved, after, before, ends = ff_forward(
            me_ref, residual_all, w_first, w_second, 0, (BF, BF, BF)
        )
        sent = scatter_start(ends, after, before, n)
        *saved, far = ff_forward(me_ref, residual_all, w_first, w_second, 2, (F32,), saved)
        far, sent[0], residual_late = fence((far, sent[0], residual_all))
        sent[0] = scatter_far(far, sent[0], n)
        gate, up, hidden, own = ff_forward(
            me_ref, residual_late, w_first, w_second, 3, (F32,), saved
        )
        ff_out = scatter_end(own, sent)
        ff_factor = inv_rms(ff_out)
        ff_normed = ff_out * ff_factor
        activation = (residual + ff_normed * ff_gain).astype(BF)
        grad_ff_gain = jnp.sum(cot.astype(F32) * ff_normed, axis=0)
        d_ff = rms_back(ff_normed, ff_factor, ff_gain, cot.astype(F32)).astype(BF)
        d_ffs = gather_cyclic(d_ff, n)
        d_both, own = ff_backward(me_ref, d_ffs[:1], w_first, w_second, gate, up, 3, (F32,))
        d_ffs, d_both = fence((d_ffs, d_both))
        d_both, after, before, ends = ff_backward(
            me_ref, d_ffs[1::2], w_first, w_second, gate, up, 0, (BF, BF, BF), (d_both,)
        )
        sent = scatter_start(ends, after, before, n)
        d_both, far = ff_backward(
            me_ref, d_ffs[2:3], w_first, w_second, gate, up, 2, (F32,), (d_both,)
        )
        d_both, far, sent[0], d_ffs, hidden = fence((d_both, far, sent[0], d_ffs, hidden))
        sent[0] = scatter_far(far, sent[0], n)
        joined = lambda g: g.transpose(1, 0, 2).reshape(shard_rows, -1).astype(F32)
        down_grad = weight_grad([d_ffs[1], d_ffs[3], d_ffs[2], d_ffs[0]], hidden)
        down_rows = scatter_dp(down_grad)
        down_grad, sent = fence((down_grad, sent))
        d_res, d_attn, grad_attn_gain, *d_pieces = residual_back(
            me_ref, own, sent, cot, attn_out, attn_gain, w_first, n
        )
        d_mixed = [d_pieces[0]] + [None] * (n - 1)
        for p in range(1, n):
            d_mixed[n - p] = lax.ppermute(
                d_pieces[p], "seq", [(i, (i + p) % n) for i in range(n)]
            )
        residual_all, d_both, _ = fence((residual_all, d_both, d_pieces[0]))
        gate_up_grad = weight_grad([residual_all], d_both)
        d_mixed, d_attn, gate_up_grad = fence((d_mixed, d_attn, gate_up_grad))
        gate_up_rows = scatter_dp(gate_up_grad)
        d_attn_part = columns_to_parts(d_attn, me, n)
        d_query, d_key, d_v, inner, gain_sums = attend_back(
            me_ref, d_mixed, q_low, k_low, v_low, qkv, factors, q_gain, k_gain, tables, seg, n
        )
        inner, d_attn_part, down_back = fence(
            (inner, d_attn_part, row_blocks(down_rows, me, n))
        )
        inner = sum_stats(inner, n)
        inner, down_back = fence((inner, down_back))
        down_back = send_blocks(down_back)
        d_qkv, ends, after, before, far, own = input_back(
            me_ref, d_query, d_key, d_v, qkv, stat_columns(inner) / width, factors, w_qkv
        )
        d_qkv, ends, after, before, far, own, down_back = fence(
            (d_qkv, ends, after, before, far, own, down_back)
        )
        ends, *sent = scatter_start(ends, after, before, n)
        sent.append(lax.ppermute(far, "seq", [(0, 2), (3, 1)]))
        attn_grads = attn_grad(me_ref, x_all, d_qkv, pieces, d_attn_part)
        ends, attn_grads = fence((ends, attn_grads))
        attn_rows = scatter_dp(attn_grads)
        far = (far.astype(F32) + ends.astype(F32)).astype(BF)
        sent.append(lax.ppermute(far, "seq", [(1, 3), (2, 0)]))
        gate_up_back = row_blocks(gate_up_rows, me, n)
        sent, gate_up_back = fence((sent, gate_up_back))
        input_grad = add_up([d_res, own] + sent)
        spread = lambda g: lax.dynamic_update_slice(jnp.zeros(width, F32), g, (me * part,))
        gains = jnp.stack(
            [spread(gain_sums[0, 0]), spread(gain_sums[1, 0]), grad_attn_gain[0], grad_ff_gain]
        )
        input_grad, gains = fence((input_grad, gains))
        gate_up_back = send_blocks(gate_up_back)
        gains = sum_everywhere(gains, dp_count, n)
        attn_rows, input_grad, gate_up_back, down_back, gains = fence(
            (attn_rows, input_grad, gate_up_back, down_back, gains)
        )
        attn_back = swap_blocks(attn_rows.reshape(n, shard_rows, -1))
        grad_gate, grad_up = join_columns(me_ref, gate_up_back, 2)
        grad_down = join_columns(me_ref, down_back, 1)[0].T
        attn_back, grad_gate, grad_up, grad_down = fence(
            (attn_back, grad_gate, grad_up, grad_down)
        )
        grad_query, grad_key, grad_value, grad_output = (
            joined(attn_back[:, :, j * part : (j + 1) * part]) for j in range(4)
        )

        share = width // devices
        gains = lax.dynamic_slice_in_dim(
            gains, (lax.axis_index("dp") * n + me) * share, share, 1
        )
        return (
            activation[None],
            input_grad[None],
            grad_query,
            grad_key,
            grad_value,
            grad_output,
            grad_gate,
            grad_up,
            grad_down,
            gains[0],
            gains[1],
            gains[2],
            gains[3],
        )

    return shards


def solution(mesh):
    both = P(("dp", "seq"), None)
    tokens = P("dp", "seq", None)
    columns = P(None, ("dp", "seq"))
    gain = P(("dp", "seq"))
    return jax.shard_map(
        build(mesh.shape["dp"], mesh.shape["seq"]),
        mesh=mesh,
        in_specs=(tokens, P("dp", None)) + (both,) * 6 + (columns,) + (P(),) * 4 + (tokens,),
        out_specs=(tokens, tokens) + (both,) * 6 + (columns,) + (gain,) * 4,
        check_vma=False,
    )
```

```python
import functools

import jax
import jax.numpy as jnp
from jax import lax
from jax.experimental import pallas as pl
from jax.experimental.pallas import tpu as pltpu
from jax.sharding import PartitionSpec as P

HD = 128
EPSILON = 1e-06
ROPE_BASE = 500000.0
MASKED = -1e30
LOG2E = 1.4426950408889634
BF = jnp.bfloat16
F32 = jnp.float32


def inv_rms(values):
    return lax.rsqrt(jnp.mean(values * values, axis=-1, keepdims=True) + EPSILON)


def rms_back(normed, factor, gain, grad):
    scaled = grad * gain
    inner = jnp.mean(scaled * normed, axis=-1, keepdims=True)
    return (scaled - normed * inner) * factor


def rope_tables(positions):
    half_dim = HD // 2
    frequency = jnp.power(F32(ROPE_BASE), -jnp.arange(half_dim, dtype=F32) * (2.0 / HD))
    angles = positions[:, None] * frequency[None, :]
    cosine, sine = jnp.cos(angles), jnp.sin(angles)
    return (jnp.concatenate([cosine, cosine], axis=-1), jnp.concatenate([-sine, sine], axis=-1))


def shift(values, count, step):
    return lax.ppermute(values, "seq", [((i + step) % count, i) for i in range(count)])


def gather_raw(values, count):
    far = lax.ppermute(values, "seq", [(i ^ 2, i) for i in range(count)])
    after = lax.ppermute(values, "seq", [(i + 1, i) for i in range(count - 1)])
    before = lax.ppermute(values, "seq", [(i, i + 1) for i in range(count - 1)])
    ends = lax.ppermute(far, "seq", [(2, 3), (1, 0)])
    return [values, after, far, before, ends]


def gather_cyclic(values, count):
    own, after, far, before, ends = gather_raw(values, count)
    me = lax.axis_index("seq")
    after = jnp.where(me == count - 1, ends, after)
    return [own, after, far, jnp.where(me == 0, ends, before)]


def scatter_start(ends, after, before, count):
    ends = lax.ppermute(ends, "seq", [(0, 1), (count - 1, count - 2)])
    step = [(i, i + 1) for i in range(count - 1)]
    after = lax.ppermute(after, "seq", step)
    before = lax.ppermute(before, "seq", [(j, i) for i, j in step])
    return [ends, after, before]


def scatter_far(far, ends, count):
    far_sum = (far + ends.astype(F32)).astype(BF)
    return lax.ppermute(far_sum, "seq", [(i, i ^ 2) for i in range(count)])


def scatter_end(own, got):
    for part in got:
        own = own + part.astype(F32)
    return own


def sum_stats(stats, count):
    total = stats
    for p in range(1, count):
        total = total + jnp.roll(shift(stats, count, p), p, axis=0)
    return total


def stat_columns(stats):
    return stats[:, :2].transpose(0, 2, 1).reshape(-1, 2)


def sum_everywhere(values, dp_count, seq_count):
    for name, count in (("dp", dp_count), ("seq", seq_count)):
        if count & (count - 1):
            values = lax.psum(values, name)
            continue
        bit = 1
        while bit < count:
            values = values + lax.ppermute(values, name, [(i, i ^ bit) for i in range(count)])
            bit *= 2
    return values


def swap_blocks(values):
    return lax.all_to_all(values, "seq", split_axis=0, concat_axis=0, tiled=True)


def part_columns(values, me, count):
    part = values.shape[1] // count
    return [
        lax.dynamic_slice_in_dim(values, (me + p) % count * part, part, 1) for p in range(count)
    ]


def place_blocks(blocks, me, first, width, total=None):
    count = len(blocks)
    rows = blocks[0].shape[0]
    if total is None:
        total = jnp.zeros((count * rows, width), blocks[0].dtype)
    for p, block in enumerate(blocks):
        total = lax.dynamic_update_slice(total, block, ((me - p) % count * rows, first))
    return total


def row_blocks(values, me, count):
    size = values.shape[0] // count
    return [
        lax.dynamic_slice_in_dim(values, (me + p) % count * size, size, 0) for p in range(count)
    ]


def send_blocks(blocks):
    count = len(blocks)
    return blocks[:1] + [
        lax.ppermute(blocks[p], "seq", [(i, (i + p) % count) for i in range(count)])
        for p in range(1, count)
    ]


def join_kernel(sides, me_ref, *refs):
    blocks, outs = refs[:-sides], refs[-sides:]
    for p, block in enumerate(blocks):

        @pl.when(pl.program_id(0) == p)
        def _(block=block):
            for j, out in enumerate(outs):
                tile = min(FF_TILE, out.shape[1])
                for at in range(0, out.shape[1], tile):
                    first = at * sides + j * tile
                    out[:, at : at + tile] = block[:, first : first + tile].astype(F32)


def join_columns(me, blocks, sides):
    count = len(blocks)
    rows, columns = blocks[0].shape
    part = columns // sides
    out = pl.BlockSpec((rows, part), lambda p, me: (0, (me[0] + count - p) % count))
    return pl.pallas_call(
        functools.partial(join_kernel, sides),
        grid_spec=pltpu.PrefetchScalarGridSpec(
            num_scalar_prefetch=1,
            grid=(count,),
            in_specs=[once((rows, columns), lambda p, me: (0, 0))] * count,
            out_specs=[out] * sides,
        ),
        out_shape=[jax.ShapeDtypeStruct((rows, count * part), F32)] * sides,
        compiler_params=params(),
        cost_estimate=cost(0, 0),
        name="join_columns",
    )(me, *blocks)


def gather_dp(values):
    return lax.all_gather(values, "dp", axis=0, tiled=True)


def scatter_dp(values):
    return lax.psum_scatter(values, "dp", scatter_dimension=0, tiled=True)


def softmax_window(q, k_ref, seg_q, seg_row_ref, valid_from, place, tokens, count, span):
    parts = []
    for w in range(span):
        at = ((place - w) % count) * tokens
        scores = lax.dot_general(
            q, k_ref[at : at + tokens, :], (((1,), (1,)), ((), ())), preferred_element_type=F32
        )
        seg = seg_q if w == 0 else jnp.where(valid_from >= w, seg_q, -1)
        allowed = seg == seg_row_ref[:, at : at + tokens]
        if w == 0:
            rows = lax.broadcasted_iota(jnp.int32, (tokens, tokens), 0)
            cols = lax.broadcasted_iota(jnp.int32, (tokens, tokens), 1)
            allowed = allowed & (cols <= rows)
        parts.append(jnp.where(allowed, scores, MASKED))
    top = parts[0]
    for part in parts[1:]:
        top = jnp.maximum(top, part)
    top = jnp.max(top, axis=-1, keepdims=True)
    exps = [jnp.exp2((part - top) * (HD**-0.5 * LOG2E)) for part in parts]
    total = exps[0]
    for part in exps[1:]:
        total = total + part
    inverse = 1.0 / jnp.sum(total, axis=-1, keepdims=True)
    return [part * inverse for part in exps]


def turn(values, cosine, sine):
    return values * cosine + pltpu.roll(values, HD // 2, 1) * sine


def attend_kernel(
    tokens, count, span,
    me_ref, q_ref, k_ref, v_ref, f_ref, qg_ref, kg_ref, cos_ref, sin_ref, segc_ref, segr_ref,
    o_ref, qb_ref, kb_ref, vb_ref,
):
    cosine, sine = cos_ref[...], sin_ref[...]
    factors = f_ref[...]
    qb_ref[...] = turn(q_ref[...] * factors[:, 0:1] * qg_ref[...], cosine, sine).astype(BF)
    kb_ref[...] = turn(k_ref[...] * factors[:, 1:2] * kg_ref[...], cosine, sine).astype(BF)
    vb_ref[...] = v_ref[...].astype(BF)
    for place in range(count):
        rows = slice(place * tokens, (place + 1) * tokens)
        chunk = (me_ref[0] + place) % count
        probs = softmax_window(
            qb_ref[rows, :], kb_ref, segc_ref[rows, :], segr_ref, chunk, place, tokens, count, span
        )
        mixed = None
        for w in range(span):
            at = ((place - w) % count) * tokens
            part = jnp.dot(probs[w].astype(BF), vb_ref[at : at + tokens, :], preferred_element_type=F32)
            mixed = part if mixed is None else mixed + part
        o_ref[rows, :] = mixed.astype(BF)


def attend_back_kernel(
    tokens, count, span, me_ref, *refs
):
    grads_in = refs[:count]
    (q_ref, k_ref, v_ref, qp_ref, kp_ref, f_ref, qg_ref, kg_ref, cos_ref, sin_ref, segc_ref, segr_ref,
     dq_ref, dk_ref, dv_ref, inner_ref, gain_ref, dk_sum, dv_sum) = refs[count:]
    scale = HD**-0.5
    dk_sum[...] = jnp.zeros_like(dk_sum)
    dv_sum[...] = jnp.zeros_like(dv_sum)
    for place in range(count):
        rows = slice(place * tokens, (place + 1) * tokens)
        chunk = (me_ref[0] + place) % count
        q = q_ref[rows, :]
        grad = grads_in[place][...]
        probs = softmax_window(
            q, k_ref, segc_ref[rows, :], segr_ref, chunk, place, tokens, count, span
        )
        grads = []
        inner = None
        for w in range(span):
            at = ((place - w) % count) * tokens
            part = nt_dot(grad, v_ref[at : at + tokens, :])
            grads.append(part)
            inner = probs[w] * part if inner is None else inner + probs[w] * part
            dv_sum[at : at + tokens, :] += lax.dot_general(
                probs[w].astype(BF), grad, (((0,), (0,)), ((), ())), preferred_element_type=F32
            )
        inner = jnp.sum(inner, axis=-1, keepdims=True)
        dq = None
        for w in range(span):
            at = ((place - w) % count) * tokens
            ds = (probs[w] * (grads[w] - inner)).astype(BF)
            part = jnp.dot(ds, k_ref[at : at + tokens, :], preferred_element_type=F32)
            dq = part if dq is None else dq + part
            dk_sum[at : at + tokens, :] += lax.dot_general(
                ds, q, (((0,), (0,)), ((), ())), preferred_element_type=F32
            )
        dq_ref[rows, :] = dq
    first = pl.program_id(0) == 0
    sums = []
    sides = ((dq_ref, dq_ref, qp_ref, qg_ref), (dk_sum, dk_ref, kp_ref, kg_ref))
    for j, (raw_ref, out_ref, proj_ref, g_ref) in enumerate(sides):
        raw = (raw_ref[...] * scale).astype(BF).astype(F32)
        back = turn(raw, cos_ref[...], -sin_ref[...])
        normed = proj_ref[...] * f_ref[:, j : j + 1]
        gain_ref[j] = jnp.broadcast_to(jnp.sum(back * normed, axis=0, keepdims=True), (8, HD))
        back = back * g_ref[...]
        out_ref[...] = back
        sums.append(feature_sums(back * normed))
    sums = two_rows(*sums)
    for place in range(count):
        part = sums[:, place * tokens : (place + 1) * tokens]
        inner_ref[place] = jnp.where(first, part, inner_ref[place] + part)
    dv_ref[...] = dv_sum[...].astype(BF)


def attend_specs(length, heads):
    head = lambda j: pl.BlockSpec((length, HD), lambda h, me: (0, j * heads + h))
    whole = lambda *shape: pl.BlockSpec(shape, lambda h, me: (0, 0))
    gain = pl.BlockSpec((1, HD), lambda h, me: (0, h))
    return head, whole, gain


def attend(me, qkv, factors, q_gain, k_gain, tables, seg, count):
    length = qkv.shape[0]
    part = qkv.shape[1] // 3
    heads = part // HD
    tokens = length // count
    span = min(count, (length // 2 - 1 + tokens - 1) // tokens + 1)
    head, whole, gain = attend_specs(length, heads)
    low = jax.ShapeDtypeStruct((length, part), BF)
    return pl.pallas_call(
        functools.partial(attend_kernel, tokens, count, span),
        grid_spec=pltpu.PrefetchScalarGridSpec(
            num_scalar_prefetch=1,
            grid=(heads,),
            in_specs=[head(0), head(1), head(2), whole(length, 2), gain, gain]
            + [whole(length, HD)] * 2
            + [whole(length, 1), whole(1, length)],
            out_specs=[head(0)] * 4,
        ),
        out_shape=[low] * 4,
        compiler_params=params(),
        cost_estimate=cost(0, 0),
        name="attend",
    )(me, qkv, qkv, qkv, factors, q_gain[None], k_gain[None], *tables, seg[:, None], seg[None])


def attend_back(me, pieces, query, key, value, qkv, factors, q_gain, k_gain, tables, seg, count):
    length, part = query.shape
    heads = part // HD
    tokens = length // count
    span = min(count, (length // 2 - 1 + tokens - 1) // tokens + 1)
    head, whole, gain = attend_specs(length, heads)
    return pl.pallas_call(
        functools.partial(attend_back_kernel, tokens, count, span),
        grid_spec=pltpu.PrefetchScalarGridSpec(
            num_scalar_prefetch=1,
            grid=(heads,),
            in_specs=[pl.BlockSpec((tokens, HD), lambda h, me: (0, h))] * count
            + [head(0)] * 3
            + [head(0), head(1), whole(length, 2), gain, gain]
            + [whole(length, HD)] * 2
            + [whole(length, 1), whole(1, length)],
            out_specs=[head(0)] * 3
            + [
                pl.BlockSpec((count, 8, tokens), lambda h, me: (0, 0, 0)),
                pl.BlockSpec((2, 8, HD), lambda h, me: (0, 0, h)),
            ],
            scratch_shapes=[pltpu.VMEM((length, HD), F32)] * 2,
        ),
        out_shape=[jax.ShapeDtypeStruct((length, part), t) for t in (F32, F32, BF)]
        + [jax.ShapeDtypeStruct(m, F32) for m in ((count, 8, tokens), (2, 8, part))],
        compiler_params=params(),
        cost_estimate=cost(0, 0),
        name="attend_back",
    )(me, *pieces, query, key, value, qkv, qkv, factors, q_gain[None], k_gain[None], *tables,
      seg[:, None], seg[None])


def residual_back_kernel(
    me_ref, own_ref, a_ref, b_ref, c_ref, cot_ref, attn_ref, gain_ref, w_ref, res_ref, d_ref, sum_ref, *outs
):
    step = pl.program_id(0)

    @pl.when(step == 0)
    def _():
        grad = cot_ref[...].astype(F32) + own_ref[...]
        for ref in (a_ref, b_ref, c_ref):
            grad = grad + ref[...].astype(F32)
        res_ref[...] = grad
        attn = attn_ref[...]
        factor = inv_rms(attn)
        normed = attn * factor
        sums = jnp.sum(grad * normed, axis=0, keepdims=True)
        sum_ref[...] = jnp.broadcast_to(sums, sum_ref.shape)
        d_ref[...] = rms_back(normed, factor, gain_ref[...], grad).astype(BF)

    piece = nt_dot(d_ref[...], w_ref[...]).astype(BF)
    for p, out in enumerate(outs):

        @pl.when(step == p)
        def _(out=out):
            out[...] = piece


def residual_back(me, own, got, cot, attn_out, gain, w_first, count):
    tokens, width = own.shape
    part = width // count
    piece = pl.BlockSpec((tokens, part), lambda p, me: (0, 0))
    full = once((tokens, width), lambda p, me: (0, 0))
    whole = lambda rows: pl.BlockSpec((rows, width), lambda p, me: (0, 0))
    return pl.pallas_call(
        residual_back_kernel,
        grid_spec=pltpu.PrefetchScalarGridSpec(
            num_scalar_prefetch=1,
            grid=(count,),
            in_specs=[full] * 6
            + [whole(1), pl.BlockSpec((part, width), lambda p, me: ((me[0] + p) % count, 0))],
            out_specs=[whole(tokens), whole(tokens), whole(8)] + [piece] * count,
        ),
        out_shape=[
            jax.ShapeDtypeStruct((tokens, width), F32),
            jax.ShapeDtypeStruct((tokens, width), BF),
            jax.ShapeDtypeStruct((8, width), F32),
        ]
        + [jax.ShapeDtypeStruct((tokens, part), BF)] * count,
        compiler_params=params(),
        cost_estimate=cost(LATE_COST, 0),
        name="residual_back",
    )(me, own, *got, cot, attn_out, gain[None], w_first)


def input_back_kernel(
    part, me_ref, q_ref, k_ref, v_ref, qp_ref, kp_ref, in_ref, f_ref, w_ref, d_ref, ends_ref, *outs
):
    for j, (grad, proj) in enumerate(((q_ref, qp_ref), (k_ref, kp_ref))):
        factor = f_ref[:, j : j + 1]
        normed = proj[...] * factor
        low = ((grad[...] - normed * in_ref[:, j : j + 1]) * factor).astype(BF)
        d_ref[:, j * part : (j + 1) * part] = low
    d_ref[:, 2 * part :] = v_ref[...]
    total = nt_dot(d_ref[...], w_ref[...])
    step = pl.program_id(0)
    for j, out in enumerate(outs):

        @pl.when(step == j)
        def _(out=out):
            out[...] = total.astype(out.dtype)

    @pl.when((step == 0) | ((step == 1) & (me_ref[0] == 0)))
    def _():
        ends_ref[...] = total.astype(BF)


def input_back(me, d_query, d_key, d_v, qkv, inner, factors, w_qkv):
    length, part = d_query.shape
    width = w_qkv.shape[0]
    tokens = length // 4
    place = lambda t: jnp.where(t == 0, 1, jnp.where(t == 1, 3, jnp.where(t == 2, 2, 0)))
    rows = lambda columns, at=0: pl.BlockSpec((tokens, columns), lambda t, me: (place(t), at))
    kinds = (BF, BF, BF, BF, F32)
    return pl.pallas_call(
        functools.partial(input_back_kernel, part),
        grid_spec=pltpu.PrefetchScalarGridSpec(
            num_scalar_prefetch=1,
            grid=(4,),
            in_specs=[rows(part)] * 3
            + [rows(part), rows(part, 1), rows(2), rows(2)]
            + [once((width, 3 * part), lambda t, me: (0, 0))],
            out_specs=[rows(3 * part)]
            + [pl.BlockSpec((tokens, width), lambda t, me: (0, 0))] * len(kinds),
        ),
        out_shape=[jax.ShapeDtypeStruct((length, 3 * part), BF)]
        + [jax.ShapeDtypeStruct((tokens, width), kind) for kind in kinds],
        compiler_params=params(),
        cost_estimate=cost(0, 0),
        name="input_back",
    )(me, d_query, d_key, d_v, qkv, qkv, inner, factors, w_qkv)


def add_up_kernel(*refs):
    total = refs[0][...]
    for ref in refs[1:-1]:
        total = total + ref[...].astype(F32)
    refs[-1][...] = total.astype(BF)


def add_up(parts):
    tokens, width = parts[0].shape
    tile = tokens // 4
    block = pl.BlockSpec((tile, width), lambda i: (i, 0))
    return pl.pallas_call(
        add_up_kernel,
        grid=(4,),
        in_specs=[block] * len(parts),
        out_specs=block,
        out_shape=jax.ShapeDtypeStruct((tokens, width), BF),
        compiler_params=params(),
        cost_estimate=cost(LATE_COST, 0),
        name="add_up",
    )(*parts)


def tn_dot(left, right):
    return lax.dot_general(left, right, (((0,), (0,)), ((), ())), preferred_element_type=F32)


def weight_grad_kernel(lefts, right_ref, out_ref):
    total, at = None, 0
    for left in lefts:
        rows = left.shape[0]
        product = tn_dot(left[...], right_ref[at : at + rows, :])
        total = product if total is None else total + product
        at += rows
    out_ref[...] = total.astype(BF)


def weight_grad(lefts, right):
    width = lefts[0].shape[1]
    length, columns = right.shape
    tile, wide = 256, min(columns, 2048)
    return pl.pallas_call(
        lambda *refs: weight_grad_kernel(refs[:-2], *refs[-2:]),
        grid=(columns // wide, width // tile),
        in_specs=[pl.BlockSpec((left.shape[0], tile), lambda j, i: (0, i)) for left in lefts]
        + [pl.BlockSpec((length, wide), lambda j, i: (0, j))],
        out_specs=pl.BlockSpec((tile, wide), lambda j, i: (i, j)),
        out_shape=jax.ShapeDtypeStruct((width, columns), BF),
        compiler_params=params(),
        cost_estimate=cost(0, 0),
        name="weight_grad",
    )(*lefts, right)


def attn_grad_kernel(count, me_ref, x_ref, d_ref, *refs):
    pieces, parts, out_ref = refs[:count], refs[count : 2 * count], refs[-1]
    columns = d_ref.shape[1]
    out_ref[:, :columns] = tn_dot(x_ref[...], d_ref[...]).astype(BF)
    source = (pl.program_id(0) // (pl.num_programs(0) // count) + count - me_ref[0]) % count
    for p, piece in enumerate(pieces):

        @pl.when(source == p)
        def _(p=p, piece=piece):
            total, tokens = None, parts[0].shape[0]
            for q in range(count):
                rows = slice(q * tokens, (q + 1) * tokens)
                product = tn_dot(piece[rows, :], parts[(q + p) % count][...])
                total = product if total is None else total + product
            out_ref[:, columns:] = total.astype(BF)


def attn_grad(me, x_all, d_qkv, pieces, d_parts):
    count = len(pieces)
    length, width = x_all.shape
    columns, part = d_qkv.shape[1], d_parts[0].shape[1]
    tile = min(256, part)
    per_part = part // tile
    return pl.pallas_call(
        functools.partial(attn_grad_kernel, count),
        grid_spec=pltpu.PrefetchScalarGridSpec(
            num_scalar_prefetch=1,
            grid=(width // tile,),
            in_specs=[
                pl.BlockSpec((length, tile), lambda i, me: (0, i)),
                once((length, columns), lambda i, me: (0, 0)),
            ]
            + [pl.BlockSpec((length, tile), lambda i, me: (0, i % per_part))] * count
            + [once((length // count, part), lambda i, me: (0, 0))] * count,
            out_specs=pl.BlockSpec((tile, columns + part), lambda i, me: (i, 0)),
        ),
        out_shape=jax.ShapeDtypeStruct((width, columns + part), BF),
        compiler_params=params(),
        cost_estimate=cost(SIDE_COST, 0),
        name="attn_grad",
    )(me, x_all, d_qkv, *pieces, *d_parts)


def cost(flops, moved, exps=0):
    return pl.CostEstimate(flops=flops, bytes_accessed=moved, transcendentals=exps)


def params():
    return pltpu.CompilerParams(vmem_limit_bytes=56 << 20)


def once(shape, index):
    return pl.BlockSpec(shape, index, pipeline_mode=pl.Buffered(1))


def nt_dot(left, right):
    return lax.dot_general(left, right, (((1,), (1,)), ((), ())), preferred_element_type=F32)


def feature_sums(values):
    ones = jnp.ones((8, values.shape[1]), BF)
    total = None
    for _ in range(3):
        term = values.astype(BF)
        values = values - term.astype(F32)
        total = nt_dot(ones, term) if total is None else total + nt_dot(ones, term)
    return total


def two_rows(first, second):
    return jnp.where(lax.broadcasted_iota(jnp.int32, first.shape, 0) == 0, first, second)


def qkv_kernel(part, saved, me_ref, *refs):
    chunks, w_ref, (x_ref, qkv_ref, sq_ref) = refs[: -4 - saved], refs[-4 - saved], refs[-3:]
    step, me = pl.program_id(0), me_ref[0]
    at_end = (step == 0) & (me == 3) | (step == 1) & (me == 0) if len(chunks) == 3 else step < 0
    for q in range(2):

        @pl.when((step == q) & jnp.logical_not(at_end))
        def _(q=q):
            x_ref[...] = chunks[q][...]

    @pl.when(at_end)
    def _():
        x_ref[...] = chunks[-1][...]

    qkv = jnp.dot(x_ref[...], w_ref[...], preferred_element_type=F32)
    qkv_ref[...] = qkv
    q, k = (qkv[:, j * part : (j + 1) * part] for j in range(2))
    sq_ref[0] = two_rows(feature_sums(q * q), feature_sums(k * k))


def qkv_project(me, first, chunks, w_qkv, saved=()):
    tokens, width = chunks[0].shape
    columns = w_qkv.shape[1]
    length = 4 * tokens
    place = lambda q: 2 * q + first
    return pl.pallas_call(
        functools.partial(qkv_kernel, columns // 3, len(saved)),
        grid_spec=pltpu.PrefetchScalarGridSpec(
            num_scalar_prefetch=1,
            grid=(2,),
            in_specs=[once((tokens, width), lambda q, me: (0, 0))] * len(chunks)
            + [once((width, columns), lambda q, me: (0, 0))]
            + [pl.BlockSpec(memory_space=pl.ANY)] * len(saved),
            out_specs=[
                pl.BlockSpec((tokens, width), lambda q, me: (place(q), 0)),
                pl.BlockSpec((tokens, columns), lambda q, me: (place(q), 0)),
                pl.BlockSpec((1, 8, tokens), lambda q, me: (place(q), 0, 0)),
            ],
        ),
        out_shape=[
            jax.ShapeDtypeStruct((length, width), BF),
            jax.ShapeDtypeStruct((length, columns), F32),
            jax.ShapeDtypeStruct((4, 8, tokens), F32),
        ],
        input_output_aliases={2 + len(chunks) + j: j for j in range(len(saved))},
        compiler_params=params(),
        cost_estimate=cost(0, 0),
        name="qkv_project",
    )(me, *chunks, w_qkv, *saved)


FF_TILE = 512
LATE_COST = 10**12
SIDE_COST = 10**11


def ff_finish(step, product, acc, me_ref, outs):
    @pl.when(step == 0)
    def _():
        acc[...] = product

    @pl.when(step > 0)
    def _():
        acc[...] += product

    @pl.when(step == pl.num_programs(0) - 1)
    def _():
        tokens = outs[0].shape[0]
        for j, out in enumerate(outs[:2]):
            out[...] = acc[j * tokens : (j + 1) * tokens].astype(out.dtype)
        if len(outs) == 3:
            at = pl.multiple_of(jnp.where(me_ref[0] == 0, tokens, 0), tokens)
            outs[2][...] = acc[pl.ds(at, tokens), :].astype(BF)


def ff_kernel(saved, me_ref, h_ref, wg_ref, wu_ref, wd_ref, *refs):
    gate_ref, up_ref, hid_ref = refs[saved : saved + 3]
    h = h_ref[...]
    gate = jnp.dot(h, wg_ref[...], preferred_element_type=F32)
    up = jnp.dot(h, wu_ref[...], preferred_element_type=F32)
    hidden = (gate * (1.0 / (1.0 + jnp.exp(-gate))) * up).astype(BF)
    gate_ref[...] = gate
    up_ref[...] = up
    hid_ref[...] = hidden
    product = nt_dot(hidden, wd_ref[...])
    ff_finish(pl.program_id(0), product, refs[-1], me_ref, refs[saved + 3 : -1])


def ff_back_kernel(saved, groups, me_ref, *refs):
    d_refs, (wg_ref, wu_ref, wd_ref, gate_ref, up_ref) = refs[:groups], refs[groups : groups + 5]
    refs = refs[groups + 5 :]
    dgu_ref = refs[saved]
    tile = wg_ref.shape[1]
    d_ff = d_refs[0][...] if groups == 1 else jnp.concatenate([d[...] for d in d_refs], axis=0)
    d_hidden = jnp.dot(d_ff, wd_ref[...], preferred_element_type=F32)
    gate = gate_ref[...]
    sig = 1.0 / (1.0 + jnp.exp(-gate))
    d_gate = (d_hidden * up_ref[...] * sig * (1.0 + gate * (1.0 - sig))).astype(BF)
    d_up = (d_hidden * gate * sig).astype(BF)
    dgu_ref[:, :tile] = d_gate
    dgu_ref[:, tile:] = d_up
    product = nt_dot(d_gate, wg_ref[...]) + nt_dot(d_up, wu_ref[...])
    ff_finish(pl.program_id(0), product, refs[-1], me_ref, refs[saved + 1 : -1])


def ff_specs(width, tile, gate_at):
    rest = pl.BlockSpec((width, tile), lambda t: (0, t))
    return [pl.BlockSpec((width, tile), lambda t: (0, gate_at // tile + t)), rest, rest]


def ff_forward(me, residual_all, w_first, w_up, w_down, place, kinds, saved=()):
    length, width = residual_all.shape
    tokens = length // 4
    group = min(len(kinds), 2)
    rows = group * tokens
    ff_part = w_up.shape[1]
    tile = min(FF_TILE, ff_part)
    block = pl.BlockSpec((rows, tile), lambda t: (place // group, t))
    whole = pl.BlockSpec((tokens, width), lambda t: (0, 0))
    shape = lambda kind: jax.ShapeDtypeStruct((length, ff_part), kind)
    return pl.pallas_call(
        functools.partial(ff_kernel, len(saved)),
        grid=(ff_part // tile,),
        in_specs=[pl.BlockSpec(memory_space=pltpu.SMEM)]
        + [once((rows, width), lambda t: (place // group, 0))]
        + ff_specs(width, tile, w_first.shape[1] - ff_part)
        + [pl.BlockSpec(memory_space=pl.ANY)] * len(saved),
        out_specs=[block] * 3 + [whole] * len(kinds),
        out_shape=[shape(F32), shape(F32), shape(BF)]
        + [jax.ShapeDtypeStruct((tokens, width), kind) for kind in kinds],
        scratch_shapes=[pltpu.VMEM((rows, width), F32)],
        input_output_aliases={5 + j: j for j in range(len(saved))},
        compiler_params=params(),
        cost_estimate=cost(0, 0),
        name="ff_forward",
    )(me, residual_all, w_first, w_up, w_down, *saved)


def ff_backward(me, d_ffs, w_first, w_up, w_down, gate, up, place, kinds, saved=()):
    tokens, width = d_ffs[0].shape
    group = len(d_ffs)
    rows = group * tokens
    length = gate.shape[0]
    ff_part = w_up.shape[1]
    tile = min(FF_TILE, ff_part)
    block = pl.BlockSpec((rows, tile), lambda t: (place // group, t))
    whole = pl.BlockSpec((tokens, width), lambda t: (0, 0))
    return pl.pallas_call(
        functools.partial(ff_back_kernel, len(saved), group),
        grid=(ff_part // tile,),
        in_specs=[pl.BlockSpec(memory_space=pltpu.SMEM)]
        + [once((tokens, width), lambda t: (0, 0))] * group
        + ff_specs(width, tile, w_first.shape[1] - ff_part)
        + [block, block]
        + [pl.BlockSpec(memory_space=pl.ANY)] * len(saved),
        out_specs=[pl.BlockSpec((rows, 2 * tile), lambda t: (place // group, t))]
        + [whole] * len(kinds),
        out_shape=[jax.ShapeDtypeStruct((length, 2 * ff_part), BF)]
        + [jax.ShapeDtypeStruct((tokens, width), kind) for kind in kinds],
        scratch_shapes=[pltpu.VMEM((rows, width), F32)],
        input_output_aliases={6 + group + j: j for j in range(len(saved))},
        compiler_params=params(),
        cost_estimate=cost(SIDE_COST, 0),
        name="ff_backward",
    )(me, *d_ffs, w_first, w_up, w_down, gate, up, *saved)


def out_kernel(count, part, saved, me_ref, *refs):
    pieces, (w_ref, x_ref, g_ref), outs = refs[:count], refs[count : count + 3], refs[count + 3 + saved :]
    total = None
    for p, piece in enumerate(pieces):
        rows = pl.ds(pl.multiple_of((me_ref[0] + p) % count * part, part), part)
        product = jnp.dot(piece[...], w_ref[rows, :], preferred_element_type=F32)
        total = product if total is None else total + product
    normed = total * inv_rms(total)
    outs[0][...] = (x_ref[...].astype(F32) + normed * g_ref[...]).astype(BF)
    if saved:

        @pl.when(pl.program_id(0) == 1)
        def _():
            outs[1][...] = total


def ff_place(q):
    return jnp.where(q == 0, 3, jnp.where(q == 3, 1, jnp.where(q == 2, 2, 0)))


def out_project(me, pieces, w_out, x_all, gain, count, saved=()):
    length, width = x_all.shape
    tokens = length // count
    part = pieces[0].shape[1]
    place = lambda t: 2 - 2 * t if saved else 2 * t + 1
    rolled = lambda p: pl.BlockSpec((tokens, part), lambda t, me: ((place(t) + count - p) % count, 0))
    chunk = pl.BlockSpec((tokens, width), lambda t, me: (place(t), 0))
    moved = pl.BlockSpec((tokens, width), lambda t, me: (ff_place(place(t)), 0))
    own = pl.BlockSpec((tokens, width), lambda t, me: (0, 0))
    return pl.pallas_call(
        functools.partial(out_kernel, count, part, len(saved)),
        grid_spec=pltpu.PrefetchScalarGridSpec(
            num_scalar_prefetch=1,
            grid=(2,),
            in_specs=[rolled(p) for p in range(count)]
            + [once((width, width), lambda t, me: (0, 0))]
            + [chunk, pl.BlockSpec((1, width), lambda t, me: (0, 0))]
            + [pl.BlockSpec(memory_space=pl.ANY)] * len(saved),
            out_specs=[moved] + [own] * len(saved),
        ),
        out_shape=[jax.ShapeDtypeStruct((length, width), BF)]
        + [jax.ShapeDtypeStruct((tokens, width), F32)] * len(saved),
        input_output_aliases={4 + count + j: j for j in range(len(saved))},
        compiler_params=params(),
        cost_estimate=cost(0, 0),
        name="out_project",
    )(me, *pieces, w_out, x_all, gain[None], *saved)


def columns_to_parts(values, me, count):
    part = values.shape[1] // count
    columns = lambda p: lax.dynamic_slice_in_dim(values, (me + p) % count * part, part, 1)
    got = [columns(0)] + [
        lax.ppermute(columns(p), "seq", [(i, (i + p) % count) for i in range(count)])
        for p in range(1, count)
    ]
    return [got[(count - q) % count] for q in range(count)]


def build(dp_count, seq_count):
    assert seq_count == 4

    def shards(
        layer_input,
        segments,
        w_query,
        w_key,
        w_value,
        w_output,
        w_gate,
        w_up,
        w_down,
        query_gain,
        key_gain,
        attn_gain,
        ff_gain,
        cotangent,
    ):
        n = seq_count
        tokens, width = layer_input.shape[1:]
        shard_rows = w_query.shape[0]
        part = width // n
        ff_part = w_gate.shape[1] // n
        length = n * tokens
        devices = dp_count * n
        me = lax.axis_index("seq")
        me_ref = me[None].astype(jnp.int32)
        cot = cotangent[0]
        by_part = lambda w: w.reshape(shard_rows, n, -1).transpose(1, 0, 2)
        rows_of = lambda blocks: blocks.reshape(n * shard_rows, -1)

        fence = lax.optimization_barrier
        qkv_blocks = jnp.concatenate([by_part(w) for w in (w_query, w_key, w_value)], axis=2)
        qkv_blocks = swap_blocks(qkv_blocks)
        w_qkv = gather_dp(rows_of(qkv_blocks))
        natural = jnp.arange(length, dtype=jnp.int32)
        positions = (natural + me * tokens) % length
        seg_row = segments[0]
        seg = lax.dynamic_slice_in_dim(
            jnp.concatenate([seg_row, seg_row]), me * tokens, length, 0
        )
        tables = rope_tables(positions.astype(F32))
        own_gain = lambda g: lax.dynamic_slice_in_dim(g, me * part, part, 0)
        q_gain = own_gain(query_gain)
        k_gain = own_gain(key_gain)

        up_columns, down_columns = (part_columns(w, me, n) for w in (w_up, w_down.T))
        ready = (seg, tables, q_gain, k_gain, up_columns, down_columns)
        qkv_blocks, w_output, w_gate = fence((qkv_blocks, w_output, w_gate))
        out_blocks = gather_cyclic(w_output, n)
        gate_blocks = send_blocks(part_columns(w_gate, me, n))
        out_blocks, gate_blocks, x_own, ready = fence(
            (out_blocks, gate_blocks, layer_input[0], ready)
        )
        seg, tables, q_gain, k_gain, up_columns, down_columns = ready
        out_blocks = out_blocks[:1] + out_blocks[:0:-1]
        w_first = place_blocks(out_blocks, me, 0, width + ff_part)
        w_first = gather_dp(place_blocks(gate_blocks, me, width, width + ff_part, w_first))
        x_own, x_after, x_far, x_before, x_ends = gather_raw(x_own, n)
        saved = qkv_project(me_ref, 0, [x_own, x_far], w_qkv)
        x_sides, saved, up_columns = fence(([x_after, x_before, x_ends], saved, up_columns))
        up_blocks = send_blocks(up_columns)
        x_all, qkv, squares = qkv_project(me_ref, 1, x_sides, w_qkv, saved)
        squares, up_blocks = fence((squares, up_blocks))
        w_up_all = gather_dp(place_blocks(up_blocks, me, 0, ff_part))

        squares = sum_stats(squares, n)
        squares, down_columns = fence((squares, down_columns))
        down_blocks = send_blocks(down_columns)
        factors = lax.rsqrt(stat_columns(squares) / width + EPSILON)
        mixed, q_low, k_low, v_low = attend(me_ref, qkv, factors, q_gain, k_gain, tables, seg, n)

        mixed, down_blocks = fence((mixed, down_blocks))
        w_down_all = gather_dp(place_blocks(down_blocks, me, 0, ff_part))
        pieces = gather_cyclic(mixed, n)
        operands = (w_first, x_all, attn_gain, n)
        saved_residual = out_project(me_ref, pieces, *operands)
        *saved, after, before, ends = ff_forward(
            me_ref, saved_residual[0], w_first, w_up_all, w_down_all, 0, (BF, BF, BF)
        )
        sent = scatter_start(ends, after, before, n)
        saved_residual, after = fence((saved_residual, after))
        residual_all, attn_out = out_project(me_ref, pieces, *operands, saved_residual)
        attn_factor = inv_rms(attn_out)
        attn_normed = attn_out * attn_factor
        residual = x_own.astype(F32) + attn_normed * attn_gain
        *saved, far = ff_forward(
            me_ref, residual_all, w_first, w_up_all, w_down_all, 2, (F32,), saved
        )
        far, sent[0], residual_late = fence((far, sent[0], residual_all))
        sent[0] = scatter_far(far, sent[0], n)
        gate, up, hidden, own = ff_forward(
            me_ref, residual_late, w_first, w_up_all, w_down_all, 3, (F32,), saved
        )
        ff_out = scatter_end(own, sent)
        ff_factor = inv_rms(ff_out)
        ff_normed = ff_out * ff_factor
        activation = (residual + ff_normed * ff_gain).astype(BF)
        grad_ff_gain = jnp.sum(cot.astype(F32) * ff_normed, axis=0)
        d_ff = rms_back(ff_normed, ff_factor, ff_gain, cot.astype(F32)).astype(BF)
        d_ffs = gather_cyclic(d_ff, n)
        d_both, own = ff_backward(me_ref, d_ffs[:1], w_first, w_up_all, w_down_all, gate, up, 3, (F32,))
        d_ffs, d_both = fence((d_ffs, d_both))
        d_both, after, before, ends = ff_backward(
            me_ref, d_ffs[1::2], w_first, w_up_all, w_down_all, gate, up, 0, (BF, BF, BF), (d_both,)
        )
        sent = scatter_start(ends, after, before, n)
        d_both, far = ff_backward(
            me_ref, d_ffs[2:3], w_first, w_up_all, w_down_all, gate, up, 2, (F32,), (d_both,)
        )
        d_both, far, sent[0], d_ffs, hidden = fence((d_both, far, sent[0], d_ffs, hidden))
        sent[0] = scatter_far(far, sent[0], n)
        joined = lambda g: g.transpose(1, 0, 2).reshape(shard_rows, -1).astype(F32)
        down_grad = weight_grad([d_ffs[1], d_ffs[3], d_ffs[2], d_ffs[0]], hidden)
        down_rows = scatter_dp(down_grad)
        down_grad, sent = fence((down_grad, sent))
        d_res, d_attn, grad_attn_gain, *d_pieces = residual_back(
            me_ref, own, sent, cot, attn_out, attn_gain, w_first, n
        )
        d_mixed = [d_pieces[0]] + [None] * (n - 1)
        for p in range(1, n):
            d_mixed[n - p] = lax.ppermute(
                d_pieces[p], "seq", [(i, (i + p) % n) for i in range(n)]
            )
        residual_all, d_both, _ = fence((residual_all, d_both, d_pieces[0]))
        gate_up_grad = weight_grad([residual_all], d_both)
        d_mixed, d_attn, gate_up_grad = fence((d_mixed, d_attn, gate_up_grad))
        gate_up_rows = scatter_dp(gate_up_grad)
        d_attn_part = columns_to_parts(d_attn, me, n)
        d_query, d_key, d_v, inner, gain_sums = attend_back(
            me_ref, d_mixed, q_low, k_low, v_low, qkv, factors, q_gain, k_gain, tables, seg, n
        )
        inner, d_attn_part, down_back = fence(
            (inner, d_attn_part, row_blocks(down_rows, me, n))
        )
        inner = sum_stats(inner, n)
        inner, down_back = fence((inner, down_back))
        down_back = send_blocks(down_back)
        d_qkv, ends, after, before, far, own = input_back(
            me_ref, d_query, d_key, d_v, qkv, stat_columns(inner) / width, factors, w_qkv
        )
        d_qkv, ends, after, before, far, own, down_back = fence(
            (d_qkv, ends, after, before, far, own, down_back)
        )
        ends, *sent = scatter_start(ends, after, before, n)
        sent.append(lax.ppermute(far, "seq", [(0, 2), (3, 1)]))
        attn_grads = attn_grad(me_ref, x_all, d_qkv, pieces, d_attn_part)
        ends, attn_grads = fence((ends, attn_grads))
        attn_rows = scatter_dp(attn_grads)
        far = (far.astype(F32) + ends.astype(F32)).astype(BF)
        sent.append(lax.ppermute(far, "seq", [(1, 3), (2, 0)]))
        gate_up_back = row_blocks(gate_up_rows, me, n)
        sent, gate_up_back = fence((sent, gate_up_back))
        input_grad = add_up([d_res, own] + sent)
        spread = lambda g: lax.dynamic_update_slice(jnp.zeros(width, F32), g, (me * part,))
        gains = jnp.stack(
            [spread(gain_sums[0, 0]), spread(gain_sums[1, 0]), grad_attn_gain[0], grad_ff_gain]
        )
        input_grad, gains = fence((input_grad, gains))
        gate_up_back = send_blocks(gate_up_back)
        gains = sum_everywhere(gains, dp_count, n)
        attn_rows, input_grad, gate_up_back, down_back, gains = fence(
            (attn_rows, input_grad, gate_up_back, down_back, gains)
        )
        attn_back = swap_blocks(attn_rows.reshape(n, shard_rows, -1))
        grad_gate, grad_up = join_columns(me_ref, gate_up_back, 2)
        grad_down = join_columns(me_ref, down_back, 1)[0].T
        attn_back, grad_gate, grad_up, grad_down = fence(
            (attn_back, grad_gate, grad_up, grad_down)
        )
        grad_query, grad_key, grad_value, grad_output = (
            joined(attn_back[:, :, j * part : (j + 1) * part]) for j in range(4)
        )

        share = width // devices
        gains = lax.dynamic_slice_in_dim(
            gains, (lax.axis_index("dp") * n + me) * share, share, 1
        )
        return (
            activation[None],
            input_grad[None],
            grad_query,
            grad_key,
            grad_value,
            grad_output,
            grad_gate,
            grad_up,
            grad_down,
            gains[0],
            gains[1],
            gains[2],
            gains[3],
        )

    return shards


def solution(mesh):
    both = P(("dp", "seq"), None)
    tokens = P("dp", "seq", None)
    columns = P(None, ("dp", "seq"))
    gain = P(("dp", "seq"))
    return jax.shard_map(
        build(mesh.shape["dp"], mesh.shape["seq"]),
        mesh=mesh,
        in_specs=(tokens, P("dp", None)) + (both,) * 6 + (columns,) + (P(),) * 4 + (tokens,),
        out_specs=(tokens, tokens) + (both,) * 6 + (columns,) + (gain,) * 4,
        check_vma=False,
    )
```

```python
import functools

import jax
import jax.numpy as jnp
from jax import lax
from jax.experimental import pallas as pl
from jax.experimental.pallas import tpu as pltpu
from jax.sharding import PartitionSpec as P

HD = 128
EPSILON = 1e-06
ROPE_BASE = 500000.0
MASKED = -1e30
LOG2E = 1.4426950408889634
BF = jnp.bfloat16
F32 = jnp.float32


def inv_rms(values):
    return lax.rsqrt(jnp.mean(values * values, axis=-1, keepdims=True) + EPSILON)


def rms_back(normed, factor, gain, grad):
    scaled = grad * gain
    inner = jnp.mean(scaled * normed, axis=-1, keepdims=True)
    return (scaled - normed * inner) * factor


def rope_tables(positions):
    half_dim = HD // 2
    frequency = jnp.power(F32(ROPE_BASE), -jnp.arange(half_dim, dtype=F32) * (2.0 / HD))
    angles = positions[:, None] * frequency[None, :]
    cosine, sine = jnp.cos(angles), jnp.sin(angles)
    return (jnp.concatenate([cosine, cosine], axis=-1), jnp.concatenate([-sine, sine], axis=-1))


def shift(values, count, step):
    return lax.ppermute(values, "seq", [((i + step) % count, i) for i in range(count)])


def gather_raw(values, count):
    far = lax.ppermute(values, "seq", [(i ^ 2, i) for i in range(count)])
    after = lax.ppermute(values, "seq", [(i + 1, i) for i in range(count - 1)])
    before = lax.ppermute(values, "seq", [(i, i + 1) for i in range(count - 1)])
    ends = lax.ppermute(far, "seq", [(2, 3), (1, 0)])
    return [values, after, far, before, ends]


def gather_cyclic(values, count):
    own, after, far, before, ends = gather_raw(values, count)
    me = lax.axis_index("seq")
    after = jnp.where(me == count - 1, ends, after)
    return [own, after, far, jnp.where(me == 0, ends, before)]


def scatter_start(ends, after, before, count):
    ends = lax.ppermute(ends, "seq", [(0, 1), (count - 1, count - 2)])
    step = [(i, i + 1) for i in range(count - 1)]
    after = lax.ppermute(after, "seq", step)
    before = lax.ppermute(before, "seq", [(j, i) for i, j in step])
    return [ends, after, before]


def scatter_far(far, ends):
    far = (far.astype(F32) + ends.astype(F32)).astype(BF)
    return lax.ppermute(far, "seq", [(1, 3), (2, 0)])


def scatter_end(own, got):
    for part in got:
        own = own + part.astype(F32)
    return own


def sum_stats(stats, count):
    total = stats
    for p in range(1, count):
        total = total + jnp.roll(shift(stats, count, p), p, axis=0)
    return total


def stat_columns(stats):
    return stats[:, :2].transpose(0, 2, 1).reshape(-1, 2)


def sum_everywhere(values, dp_count, seq_count):
    for name, count in (("dp", dp_count), ("seq", seq_count)):
        if count & (count - 1):
            values = lax.psum(values, name)
            continue
        bit = 1
        while bit < count:
            values = values + lax.ppermute(values, name, [(i, i ^ bit) for i in range(count)])
            bit *= 2
    return values


def swap_blocks(values):
    return lax.all_to_all(values, "seq", split_axis=0, concat_axis=0, tiled=True)


def part_columns(values, me, count):
    part = values.shape[1] // count
    return [
        lax.dynamic_slice_in_dim(values, (me + p) % count * part, part, 1) for p in range(count)
    ]


def place_blocks(blocks, me, first, width, total=None):
    count = len(blocks)
    rows = blocks[0].shape[0]
    if total is None:
        total = jnp.zeros((count * rows, width), blocks[0].dtype)
    for p, block in enumerate(blocks):
        total = lax.dynamic_update_slice(total, block, ((me - p) % count * rows, first))
    return total


def row_blocks(values, me, count):
    size = values.shape[0] // count
    return [
        lax.dynamic_slice_in_dim(values, (me + p) % count * size, size, 0) for p in range(count)
    ]


def send_blocks(blocks):
    count = len(blocks)
    return blocks[:1] + [
        lax.ppermute(blocks[p], "seq", [(i, (i + p) % count) for i in range(count)])
        for p in range(1, count)
    ]


def join_kernel(sides, me_ref, *refs):
    blocks, outs = refs[:-sides], refs[-sides:]
    for p, block in enumerate(blocks):

        @pl.when(pl.program_id(0) == p)
        def _(block=block):
            for j, out in enumerate(outs):
                tile = min(FF_TILE, out.shape[1])
                for at in range(0, out.shape[1], tile):
                    first = at * sides + j * tile
                    out[:, at : at + tile] = block[:, first : first + tile].astype(F32)


def join_columns(me, blocks, sides):
    count = len(blocks)
    rows, columns = blocks[0].shape
    part = columns // sides
    out = pl.BlockSpec((rows, part), lambda p, me: (0, (me[0] + count - p) % count))
    return pl.pallas_call(
        functools.partial(join_kernel, sides),
        grid_spec=pltpu.PrefetchScalarGridSpec(
            num_scalar_prefetch=1,
            grid=(count,),
            in_specs=[once((rows, columns), lambda p, me: (0, 0))] * count,
            out_specs=[out] * sides,
        ),
        out_shape=[jax.ShapeDtypeStruct((rows, count * part), F32)] * sides,
        compiler_params=params(),
        cost_estimate=cost(0, 0),
        name="join_columns",
    )(me, *blocks)


def gather_dp(values):
    return lax.all_gather(values, "dp", axis=0, tiled=True)


def scatter_dp(values):
    return lax.psum_scatter(values, "dp", scatter_dimension=0, tiled=True)


def softmax_window(q, k_ref, seg_q, seg_row_ref, valid_from, place, tokens, count, span):
    parts = []
    for w in range(span):
        at = ((place - w) % count) * tokens
        scores = lax.dot_general(
            q, k_ref[at : at + tokens, :], (((1,), (1,)), ((), ())), preferred_element_type=F32
        )
        seg = seg_q if w == 0 else jnp.where(valid_from >= w, seg_q, -1)
        allowed = seg == seg_row_ref[:, at : at + tokens]
        if w == 0:
            rows = lax.broadcasted_iota(jnp.int32, (tokens, tokens), 0)
            cols = lax.broadcasted_iota(jnp.int32, (tokens, tokens), 1)
            allowed = allowed & (cols <= rows)
        parts.append(jnp.where(allowed, scores, MASKED))
    top = parts[0]
    for part in parts[1:]:
        top = jnp.maximum(top, part)
    top = jnp.max(top, axis=-1, keepdims=True)
    exps = [jnp.exp2((part - top) * (HD**-0.5 * LOG2E)) for part in parts]
    total = exps[0]
    for part in exps[1:]:
        total = total + part
    inverse = 1.0 / jnp.sum(total, axis=-1, keepdims=True)
    return [part * inverse for part in exps]


def turn(values, cosine, sine):
    return values * cosine + pltpu.roll(values, HD // 2, 1) * sine


def attend_kernel(
    tokens, count, span,
    me_ref, q_ref, k_ref, v_ref, f_ref, qg_ref, kg_ref, cos_ref, sin_ref, segc_ref, segr_ref,
    o_ref, qb_ref, kb_ref, vb_ref,
):
    cosine, sine = cos_ref[...], sin_ref[...]
    factors = f_ref[...]
    qb_ref[...] = turn(q_ref[...] * factors[:, 0:1] * qg_ref[...], cosine, sine).astype(BF)
    kb_ref[...] = turn(k_ref[...] * factors[:, 1:2] * kg_ref[...], cosine, sine).astype(BF)
    vb_ref[...] = v_ref[...].astype(BF)
    for place in range(count):
        rows = slice(place * tokens, (place + 1) * tokens)
        chunk = (me_ref[0] + place) % count
        probs = softmax_window(
            qb_ref[rows, :], kb_ref, segc_ref[rows, :], segr_ref, chunk, place, tokens, count, span
        )
        mixed = None
        for w in range(span):
            at = ((place - w) % count) * tokens
            part = jnp.dot(probs[w].astype(BF), vb_ref[at : at + tokens, :], preferred_element_type=F32)
            mixed = part if mixed is None else mixed + part
        o_ref[rows, :] = mixed.astype(BF)


def attend_back_kernel(
    tokens, count, span, me_ref, *refs
):
    grads_in = refs[:count]
    (q_ref, k_ref, v_ref, qp_ref, kp_ref, f_ref, qg_ref, kg_ref, cos_ref, sin_ref, segc_ref, segr_ref,
     dq_ref, dk_ref, dv_ref, inner_ref, gain_ref, dk_sum, dv_sum) = refs[count:]
    scale = HD**-0.5
    dk_sum[...] = jnp.zeros_like(dk_sum)
    dv_sum[...] = jnp.zeros_like(dv_sum)
    for place in range(count):
        rows = slice(place * tokens, (place + 1) * tokens)
        chunk = (me_ref[0] + place) % count
        q = q_ref[rows, :]
        grad = grads_in[place][...]
        probs = softmax_window(
            q, k_ref, segc_ref[rows, :], segr_ref, chunk, place, tokens, count, span
        )
        grads = []
        inner = None
        for w in range(span):
            at = ((place - w) % count) * tokens
            part = nt_dot(grad, v_ref[at : at + tokens, :])
            grads.append(part)
            inner = probs[w] * part if inner is None else inner + probs[w] * part
            dv_sum[at : at + tokens, :] += lax.dot_general(
                probs[w].astype(BF), grad, (((0,), (0,)), ((), ())), preferred_element_type=F32
            )
        inner = jnp.sum(inner, axis=-1, keepdims=True)
        dq = None
        for w in range(span):
            at = ((place - w) % count) * tokens
            ds = (probs[w] * (grads[w] - inner)).astype(BF)
            part = jnp.dot(ds, k_ref[at : at + tokens, :], preferred_element_type=F32)
            dq = part if dq is None else dq + part
            dk_sum[at : at + tokens, :] += lax.dot_general(
                ds, q, (((0,), (0,)), ((), ())), preferred_element_type=F32
            )
        dq_ref[rows, :] = dq
    first = pl.program_id(0) == 0
    sums = []
    sides = ((dq_ref, dq_ref, qp_ref, qg_ref), (dk_sum, dk_ref, kp_ref, kg_ref))
    for j, (raw_ref, out_ref, proj_ref, g_ref) in enumerate(sides):
        raw = (raw_ref[...] * scale).astype(BF).astype(F32)
        back = turn(raw, cos_ref[...], -sin_ref[...])
        normed = proj_ref[...] * f_ref[:, j : j + 1]
        gain_ref[j] = jnp.broadcast_to(jnp.sum(back * normed, axis=0, keepdims=True), (8, HD))
        back = back * g_ref[...]
        out_ref[...] = back
        sums.append(feature_sums(back * normed))
    sums = two_rows(*sums)
    for place in range(count):
        part = sums[:, place * tokens : (place + 1) * tokens]
        inner_ref[place] = jnp.where(first, part, inner_ref[place] + part)
    dv_ref[...] = dv_sum[...].astype(BF)


def attend_specs(length, heads):
    head = lambda j: pl.BlockSpec((length, HD), lambda h, me: (0, j * heads + h))
    whole = lambda *shape: pl.BlockSpec(shape, lambda h, me: (0, 0))
    gain = pl.BlockSpec((1, HD), lambda h, me: (0, h))
    return head, whole, gain


def attend(me, qkv, factors, q_gain, k_gain, tables, seg, count):
    length = qkv.shape[0]
    part = qkv.shape[1] // 3
    heads = part // HD
    tokens = length // count
    span = min(count, (length // 2 - 1 + tokens - 1) // tokens + 1)
    head, whole, gain = attend_specs(length, heads)
    low = jax.ShapeDtypeStruct((length, part), BF)
    return pl.pallas_call(
        functools.partial(attend_kernel, tokens, count, span),
        grid_spec=pltpu.PrefetchScalarGridSpec(
            num_scalar_prefetch=1,
            grid=(heads,),
            in_specs=[head(0), head(1), head(2), whole(length, 2), gain, gain]
            + [whole(length, HD)] * 2
            + [whole(length, 1), whole(1, length)],
            out_specs=[head(0)] * 4,
        ),
        out_shape=[low] * 4,
        compiler_params=params(),
        cost_estimate=cost(0, 0),
        name="attend",
    )(me, qkv, qkv, qkv, factors, q_gain[None], k_gain[None], *tables, seg[:, None], seg[None])


def attend_back(me, pieces, query, key, value, qkv, factors, q_gain, k_gain, tables, seg, count):
    length, part = query.shape
    heads = part // HD
    tokens = length // count
    span = min(count, (length // 2 - 1 + tokens - 1) // tokens + 1)
    head, whole, gain = attend_specs(length, heads)
    return pl.pallas_call(
        functools.partial(attend_back_kernel, tokens, count, span),
        grid_spec=pltpu.PrefetchScalarGridSpec(
            num_scalar_prefetch=1,
            grid=(heads,),
            in_specs=[pl.BlockSpec((tokens, HD), lambda h, me: (0, h))] * count
            + [head(0)] * 3
            + [head(0), head(1), whole(length, 2), gain, gain]
            + [whole(length, HD)] * 2
            + [whole(length, 1), whole(1, length)],
            out_specs=[head(0)] * 3
            + [
                pl.BlockSpec((count, 8, tokens), lambda h, me: (0, 0, 0)),
                pl.BlockSpec((2, 8, HD), lambda h, me: (0, 0, h)),
            ],
            scratch_shapes=[pltpu.VMEM((length, HD), F32)] * 2,
        ),
        out_shape=[jax.ShapeDtypeStruct((length, part), t) for t in (F32, F32, BF)]
        + [jax.ShapeDtypeStruct(m, F32) for m in ((count, 8, tokens), (2, 8, part))],
        compiler_params=params(),
        cost_estimate=cost(0, 0),
        name="attend_back",
    )(me, *pieces, query, key, value, qkv, qkv, factors, q_gain[None], k_gain[None], *tables,
      seg[:, None], seg[None])


def residual_back_kernel(
    me_ref, own_ref, a_ref, b_ref, c_ref, e_ref, cot_ref, attn_ref, gain_ref, w_ref, res_ref, d_ref, sum_ref, *outs
):
    step = pl.program_id(0)

    @pl.when(step == 0)
    def _():
        grad = cot_ref[...].astype(F32) + own_ref[...]
        for ref in (a_ref, b_ref, c_ref, e_ref):
            grad = grad + ref[...].astype(F32)
        res_ref[...] = grad
        attn = attn_ref[...]
        factor = inv_rms(attn)
        normed = attn * factor
        sums = jnp.sum(grad * normed, axis=0, keepdims=True)
        sum_ref[...] = jnp.broadcast_to(sums, sum_ref.shape)
        d_ref[...] = rms_back(normed, factor, gain_ref[...], grad).astype(BF)

    piece = nt_dot(d_ref[...], w_ref[...]).astype(BF)
    for p, out in enumerate(outs):

        @pl.when(step == p)
        def _(out=out):
            out[...] = piece


def residual_back(me, own, got, cot, attn_out, gain, w_first, count):
    tokens, width = own.shape
    part = width // count
    piece = pl.BlockSpec((tokens, part), lambda p, me: (0, 0))
    full = once((tokens, width), lambda p, me: (0, 0))
    whole = lambda rows: pl.BlockSpec((rows, width), lambda p, me: (0, 0))
    return pl.pallas_call(
        residual_back_kernel,
        grid_spec=pltpu.PrefetchScalarGridSpec(
            num_scalar_prefetch=1,
            grid=(count,),
            in_specs=[full] * 7
            + [whole(1), pl.BlockSpec((part, width), lambda p, me: ((me[0] + p) % count, 0))],
            out_specs=[whole(tokens), whole(tokens), whole(8)] + [piece] * count,
        ),
        out_shape=[
            jax.ShapeDtypeStruct((tokens, width), F32),
            jax.ShapeDtypeStruct((tokens, width), BF),
            jax.ShapeDtypeStruct((8, width), F32),
        ]
        + [jax.ShapeDtypeStruct((tokens, part), BF)] * count,
        compiler_params=params(),
        cost_estimate=cost(LATE_COST, 0),
        name="residual_back",
    )(me, own, *got, cot, attn_out, gain[None], w_first)


def input_back_kernel(
    part, me_ref, q_ref, k_ref, v_ref, qp_ref, kp_ref, in_ref, f_ref, w_ref, d_ref, ends_ref, *outs
):
    for j, (grad, proj) in enumerate(((q_ref, qp_ref), (k_ref, kp_ref))):
        factor = f_ref[:, j : j + 1]
        normed = proj[...] * factor
        low = ((grad[...] - normed * in_ref[:, j : j + 1]) * factor).astype(BF)
        d_ref[:, j * part : (j + 1) * part] = low
    d_ref[:, 2 * part :] = v_ref[...]
    total = nt_dot(d_ref[...], w_ref[...])
    step = pl.program_id(0)
    for j, out in enumerate(outs):

        @pl.when(step == j)
        def _(out=out):
            out[...] = total.astype(out.dtype)

    @pl.when((step == 0) | ((step == 1) & (me_ref[0] == 0)))
    def _():
        ends_ref[...] = total.astype(BF)


def input_back(me, d_query, d_key, d_v, qkv, inner, factors, w_qkv):
    length, part = d_query.shape
    width = w_qkv.shape[0]
    tokens = length // 4
    place = lambda t: jnp.where(t == 0, 1, jnp.where(t == 1, 3, jnp.where(t == 2, 2, 0)))
    rows = lambda columns, at=0: pl.BlockSpec((tokens, columns), lambda t, me: (place(t), at))
    kinds = (BF, BF, BF, BF, F32)
    return pl.pallas_call(
        functools.partial(input_back_kernel, part),
        grid_spec=pltpu.PrefetchScalarGridSpec(
            num_scalar_prefetch=1,
            grid=(4,),
            in_specs=[rows(part)] * 3
            + [rows(part), rows(part, 1), rows(2), rows(2)]
            + [once((width, 3 * part), lambda t, me: (0, 0))],
            out_specs=[rows(3 * part)]
            + [pl.BlockSpec((tokens, width), lambda t, me: (0, 0))] * len(kinds),
        ),
        out_shape=[jax.ShapeDtypeStruct((length, 3 * part), BF)]
        + [jax.ShapeDtypeStruct((tokens, width), kind) for kind in kinds],
        compiler_params=params(),
        cost_estimate=cost(0, 0),
        name="input_back",
    )(me, d_query, d_key, d_v, qkv, qkv, inner, factors, w_qkv)


def add_up_kernel(*refs):
    total = refs[0][...]
    for ref in refs[1:-1]:
        total = total + ref[...].astype(F32)
    refs[-1][...] = total.astype(BF)


def add_up(parts):
    tokens, width = parts[0].shape
    tile = tokens // 4
    block = pl.BlockSpec((tile, width), lambda i: (i, 0))
    return pl.pallas_call(
        add_up_kernel,
        grid=(4,),
        in_specs=[block] * len(parts),
        out_specs=block,
        out_shape=jax.ShapeDtypeStruct((tokens, width), BF),
        compiler_params=params(),
        cost_estimate=cost(LATE_COST, 0),
        name="add_up",
    )(*parts)


def tn_dot(left, right):
    return lax.dot_general(left, right, (((0,), (0,)), ((), ())), preferred_element_type=F32)


def weight_grad_kernel(lefts, right_ref, out_ref):
    total, at = None, 0
    for left in lefts:
        rows = left.shape[0]
        product = tn_dot(left[...], right_ref[at : at + rows, :])
        total = product if total is None else total + product
        at += rows
    out_ref[...] = total.astype(BF)


def weight_grad(lefts, right, declared=0):
    width = lefts[0].shape[1]
    length, columns = right.shape
    tile, wide = 256, min(columns, 2048)
    return pl.pallas_call(
        lambda *refs: weight_grad_kernel(refs[:-2], *refs[-2:]),
        grid=(columns // wide, width // tile),
        in_specs=[pl.BlockSpec((left.shape[0], tile), lambda j, i: (0, i)) for left in lefts]
        + [pl.BlockSpec((length, wide), lambda j, i: (0, j))],
        out_specs=pl.BlockSpec((tile, wide), lambda j, i: (i, j)),
        out_shape=jax.ShapeDtypeStruct((width, columns), BF),
        compiler_params=params(),
        cost_estimate=cost(declared, 0),
        name="weight_grad",
    )(*lefts, right)


def attn_grad_kernel(count, me_ref, x_ref, d_ref, *refs):
    pieces, parts, out_ref = refs[:count], refs[count : 2 * count], refs[-1]
    columns = d_ref.shape[1]
    out_ref[:, :columns] = tn_dot(x_ref[...], d_ref[...]).astype(BF)
    source = (pl.program_id(0) // (pl.num_programs(0) // count) + count - me_ref[0]) % count
    for p, piece in enumerate(pieces):

        @pl.when(source == p)
        def _(p=p, piece=piece):
            total, tokens = None, parts[0].shape[0]
            for q in range(count):
                rows = slice(q * tokens, (q + 1) * tokens)
                product = tn_dot(piece[rows, :], parts[(q + p) % count][...])
                total = product if total is None else total + product
            out_ref[:, columns:] = total.astype(BF)


def attn_grad(me, x_all, d_qkv, pieces, d_parts):
    count = len(pieces)
    length, width = x_all.shape
    columns, part = d_qkv.shape[1], d_parts[0].shape[1]
    tile = min(256, part)
    per_part = part // tile
    return pl.pallas_call(
        functools.partial(attn_grad_kernel, count),
        grid_spec=pltpu.PrefetchScalarGridSpec(
            num_scalar_prefetch=1,
            grid=(width // tile,),
            in_specs=[
                pl.BlockSpec((length, tile), lambda i, me: (0, i)),
                once((length, columns), lambda i, me: (0, 0)),
            ]
            + [pl.BlockSpec((length, tile), lambda i, me: (0, i % per_part))] * count
            + [once((length // count, part), lambda i, me: (0, 0))] * count,
            out_specs=pl.BlockSpec((tile, columns + part), lambda i, me: (i, 0)),
        ),
        out_shape=jax.ShapeDtypeStruct((width, columns + part), BF),
        compiler_params=params(),
        cost_estimate=cost(SIDE_COST, 0),
        name="attn_grad",
    )(me, x_all, d_qkv, *pieces, *d_parts)


def cost(flops, moved, exps=0):
    return pl.CostEstimate(flops=flops, bytes_accessed=moved, transcendentals=exps)


def params():
    return pltpu.CompilerParams(vmem_limit_bytes=56 << 20)


def once(shape, index):
    return pl.BlockSpec(shape, index, pipeline_mode=pl.Buffered(1))


def nt_dot(left, right):
    return lax.dot_general(left, right, (((1,), (1,)), ((), ())), preferred_element_type=F32)


def feature_sums(values):
    ones = jnp.ones((8, values.shape[1]), BF)
    total = None
    for _ in range(3):
        term = values.astype(BF)
        values = values - term.astype(F32)
        total = nt_dot(ones, term) if total is None else total + nt_dot(ones, term)
    return total


def two_rows(first, second):
    return jnp.where(lax.broadcasted_iota(jnp.int32, first.shape, 0) == 0, first, second)


def qkv_kernel(part, saved, me_ref, *refs):
    chunks, w_ref, (x_ref, qkv_ref, sq_ref) = refs[: -4 - saved], refs[-4 - saved], refs[-3:]
    step, me = pl.program_id(0), me_ref[0]
    at_end = (step == 0) & (me == 3) | (step == 1) & (me == 0) if len(chunks) == 3 else step < 0
    for q in range(2):

        @pl.when((step == q) & jnp.logical_not(at_end))
        def _(q=q):
            x_ref[...] = chunks[q][...]

    @pl.when(at_end)
    def _():
        x_ref[...] = chunks[-1][...]

    qkv = jnp.dot(x_ref[...], w_ref[...], preferred_element_type=F32)
    qkv_ref[...] = qkv
    q, k = (qkv[:, j * part : (j + 1) * part] for j in range(2))
    sq_ref[0] = two_rows(feature_sums(q * q), feature_sums(k * k))


def qkv_project(me, first, chunks, w_qkv, saved=()):
    tokens, width = chunks[0].shape
    columns = w_qkv.shape[1]
    length = 4 * tokens
    place = lambda q: 2 * q + first
    return pl.pallas_call(
        functools.partial(qkv_kernel, columns // 3, len(saved)),
        grid_spec=pltpu.PrefetchScalarGridSpec(
            num_scalar_prefetch=1,
            grid=(2,),
            in_specs=[once((tokens, width), lambda q, me: (0, 0))] * len(chunks)
            + [once((width, columns), lambda q, me: (0, 0))]
            + [pl.BlockSpec(memory_space=pl.ANY)] * len(saved),
            out_specs=[
                pl.BlockSpec((tokens, width), lambda q, me: (place(q), 0)),
                pl.BlockSpec((tokens, columns), lambda q, me: (place(q), 0)),
                pl.BlockSpec((1, 8, tokens), lambda q, me: (place(q), 0, 0)),
            ],
        ),
        out_shape=[
            jax.ShapeDtypeStruct((length, width), BF),
            jax.ShapeDtypeStruct((length, columns), F32),
            jax.ShapeDtypeStruct((4, 8, tokens), F32),
        ],
        input_output_aliases={2 + len(chunks) + j: j for j in range(len(saved))},
        compiler_params=params(),
        cost_estimate=cost(0, 0),
        name="qkv_project",
    )(me, *chunks, w_qkv, *saved)


FF_TILE = 512
LATE_COST = 10**12
SIDE_COST = 10**11


def ff_finish(step, product, acc, me_ref, outs):
    @pl.when(step == 0)
    def _():
        acc[...] = product

    @pl.when(step > 0)
    def _():
        acc[...] += product

    @pl.when(step == pl.num_programs(0) - 1)
    def _():
        tokens = outs[0].shape[0]
        for j, out in enumerate(outs[:2]):
            out[...] = acc[j * tokens : (j + 1) * tokens].astype(out.dtype)
        if len(outs) == 3:
            at = pl.multiple_of(jnp.where(me_ref[0] == 0, tokens, 0), tokens)
            outs[2][...] = acc[pl.ds(at, tokens), :].astype(BF)


def ff_kernel(saved, me_ref, h_ref, wg_ref, wu_ref, wd_ref, *refs):
    gate_ref, up_ref, hid_ref = refs[saved : saved + 3]
    h = h_ref[...]
    gate = jnp.dot(h, wg_ref[...], preferred_element_type=F32)
    up = jnp.dot(h, wu_ref[...], preferred_element_type=F32)
    hidden = (gate * (1.0 / (1.0 + jnp.exp(-gate))) * up).astype(BF)
    gate_ref[...] = gate
    up_ref[...] = up
    hid_ref[...] = hidden
    product = nt_dot(hidden, wd_ref[...])
    ff_finish(pl.program_id(0), product, refs[-1], me_ref, refs[saved + 3 : -1])


def ff_back_kernel(saved, groups, me_ref, *refs):
    d_refs, (wg_ref, wu_ref, wd_ref, gate_ref, up_ref) = refs[:groups], refs[groups : groups + 5]
    refs = refs[groups + 5 :]
    dgu_ref = refs[saved]
    tile = wg_ref.shape[1]
    d_ff = d_refs[0][...] if groups == 1 else jnp.concatenate([d[...] for d in d_refs], axis=0)
    d_hidden = jnp.dot(d_ff, wd_ref[...], preferred_element_type=F32)
    gate = gate_ref[...]
    sig = 1.0 / (1.0 + jnp.exp(-gate))
    d_gate = (d_hidden * up_ref[...] * sig * (1.0 + gate * (1.0 - sig))).astype(BF)
    d_up = (d_hidden * gate * sig).astype(BF)
    dgu_ref[:, :tile] = d_gate
    dgu_ref[:, tile:] = d_up
    product = nt_dot(d_gate, wg_ref[...]) + nt_dot(d_up, wu_ref[...])
    ff_finish(pl.program_id(0), product, refs[-1], me_ref, refs[saved + 1 : -1])


def ff_specs(width, tile, gate_at):
    rest = pl.BlockSpec((width, tile), lambda t: (0, t))
    return [pl.BlockSpec((width, tile), lambda t: (0, gate_at // tile + t)), rest, rest]


def ff_forward(me, residual_all, w_first, w_up, w_down, place, kinds, saved=()):
    length, width = residual_all.shape
    tokens = length // 4
    group = min(len(kinds), 2)
    rows = group * tokens
    ff_part = w_up.shape[1]
    tile = min(FF_TILE, ff_part)
    block = pl.BlockSpec((rows, tile), lambda t: (place // group, t))
    whole = pl.BlockSpec((tokens, width), lambda t: (0, 0))
    shape = lambda kind: jax.ShapeDtypeStruct((length, ff_part), kind)
    return pl.pallas_call(
        functools.partial(ff_kernel, len(saved)),
        grid=(ff_part // tile,),
        in_specs=[pl.BlockSpec(memory_space=pltpu.SMEM)]
        + [once((rows, width), lambda t: (place // group, 0))]
        + ff_specs(width, tile, w_first.shape[1] - ff_part)
        + [pl.BlockSpec(memory_space=pl.ANY)] * len(saved),
        out_specs=[block] * 3 + [whole] * len(kinds),
        out_shape=[shape(F32), shape(F32), shape(BF)]
        + [jax.ShapeDtypeStruct((tokens, width), kind) for kind in kinds],
        scratch_shapes=[pltpu.VMEM((rows, width), F32)],
        input_output_aliases={5 + j: j for j in range(len(saved))},
        compiler_params=params(),
        cost_estimate=cost(0, 0),
        name="ff_forward",
    )(me, residual_all, w_first, w_up, w_down, *saved)


def ff_backward(me, d_ffs, w_first, w_up, w_down, gate, up, place, kinds, saved=()):
    tokens, width = d_ffs[0].shape
    group = len(d_ffs)
    rows = group * tokens
    length = gate.shape[0]
    ff_part = w_up.shape[1]
    tile = min(FF_TILE, ff_part)
    block = pl.BlockSpec((rows, tile), lambda t: (place // group, t))
    whole = pl.BlockSpec((tokens, width), lambda t: (0, 0))
    return pl.pallas_call(
        functools.partial(ff_back_kernel, len(saved), group),
        grid=(ff_part // tile,),
        in_specs=[pl.BlockSpec(memory_space=pltpu.SMEM)]
        + [once((tokens, width), lambda t: (0, 0))] * group
        + ff_specs(width, tile, w_first.shape[1] - ff_part)
        + [block, block]
        + [pl.BlockSpec(memory_space=pl.ANY)] * len(saved),
        out_specs=[pl.BlockSpec((rows, 2 * tile), lambda t: (place // group, t))]
        + [whole] * len(kinds),
        out_shape=[jax.ShapeDtypeStruct((length, 2 * ff_part), BF)]
        + [jax.ShapeDtypeStruct((tokens, width), kind) for kind in kinds],
        scratch_shapes=[pltpu.VMEM((rows, width), F32)],
        input_output_aliases={6 + group + j: j for j in range(len(saved))},
        compiler_params=params(),
        cost_estimate=cost(SIDE_COST, 0),
        name="ff_backward",
    )(me, *d_ffs, w_first, w_up, w_down, gate, up, *saved)


def out_kernel(count, part, *refs):
    me_ref, pieces, (w_ref, x_ref, g_ref, res_ref, own_ref) = refs[0], refs[1:-5], refs[-5:]
    total = None
    for p, piece in enumerate(pieces):
        rows = pl.ds(pl.multiple_of((me_ref[0] + p) % count * part, part), part)
        product = jnp.dot(piece[...], w_ref[rows, :], preferred_element_type=F32)
        total = product if total is None else total + product
    normed = total * inv_rms(total)
    res_ref[...] = (x_ref[...].astype(F32) + normed * g_ref[...]).astype(BF)

    @pl.when(pl.program_id(0) == 0)
    def _():
        own_ref[...] = total


def ff_place(q):
    return jnp.where(q == 0, 3, jnp.where(q == 3, 1, jnp.where(q == 2, 2, 0)))


def out_project(me, pieces, w_out, x_all, gain, count):
    length, width = x_all.shape
    tokens = length // count
    part = pieces[0].shape[1]
    rolled = lambda p: pl.BlockSpec((tokens, part), lambda q, me: ((q + count - p) % count, 0))
    chunk = pl.BlockSpec((tokens, width), lambda q, me: (q, 0))
    moved = pl.BlockSpec((tokens, width), lambda q, me: (ff_place(q), 0))
    return pl.pallas_call(
        functools.partial(out_kernel, count, part),
        grid_spec=pltpu.PrefetchScalarGridSpec(
            num_scalar_prefetch=1,
            grid=(count,),
            in_specs=[rolled(p) for p in range(count)]
            + [pl.BlockSpec((width, width), lambda q, me: (0, 0), pipeline_mode=pl.Buffered(1))]
            + [chunk, pl.BlockSpec((1, width), lambda q, me: (0, 0))],
            out_specs=[moved, pl.BlockSpec((tokens, width), lambda q, me: (0, 0))],
        ),
        out_shape=[
            jax.ShapeDtypeStruct((length, width), BF),
            jax.ShapeDtypeStruct((tokens, width), F32),
        ],
        compiler_params=params(),
        cost_estimate=cost(0, 0),
        name="out_project",
    )(me, *pieces, w_out, x_all, gain[None])


def columns_to_parts(values, me, count):
    part = values.shape[1] // count
    columns = lambda p: lax.dynamic_slice_in_dim(values, (me + p) % count * part, part, 1)
    got = [columns(0)] + [
        lax.ppermute(columns(p), "seq", [(i, (i + p) % count) for i in range(count)])
        for p in range(1, count)
    ]
    return [got[(count - q) % count] for q in range(count)]


def build(dp_count, seq_count):
    assert seq_count == 4

    def shards(
        layer_input,
        segments,
        w_query,
        w_key,
        w_value,
        w_output,
        w_gate,
        w_up,
        w_down,
        query_gain,
        key_gain,
        attn_gain,
        ff_gain,
        cotangent,
    ):
        n = seq_count
        tokens, width = layer_input.shape[1:]
        shard_rows = w_query.shape[0]
        part = width // n
        ff_part = w_gate.shape[1] // n
        length = n * tokens
        devices = dp_count * n
        me = lax.axis_index("seq")
        me_ref = me[None].astype(jnp.int32)
        cot = cotangent[0]
        by_part = lambda w: w.reshape(shard_rows, n, -1).transpose(1, 0, 2)
        rows_of = lambda blocks: blocks.reshape(n * shard_rows, -1)

        fence = lax.optimization_barrier
        qkv_blocks = jnp.concatenate([by_part(w) for w in (w_query, w_key, w_value)], axis=2)
        qkv_blocks = swap_blocks(qkv_blocks)
        w_qkv = gather_dp(rows_of(qkv_blocks))
        natural = jnp.arange(length, dtype=jnp.int32)
        positions = (natural + me * tokens) % length
        seg_row = segments[0]
        seg = lax.dynamic_slice_in_dim(
            jnp.concatenate([seg_row, seg_row]), me * tokens, length, 0
        )
        tables = rope_tables(positions.astype(F32))
        own_gain = lambda g: lax.dynamic_slice_in_dim(g, me * part, part, 0)
        q_gain = own_gain(query_gain)
        k_gain = own_gain(key_gain)

        up_columns, down_columns = (part_columns(w, me, n) for w in (w_up, w_down.T))
        ready = (seg, tables, q_gain, k_gain, up_columns, down_columns)
        qkv_blocks, w_output, w_gate = fence((qkv_blocks, w_output, w_gate))
        out_blocks = gather_cyclic(w_output, n)
        gate_blocks = send_blocks(part_columns(w_gate, me, n))
        out_blocks, gate_blocks, x_own, ready = fence(
            (out_blocks, gate_blocks, layer_input[0], ready)
        )
        seg, tables, q_gain, k_gain, up_columns, down_columns = ready
        out_blocks = out_blocks[:1] + out_blocks[:0:-1]
        w_first = place_blocks(out_blocks, me, 0, width + ff_part)
        w_first = gather_dp(place_blocks(gate_blocks, me, width, width + ff_part, w_first))
        x_own, x_after, x_far, x_before, x_ends = gather_raw(x_own, n)
        saved = qkv_project(me_ref, 0, [x_own, x_far], w_qkv)
        x_sides, saved, up_columns = fence(([x_after, x_before, x_ends], saved, up_columns))
        up_blocks = send_blocks(up_columns)
        x_all, qkv, squares = qkv_project(me_ref, 1, x_sides, w_qkv, saved)
        squares, up_blocks = fence((squares, up_blocks))
        w_up_all = gather_dp(place_blocks(up_blocks, me, 0, ff_part))

        squares = sum_stats(squares, n)
        squares, down_columns = fence((squares, down_columns))
        down_blocks = send_blocks(down_columns)
        factors = lax.rsqrt(stat_columns(squares) / width + EPSILON)
        mixed, q_low, k_low, v_low = attend(me_ref, qkv, factors, q_gain, k_gain, tables, seg, n)

        mixed, down_blocks = fence((mixed, down_blocks))
        w_down_all = gather_dp(place_blocks(down_blocks, me, 0, ff_part))
        pieces = gather_cyclic(mixed, n)
        residual_all, attn_out = out_project(me_ref, pieces, w_first, x_all, attn_gain, n)
        attn_factor = inv_rms(attn_out)
        attn_normed = attn_out * attn_factor
        residual = x_own.astype(F32) + attn_normed * attn_gain

        *saved, far = ff_forward(me_ref, residual_all, w_first, w_up_all, w_down_all, 2, (BF,))
        across = lax.ppermute(far, "seq", [(0, 2), (3, 1)])
        *saved, after, before, ends = ff_forward(
            me_ref, residual_all, w_first, w_up_all, w_down_all, 0, (BF, BF, BF), saved
        )
        after, before, ends, across, residual_late = fence(
            (after, before, ends, across, residual_all)
        )
        sent = scatter_start(ends, after, before, n)
        gate, up, hidden, own = ff_forward(
            me_ref, residual_late, w_first, w_up_all, w_down_all, 3, (F32,), saved
        )
        own, sent[0] = fence((own, sent[0]))
        sent[0] = scatter_far(far, sent[0])
        ff_out = scatter_end(own, sent + [across])
        ff_factor = inv_rms(ff_out)
        ff_normed = ff_out * ff_factor
        activation = (residual + ff_normed * ff_gain).astype(BF)
        grad_ff_gain = jnp.sum(cot.astype(F32) * ff_normed, axis=0)
        d_ff = rms_back(ff_normed, ff_factor, ff_gain, cot.astype(F32)).astype(BF)
        d_ffs = gather_cyclic(d_ff, n)
        d_both, own = ff_backward(me_ref, d_ffs[:1], w_first, w_up_all, w_down_all, gate, up, 3, (F32,))
        d_both, far = ff_backward(
            me_ref, d_ffs[2:3], w_first, w_up_all, w_down_all, gate, up, 2, (BF,), (d_both,)
        )
        d_ffs, d_both, far = fence((d_ffs, d_both, far))
        across = lax.ppermute(far, "seq", [(0, 2), (3, 1)])
        d_both, after, before, ends = ff_backward(
            me_ref, d_ffs[1::2], w_first, w_up_all, w_down_all, gate, up, 0, (BF, BF, BF), (d_both,)
        )
        after, before, ends, across, d_ffs, hidden = fence(
            (after, before, ends, across, d_ffs, hidden)
        )
        ends, *sent = scatter_start(ends, after, before, n)
        joined = lambda g: g.transpose(1, 0, 2).reshape(shard_rows, -1).astype(F32)
        down_grad = weight_grad([d_ffs[1], d_ffs[3], d_ffs[2], d_ffs[0]], hidden, SIDE_COST)
        ends, down_grad = fence((ends, down_grad))
        down_rows = scatter_dp(down_grad)
        sent = [scatter_far(far, ends)] + sent
        d_res, d_attn, grad_attn_gain, *d_pieces = residual_back(
            me_ref, own, sent + [across], cot, attn_out, attn_gain, w_first, n
        )
        d_mixed = [d_pieces[0]] + [None] * (n - 1)
        for p in range(1, n):
            d_mixed[n - p] = lax.ppermute(
                d_pieces[p], "seq", [(i, (i + p) % n) for i in range(n)]
            )
        residual_all, d_both, _ = fence((residual_all, d_both, d_pieces[0]))
        gate_up_grad = weight_grad([residual_all], d_both)
        d_mixed, d_attn, gate_up_grad = fence((d_mixed, d_attn, gate_up_grad))
        gate_up_rows = scatter_dp(gate_up_grad)
        d_attn_part = columns_to_parts(d_attn, me, n)
        d_query, d_key, d_v, inner, gain_sums = attend_back(
            me_ref, d_mixed, q_low, k_low, v_low, qkv, factors, q_gain, k_gain, tables, seg, n
        )
        inner, d_attn_part, down_back = fence(
            (inner, d_attn_part, row_blocks(down_rows, me, n))
        )
        inner = sum_stats(inner, n)
        inner, down_back = fence((inner, down_back))
        down_back = send_blocks(down_back)
        d_qkv, ends, after, before, far, own = input_back(
            me_ref, d_query, d_key, d_v, qkv, stat_columns(inner) / width, factors, w_qkv
        )
        d_qkv, ends, after, before, far, own, down_back = fence(
            (d_qkv, ends, after, before, far, own, down_back)
        )
        ends, *sent = scatter_start(ends, after, before, n)
        sent.append(lax.ppermute(far, "seq", [(0, 2), (3, 1)]))
        attn_grads = attn_grad(me_ref, x_all, d_qkv, pieces, d_attn_part)
        ends, attn_grads = fence((ends, attn_grads))
        attn_rows = scatter_dp(attn_grads)
        sent.append(scatter_far(far, ends))
        gate_up_back = row_blocks(gate_up_rows, me, n)
        sent, gate_up_back = fence((sent, gate_up_back))
        input_grad = add_up([d_res, own] + sent)
        spread = lambda g: lax.dynamic_update_slice(jnp.zeros(width, F32), g, (me * part,))
        gains = jnp.stack(
            [spread(gain_sums[0, 0]), spread(gain_sums[1, 0]), grad_attn_gain[0], grad_ff_gain]
        )
        input_grad, gains = fence((input_grad, gains))
        gate_up_back = send_blocks(gate_up_back)
        gains = sum_everywhere(gains, dp_count, n)
        attn_rows, input_grad, gate_up_back, down_back, gains = fence(
            (attn_rows, input_grad, gate_up_back, down_back, gains)
        )
        attn_back = swap_blocks(attn_rows.reshape(n, shard_rows, -1))
        grad_gate, grad_up = join_columns(me_ref, gate_up_back, 2)
        grad_down = join_columns(me_ref, down_back, 1)[0].T
        attn_back, grad_gate, grad_up, grad_down = fence(
            (attn_back, grad_gate, grad_up, grad_down)
        )
        grad_query, grad_key, grad_value, grad_output = (
            joined(attn_back[:, :, j * part : (j + 1) * part]) for j in range(4)
        )

        share = width // devices
        gains = lax.dynamic_slice_in_dim(
            gains, (lax.axis_index("dp") * n + me) * share, share, 1
        )
        return (
            activation[None],
            input_grad[None],
            grad_query,
            grad_key,
            grad_value,
            grad_output,
            grad_gate,
            grad_up,
            grad_down,
            gains[0],
            gains[1],
            gains[2],
            gains[3],
        )

    return shards


def solution(mesh):
    both = P(("dp", "seq"), None)
    tokens = P("dp", "seq", None)
    columns = P(None, ("dp", "seq"))
    gain = P(("dp", "seq"))
    return jax.shard_map(
        build(mesh.shape["dp"], mesh.shape["seq"]),
        mesh=mesh,
        in_specs=(tokens, P("dp", None)) + (both,) * 6 + (columns,) + (P(),) * 4 + (tokens,),
        out_specs=(tokens, tokens) + (both,) * 6 + (columns,) + (gain,) * 4,
        check_vma=False,
    )
```

```python
import functools

import jax
import jax.numpy as jnp
from jax import lax
from jax.experimental import pallas as pl
from jax.experimental.pallas import tpu as pltpu
from jax.sharding import PartitionSpec as P

HD = 128
EPSILON = 1e-06
ROPE_BASE = 500000.0
MASKED = -1e30
LOG2E = 1.4426950408889634
BF = jnp.bfloat16
F32 = jnp.float32


def inv_rms(values):
    return lax.rsqrt(jnp.mean(values * values, axis=-1, keepdims=True) + EPSILON)


def rms_back(normed, factor, gain, grad):
    scaled = grad * gain
    inner = jnp.mean(scaled * normed, axis=-1, keepdims=True)
    return (scaled - normed * inner) * factor


def rope_tables(positions):
    half_dim = HD // 2
    frequency = jnp.power(F32(ROPE_BASE), -jnp.arange(half_dim, dtype=F32) * (2.0 / HD))
    angles = positions[:, None] * frequency[None, :]
    cosine, sine = jnp.cos(angles), jnp.sin(angles)
    return (jnp.concatenate([cosine, cosine], axis=-1), jnp.concatenate([-sine, sine], axis=-1))


def shift(values, count, step):
    return lax.ppermute(values, "seq", [((i + step) % count, i) for i in range(count)])


def gather_raw(values, count):
    far = lax.ppermute(values, "seq", [(i ^ 2, i) for i in range(count)])
    after = lax.ppermute(values, "seq", [(i + 1, i) for i in range(count - 1)])
    before = lax.ppermute(values, "seq", [(i, i + 1) for i in range(count - 1)])
    ends = lax.ppermute(far, "seq", [(2, 3), (1, 0)])
    return [values, after, far, before, ends]


def gather_cyclic(values, count):
    own, after, far, before, ends = gather_raw(values, count)
    me = lax.axis_index("seq")
    after = jnp.where(me == count - 1, ends, after)
    return [own, after, far, jnp.where(me == 0, ends, before)]


def scatter_start(ends, after, before, count):
    ends = lax.ppermute(ends, "seq", [(0, 1), (count - 1, count - 2)])
    step = [(i, i + 1) for i in range(count - 1)]
    after = lax.ppermute(after, "seq", step)
    before = lax.ppermute(before, "seq", [(j, i) for i, j in step])
    return [ends, after, before]


def scatter_far(far, ends):
    far = (far.astype(F32) + ends.astype(F32)).astype(BF)
    return lax.ppermute(far, "seq", [(1, 3), (2, 0)])


def scatter_end(own, got):
    for part in got:
        own = own + part.astype(F32)
    return own


def sum_stats(stats, count):
    total = stats
    for p in range(1, count):
        total = total + jnp.roll(shift(stats, count, p), p, axis=0)
    return total


def stat_columns(stats):
    return stats[:, :2].transpose(0, 2, 1).reshape(-1, 2)


def sum_everywhere(values, dp_count, seq_count):
    for name, count in (("dp", dp_count), ("seq", seq_count)):
        if count & (count - 1):
            values = lax.psum(values, name)
            continue
        bit = 1
        while bit < count:
            values = values + lax.ppermute(values, name, [(i, i ^ bit) for i in range(count)])
            bit *= 2
    return values


def swap_blocks(values):
    return lax.all_to_all(values, "seq", split_axis=0, concat_axis=0, tiled=True)


def part_columns(values, me, count):
    part = values.shape[1] // count
    return [
        lax.dynamic_slice_in_dim(values, (me + p) % count * part, part, 1) for p in range(count)
    ]


def place_blocks(blocks, me, first, width, total=None):
    count = len(blocks)
    rows = blocks[0].shape[0]
    if total is None:
        total = jnp.zeros((count * rows, width), blocks[0].dtype)
    for p, block in enumerate(blocks):
        total = lax.dynamic_update_slice(total, block, ((me - p) % count * rows, first))
    return total


def row_blocks(values, me, count):
    size = values.shape[0] // count
    return [
        lax.dynamic_slice_in_dim(values, (me + p) % count * size, size, 0) for p in range(count)
    ]


def send_blocks(blocks):
    count = len(blocks)
    return blocks[:1] + [
        lax.ppermute(blocks[p], "seq", [(i, (i + p) % count) for i in range(count)])
        for p in range(1, count)
    ]


def join_kernel(sides, me_ref, *refs):
    blocks, outs = refs[:-sides], refs[-sides:]
    for p, block in enumerate(blocks):

        @pl.when(pl.program_id(0) == p)
        def _(block=block):
            for j, out in enumerate(outs):
                tile = min(FF_TILE, out.shape[1])
                for at in range(0, out.shape[1], tile):
                    first = at * sides + j * tile
                    out[:, at : at + tile] = block[:, first : first + tile].astype(F32)


def join_columns(me, blocks, sides):
    count = len(blocks)
    rows, columns = blocks[0].shape
    part = columns // sides
    out = pl.BlockSpec((rows, part), lambda p, me: (0, (me[0] + count - p) % count))
    return pl.pallas_call(
        functools.partial(join_kernel, sides),
        grid_spec=pltpu.PrefetchScalarGridSpec(
            num_scalar_prefetch=1,
            grid=(count,),
            in_specs=[once((rows, columns), lambda p, me: (0, 0))] * count,
            out_specs=[out] * sides,
        ),
        out_shape=[jax.ShapeDtypeStruct((rows, count * part), F32)] * sides,
        compiler_params=params(),
        cost_estimate=cost(0, 0),
        name="join_columns",
    )(me, *blocks)


def gather_dp(values):
    return lax.all_gather(values, "dp", axis=0, tiled=True)


def scatter_dp(values):
    return lax.psum_scatter(values, "dp", scatter_dimension=0, tiled=True)


def softmax_window(q, k_ref, seg_q, seg_row_ref, valid_from, place, tokens, count, span):
    parts = []
    for w in range(span):
        at = ((place - w) % count) * tokens
        scores = lax.dot_general(
            q, k_ref[at : at + tokens, :], (((1,), (1,)), ((), ())), preferred_element_type=F32
        )
        seg = seg_q if w == 0 else jnp.where(valid_from >= w, seg_q, -1)
        allowed = seg == seg_row_ref[:, at : at + tokens]
        if w == 0:
            rows = lax.broadcasted_iota(jnp.int32, (tokens, tokens), 0)
            cols = lax.broadcasted_iota(jnp.int32, (tokens, tokens), 1)
            allowed = allowed & (cols <= rows)
        parts.append(jnp.where(allowed, scores, MASKED))
    top = parts[0]
    for part in parts[1:]:
        top = jnp.maximum(top, part)
    top = jnp.max(top, axis=-1, keepdims=True)
    exps = [jnp.exp2((part - top) * (HD**-0.5 * LOG2E)) for part in parts]
    total = exps[0]
    for part in exps[1:]:
        total = total + part
    inverse = 1.0 / jnp.sum(total, axis=-1, keepdims=True)
    return [part * inverse for part in exps]


def turn(values, cosine, sine):
    return values * cosine + pltpu.roll(values, HD // 2, 1) * sine


def attend_kernel(
    tokens, count, span,
    me_ref, q_ref, k_ref, v_ref, f_ref, qg_ref, kg_ref, cos_ref, sin_ref, segc_ref, segr_ref,
    o_ref, qb_ref, kb_ref, vb_ref,
):
    cosine, sine = cos_ref[...], sin_ref[...]
    factors = f_ref[...]
    qb_ref[...] = turn(q_ref[...] * factors[:, 0:1] * qg_ref[...], cosine, sine).astype(BF)
    kb_ref[...] = turn(k_ref[...] * factors[:, 1:2] * kg_ref[...], cosine, sine).astype(BF)
    vb_ref[...] = v_ref[...].astype(BF)
    for place in range(count):
        rows = slice(place * tokens, (place + 1) * tokens)
        chunk = (me_ref[0] + place) % count
        probs = softmax_window(
            qb_ref[rows, :], kb_ref, segc_ref[rows, :], segr_ref, chunk, place, tokens, count, span
        )
        mixed = None
        for w in range(span):
            at = ((place - w) % count) * tokens
            part = jnp.dot(probs[w].astype(BF), vb_ref[at : at + tokens, :], preferred_element_type=F32)
            mixed = part if mixed is None else mixed + part
        o_ref[rows, :] = mixed.astype(BF)


def attend_back_kernel(
    tokens, count, span, me_ref, *refs
):
    grads_in = refs[:count]
    (q_ref, k_ref, v_ref, qp_ref, kp_ref, f_ref, qg_ref, kg_ref, cos_ref, sin_ref, segc_ref, segr_ref,
     dq_ref, dk_ref, dv_ref, inner_ref, gain_ref, dk_sum, dv_sum) = refs[count:]
    scale = HD**-0.5
    dk_sum[...] = jnp.zeros_like(dk_sum)
    dv_sum[...] = jnp.zeros_like(dv_sum)
    for place in range(count):
        rows = slice(place * tokens, (place + 1) * tokens)
        chunk = (me_ref[0] + place) % count
        q = q_ref[rows, :]
        grad = grads_in[place][...]
        probs = softmax_window(
            q, k_ref, segc_ref[rows, :], segr_ref, chunk, place, tokens, count, span
        )
        grads = []
        inner = None
        for w in range(span):
            at = ((place - w) % count) * tokens
            part = nt_dot(grad, v_ref[at : at + tokens, :])
            grads.append(part)
            inner = probs[w] * part if inner is None else inner + probs[w] * part
            dv_sum[at : at + tokens, :] += lax.dot_general(
                probs[w].astype(BF), grad, (((0,), (0,)), ((), ())), preferred_element_type=F32
            )
        inner = jnp.sum(inner, axis=-1, keepdims=True)
        dq = None
        for w in range(span):
            at = ((place - w) % count) * tokens
            ds = (probs[w] * (grads[w] - inner)).astype(BF)
            part = jnp.dot(ds, k_ref[at : at + tokens, :], preferred_element_type=F32)
            dq = part if dq is None else dq + part
            dk_sum[at : at + tokens, :] += lax.dot_general(
                ds, q, (((0,), (0,)), ((), ())), preferred_element_type=F32
            )
        dq_ref[rows, :] = dq
    first = pl.program_id(0) == 0
    sums = []
    sides = ((dq_ref, dq_ref, qp_ref, qg_ref), (dk_sum, dk_ref, kp_ref, kg_ref))
    for j, (raw_ref, out_ref, proj_ref, g_ref) in enumerate(sides):
        raw = (raw_ref[...] * scale).astype(BF).astype(F32)
        back = turn(raw, cos_ref[...], -sin_ref[...])
        normed = proj_ref[...] * f_ref[:, j : j + 1]
        gain_ref[j] = jnp.broadcast_to(jnp.sum(back * normed, axis=0, keepdims=True), (8, HD))
        back = back * g_ref[...]
        out_ref[...] = back
        sums.append(feature_sums(back * normed))
    sums = two_rows(*sums)
    for place in range(count):
        part = sums[:, place * tokens : (place + 1) * tokens]
        inner_ref[place] = jnp.where(first, part, inner_ref[place] + part)
    dv_ref[...] = dv_sum[...].astype(BF)


def attend_specs(length, heads):
    head = lambda j: pl.BlockSpec((length, HD), lambda h, me: (0, j * heads + h))
    whole = lambda *shape: pl.BlockSpec(shape, lambda h, me: (0, 0))
    gain = pl.BlockSpec((1, HD), lambda h, me: (0, h))
    return head, whole, gain


def attend(me, qkv, factors, q_gain, k_gain, tables, seg, count):
    length = qkv.shape[0]
    part = qkv.shape[1] // 3
    heads = part // HD
    tokens = length // count
    span = min(count, (length // 2 - 1 + tokens - 1) // tokens + 1)
    head, whole, gain = attend_specs(length, heads)
    low = jax.ShapeDtypeStruct((length, part), BF)
    return pl.pallas_call(
        functools.partial(attend_kernel, tokens, count, span),
        grid_spec=pltpu.PrefetchScalarGridSpec(
            num_scalar_prefetch=1,
            grid=(heads,),
            in_specs=[head(0), head(1), head(2), whole(length, 2), gain, gain]
            + [whole(length, HD)] * 2
            + [whole(length, 1), whole(1, length)],
            out_specs=[head(0)] * 4,
        ),
        out_shape=[low] * 4,
        compiler_params=params(),
        cost_estimate=cost(0, 0),
        name="attend",
    )(me, qkv, qkv, qkv, factors, q_gain[None], k_gain[None], *tables, seg[:, None], seg[None])


def attend_back(me, pieces, query, key, value, qkv, factors, q_gain, k_gain, tables, seg, count):
    length, part = query.shape
    heads = part // HD
    tokens = length // count
    span = min(count, (length // 2 - 1 + tokens - 1) // tokens + 1)
    head, whole, gain = attend_specs(length, heads)
    return pl.pallas_call(
        functools.partial(attend_back_kernel, tokens, count, span),
        grid_spec=pltpu.PrefetchScalarGridSpec(
            num_scalar_prefetch=1,
            grid=(heads,),
            in_specs=[pl.BlockSpec((tokens, HD), lambda h, me: (0, h))] * count
            + [head(0)] * 3
            + [head(0), head(1), whole(length, 2), gain, gain]
            + [whole(length, HD)] * 2
            + [whole(length, 1), whole(1, length)],
            out_specs=[head(0)] * 3
            + [
                pl.BlockSpec((count, 8, tokens), lambda h, me: (0, 0, 0)),
                pl.BlockSpec((2, 8, HD), lambda h, me: (0, 0, h)),
            ],
            scratch_shapes=[pltpu.VMEM((length, HD), F32)] * 2,
        ),
        out_shape=[jax.ShapeDtypeStruct((length, part), t) for t in (F32, F32, BF)]
        + [jax.ShapeDtypeStruct(m, F32) for m in ((count, 8, tokens), (2, 8, part))],
        compiler_params=params(),
        cost_estimate=cost(0, 0),
        name="attend_back",
    )(me, *pieces, query, key, value, qkv, qkv, factors, q_gain[None], k_gain[None], *tables,
      seg[:, None], seg[None])


def residual_back_kernel(
    me_ref, own_ref, a_ref, b_ref, c_ref, e_ref, cot_ref, attn_ref, gain_ref, w_ref, res_ref, d_ref, sum_ref, *outs
):
    step = pl.program_id(0)

    @pl.when(step == 0)
    def _():
        grad = cot_ref[...].astype(F32) + own_ref[...]
        for ref in (a_ref, b_ref, c_ref, e_ref):
            grad = grad + ref[...].astype(F32)
        res_ref[...] = grad
        attn = attn_ref[...]
        factor = inv_rms(attn)
        normed = attn * factor
        sums = jnp.sum(grad * normed, axis=0, keepdims=True)
        sum_ref[...] = jnp.broadcast_to(sums, sum_ref.shape)
        d_ref[...] = rms_back(normed, factor, gain_ref[...], grad).astype(BF)

    piece = nt_dot(d_ref[...], w_ref[...]).astype(BF)
    for p, out in enumerate(outs):

        @pl.when(step == p)
        def _(out=out):
            out[...] = piece


def residual_back(me, own, got, cot, attn_out, gain, w_first, count):
    tokens, width = own.shape
    part = width // count
    piece = pl.BlockSpec((tokens, part), lambda p, me: (0, 0))
    full = once((tokens, width), lambda p, me: (0, 0))
    whole = lambda rows: pl.BlockSpec((rows, width), lambda p, me: (0, 0))
    return pl.pallas_call(
        residual_back_kernel,
        grid_spec=pltpu.PrefetchScalarGridSpec(
            num_scalar_prefetch=1,
            grid=(count,),
            in_specs=[full] * 7
            + [whole(1), pl.BlockSpec((part, width), lambda p, me: ((me[0] + p) % count, 0))],
            out_specs=[whole(tokens), whole(tokens), whole(8)] + [piece] * count,
        ),
        out_shape=[
            jax.ShapeDtypeStruct((tokens, width), F32),
            jax.ShapeDtypeStruct((tokens, width), BF),
            jax.ShapeDtypeStruct((8, width), F32),
        ]
        + [jax.ShapeDtypeStruct((tokens, part), BF)] * count,
        compiler_params=params(),
        cost_estimate=cost(LATE_COST, 0),
        name="residual_back",
    )(me, own, *got, cot, attn_out, gain[None], w_first)


def input_back_kernel(
    part, me_ref, q_ref, k_ref, v_ref, qp_ref, kp_ref, in_ref, f_ref, w_ref, d_ref, ends_ref, *outs
):
    for j, (grad, proj) in enumerate(((q_ref, qp_ref), (k_ref, kp_ref))):
        factor = f_ref[:, j : j + 1]
        normed = proj[...] * factor
        low = ((grad[...] - normed * in_ref[:, j : j + 1]) * factor).astype(BF)
        d_ref[:, j * part : (j + 1) * part] = low
    d_ref[:, 2 * part :] = v_ref[...]
    total = nt_dot(d_ref[...], w_ref[...])
    step = pl.program_id(0)
    for j, out in enumerate(outs):

        @pl.when(step == j)
        def _(out=out):
            out[...] = total.astype(out.dtype)

    @pl.when((step == 0) | ((step == 1) & (me_ref[0] == 0)))
    def _():
        ends_ref[...] = total.astype(BF)


def input_back(me, d_query, d_key, d_v, qkv, inner, factors, w_qkv):
    length, part = d_query.shape
    width = w_qkv.shape[0]
    tokens = length // 4
    place = lambda t: jnp.where(t == 0, 1, jnp.where(t == 1, 3, jnp.where(t == 2, 2, 0)))
    rows = lambda columns, at=0: pl.BlockSpec((tokens, columns), lambda t, me: (place(t), at))
    kinds = (BF, BF, BF, BF, F32)
    return pl.pallas_call(
        functools.partial(input_back_kernel, part),
        grid_spec=pltpu.PrefetchScalarGridSpec(
            num_scalar_prefetch=1,
            grid=(4,),
            in_specs=[rows(part)] * 3
            + [rows(part), rows(part, 1), rows(2), rows(2)]
            + [once((width, 3 * part), lambda t, me: (0, 0))],
            out_specs=[rows(3 * part)]
            + [pl.BlockSpec((tokens, width), lambda t, me: (0, 0))] * len(kinds),
        ),
        out_shape=[jax.ShapeDtypeStruct((length, 3 * part), BF)]
        + [jax.ShapeDtypeStruct((tokens, width), kind) for kind in kinds],
        compiler_params=params(),
        cost_estimate=cost(0, 0),
        name="input_back",
    )(me, d_query, d_key, d_v, qkv, qkv, inner, factors, w_qkv)


def add_up_kernel(*refs):
    total = refs[0][...]
    for ref in refs[1:-1]:
        total = total + ref[...].astype(F32)
    refs[-1][...] = total.astype(BF)


def add_up(parts):
    tokens, width = parts[0].shape
    tile = tokens // 4
    block = pl.BlockSpec((tile, width), lambda i: (i, 0))
    return pl.pallas_call(
        add_up_kernel,
        grid=(4,),
        in_specs=[block] * len(parts),
        out_specs=block,
        out_shape=jax.ShapeDtypeStruct((tokens, width), BF),
        compiler_params=params(),
        cost_estimate=cost(LATE_COST, 0),
        name="add_up",
    )(*parts)


def tn_dot(left, right):
    return lax.dot_general(left, right, (((0,), (0,)), ((), ())), preferred_element_type=F32)


def weight_grad_kernel(lefts, right_ref, out_ref):
    total, at = None, 0
    for left in lefts:
        rows = left.shape[0]
        product = tn_dot(left[...], right_ref[at : at + rows, :])
        total = product if total is None else total + product
        at += rows
    out_ref[...] = total.astype(BF)


def weight_grad(lefts, right, declared=0):
    width = lefts[0].shape[1]
    length, columns = right.shape
    tile, wide = 256, min(columns, 2048)
    return pl.pallas_call(
        lambda *refs: weight_grad_kernel(refs[:-2], *refs[-2:]),
        grid=(columns // wide, width // tile),
        in_specs=[pl.BlockSpec((left.shape[0], tile), lambda j, i: (0, i)) for left in lefts]
        + [pl.BlockSpec((length, wide), lambda j, i: (0, j))],
        out_specs=pl.BlockSpec((tile, wide), lambda j, i: (i, j)),
        out_shape=jax.ShapeDtypeStruct((width, columns), BF),
        compiler_params=params(),
        cost_estimate=cost(declared, 0),
        name="weight_grad",
    )(*lefts, right)


def attn_grad_kernel(count, me_ref, x_ref, d_ref, *refs):
    pieces, parts, out_ref = refs[:count], refs[count : 2 * count], refs[-1]
    columns = d_ref.shape[1]
    out_ref[:, :columns] = tn_dot(x_ref[...], d_ref[...]).astype(BF)
    source = (pl.program_id(0) // (pl.num_programs(0) // count) + count - me_ref[0]) % count
    for p, piece in enumerate(pieces):

        @pl.when(source == p)
        def _(p=p, piece=piece):
            total, tokens = None, parts[0].shape[0]
            for q in range(count):
                rows = slice(q * tokens, (q + 1) * tokens)
                product = tn_dot(piece[rows, :], parts[(q + p) % count][...])
                total = product if total is None else total + product
            out_ref[:, columns:] = total.astype(BF)


def attn_grad(me, x_all, d_qkv, pieces, d_parts):
    count = len(pieces)
    length, width = x_all.shape
    columns, part = d_qkv.shape[1], d_parts[0].shape[1]
    tile = min(256, part)
    per_part = part // tile
    return pl.pallas_call(
        functools.partial(attn_grad_kernel, count),
        grid_spec=pltpu.PrefetchScalarGridSpec(
            num_scalar_prefetch=1,
            grid=(width // tile,),
            in_specs=[
                pl.BlockSpec((length, tile), lambda i, me: (0, i)),
                once((length, columns), lambda i, me: (0, 0)),
            ]
            + [pl.BlockSpec((length, tile), lambda i, me: (0, i % per_part))] * count
            + [once((length // count, part), lambda i, me: (0, 0))] * count,
            out_specs=pl.BlockSpec((tile, columns + part), lambda i, me: (i, 0)),
        ),
        out_shape=jax.ShapeDtypeStruct((width, columns + part), BF),
        compiler_params=params(),
        cost_estimate=cost(SIDE_COST, 0),
        name="attn_grad",
    )(me, x_all, d_qkv, *pieces, *d_parts)


def cost(flops, moved, exps=0):
    return pl.CostEstimate(flops=flops, bytes_accessed=moved, transcendentals=exps)


def params():
    return pltpu.CompilerParams(vmem_limit_bytes=56 << 20)


def once(shape, index):
    return pl.BlockSpec(shape, index, pipeline_mode=pl.Buffered(1))


def nt_dot(left, right):
    return lax.dot_general(left, right, (((1,), (1,)), ((), ())), preferred_element_type=F32)


def feature_sums(values):
    ones = jnp.ones((8, values.shape[1]), BF)
    total = None
    for _ in range(3):
        term = values.astype(BF)
        values = values - term.astype(F32)
        total = nt_dot(ones, term) if total is None else total + nt_dot(ones, term)
    return total


def two_rows(first, second):
    return jnp.where(lax.broadcasted_iota(jnp.int32, first.shape, 0) == 0, first, second)


def qkv_kernel(part, saved, me_ref, *refs):
    chunks, w_ref, (x_ref, qkv_ref, sq_ref) = refs[: -4 - saved], refs[-4 - saved], refs[-3:]
    step, me = pl.program_id(0), me_ref[0]
    at_end = (step == 0) & (me == 3) | (step == 1) & (me == 0) if len(chunks) == 3 else step < 0
    for q in range(2):

        @pl.when((step == q) & jnp.logical_not(at_end))
        def _(q=q):
            x_ref[...] = chunks[q][...]

    @pl.when(at_end)
    def _():
        x_ref[...] = chunks[-1][...]

    qkv = jnp.dot(x_ref[...], w_ref[...], preferred_element_type=F32)
    qkv_ref[...] = qkv
    q, k = (qkv[:, j * part : (j + 1) * part] for j in range(2))
    sq_ref[0] = two_rows(feature_sums(q * q), feature_sums(k * k))


def qkv_project(me, first, chunks, w_qkv, saved=()):
    tokens, width = chunks[0].shape
    columns = w_qkv.shape[1]
    length = 4 * tokens
    place = lambda q: 2 * q + first
    return pl.pallas_call(
        functools.partial(qkv_kernel, columns // 3, len(saved)),
        grid_spec=pltpu.PrefetchScalarGridSpec(
            num_scalar_prefetch=1,
            grid=(2,),
            in_specs=[once((tokens, width), lambda q, me: (0, 0))] * len(chunks)
            + [once((width, columns), lambda q, me: (0, 0))]
            + [pl.BlockSpec(memory_space=pl.ANY)] * len(saved),
            out_specs=[
                pl.BlockSpec((tokens, width), lambda q, me: (place(q), 0)),
                pl.BlockSpec((tokens, columns), lambda q, me: (place(q), 0)),
                pl.BlockSpec((1, 8, tokens), lambda q, me: (place(q), 0, 0)),
            ],
        ),
        out_shape=[
            jax.ShapeDtypeStruct((length, width), BF),
            jax.ShapeDtypeStruct((length, columns), F32),
            jax.ShapeDtypeStruct((4, 8, tokens), F32),
        ],
        input_output_aliases={2 + len(chunks) + j: j for j in range(len(saved))},
        compiler_params=params(),
        cost_estimate=cost(0, 0),
        name="qkv_project",
    )(me, *chunks, w_qkv, *saved)


FF_TILE = 512
LATE_COST = 10**12
SIDE_COST = 10**11


def ff_finish(step, product, acc, me_ref, outs):
    @pl.when(step == 0)
    def _():
        acc[...] = product

    @pl.when(step > 0)
    def _():
        acc[...] += product

    @pl.when(step == pl.num_programs(0) - 1)
    def _():
        tokens = outs[0].shape[0]
        for j, out in enumerate(outs[:2]):
            out[...] = acc[j * tokens : (j + 1) * tokens].astype(out.dtype)
        if len(outs) == 3:
            at = pl.multiple_of(jnp.where(me_ref[0] == 0, tokens, 0), tokens)
            outs[2][...] = acc[pl.ds(at, tokens), :].astype(BF)


def ff_kernel(saved, me_ref, h_ref, wg_ref, wu_ref, wd_ref, *refs):
    gate_ref, up_ref, hid_ref = refs[saved : saved + 3]
    h = h_ref[...]
    gate = jnp.dot(h, wg_ref[...], preferred_element_type=F32)
    up = jnp.dot(h, wu_ref[...], preferred_element_type=F32)
    hidden = (gate * (1.0 / (1.0 + jnp.exp(-gate))) * up).astype(BF)
    gate_ref[...] = gate
    up_ref[...] = up
    hid_ref[...] = hidden
    product = nt_dot(hidden, wd_ref[...])
    ff_finish(pl.program_id(0), product, refs[-1], me_ref, refs[saved + 3 : -1])


def ff_back_kernel(saved, groups, me_ref, *refs):
    d_refs, (wg_ref, wu_ref, wd_ref, gate_ref, up_ref) = refs[:groups], refs[groups : groups + 5]
    refs = refs[groups + 5 :]
    dgu_ref = refs[saved]
    tile = wg_ref.shape[1]
    d_ff = d_refs[0][...] if groups == 1 else jnp.concatenate([d[...] for d in d_refs], axis=0)
    d_hidden = jnp.dot(d_ff, wd_ref[...], preferred_element_type=F32)
    gate = gate_ref[...]
    sig = 1.0 / (1.0 + jnp.exp(-gate))
    d_gate = (d_hidden * up_ref[...] * sig * (1.0 + gate * (1.0 - sig))).astype(BF)
    d_up = (d_hidden * gate * sig).astype(BF)
    dgu_ref[:, :tile] = d_gate
    dgu_ref[:, tile:] = d_up
    product = nt_dot(d_gate, wg_ref[...]) + nt_dot(d_up, wu_ref[...])
    ff_finish(pl.program_id(0), product, refs[-1], me_ref, refs[saved + 1 : -1])


def ff_specs(width, tile, gate_at):
    rest = pl.BlockSpec((width, tile), lambda t: (0, t))
    return [pl.BlockSpec((width, tile), lambda t: (0, gate_at // tile + t)), rest, rest]


def ff_forward(me, residual_all, w_first, w_up, w_down, place, kinds, saved=()):
    length, width = residual_all.shape
    tokens = length // 4
    group = min(len(kinds), 2)
    rows = group * tokens
    ff_part = w_up.shape[1]
    tile = min(FF_TILE, ff_part)
    block = pl.BlockSpec((rows, tile), lambda t: (place // group, t))
    whole = pl.BlockSpec((tokens, width), lambda t: (0, 0))
    shape = lambda kind: jax.ShapeDtypeStruct((length, ff_part), kind)
    return pl.pallas_call(
        functools.partial(ff_kernel, len(saved)),
        grid=(ff_part // tile,),
        in_specs=[pl.BlockSpec(memory_space=pltpu.SMEM)]
        + [once((rows, width), lambda t: (place // group, 0))]
        + ff_specs(width, tile, w_first.shape[1] - ff_part)
        + [pl.BlockSpec(memory_space=pl.ANY)] * len(saved),
        out_specs=[block] * 3 + [whole] * len(kinds),
        out_shape=[shape(F32), shape(F32), shape(BF)]
        + [jax.ShapeDtypeStruct((tokens, width), kind) for kind in kinds],
        scratch_shapes=[pltpu.VMEM((rows, width), F32)],
        input_output_aliases={5 + j: j for j in range(len(saved))},
        compiler_params=params(),
        cost_estimate=cost(0, 0),
        name="ff_forward",
    )(me, residual_all, w_first, w_up, w_down, *saved)


def ff_backward(me, d_ffs, w_first, w_up, w_down, gate, up, place, kinds, saved=()):
    tokens, width = d_ffs[0].shape
    group = len(d_ffs)
    rows = group * tokens
    length = gate.shape[0]
    ff_part = w_up.shape[1]
    tile = min(FF_TILE, ff_part)
    block = pl.BlockSpec((rows, tile), lambda t: (place // group, t))
    whole = pl.BlockSpec((tokens, width), lambda t: (0, 0))
    return pl.pallas_call(
        functools.partial(ff_back_kernel, len(saved), group),
        grid=(ff_part // tile,),
        in_specs=[pl.BlockSpec(memory_space=pltpu.SMEM)]
        + [once((tokens, width), lambda t: (0, 0))] * group
        + ff_specs(width, tile, w_first.shape[1] - ff_part)
        + [block, block]
        + [pl.BlockSpec(memory_space=pl.ANY)] * len(saved),
        out_specs=[pl.BlockSpec((rows, 2 * tile), lambda t: (place // group, t))]
        + [whole] * len(kinds),
        out_shape=[jax.ShapeDtypeStruct((length, 2 * ff_part), BF)]
        + [jax.ShapeDtypeStruct((tokens, width), kind) for kind in kinds],
        scratch_shapes=[pltpu.VMEM((rows, width), F32)],
        input_output_aliases={6 + group + j: j for j in range(len(saved))},
        compiler_params=params(),
        cost_estimate=cost(SIDE_COST, 0),
        name="ff_backward",
    )(me, *d_ffs, w_first, w_up, w_down, gate, up, *saved)


def out_kernel(count, part, *refs):
    me_ref, pieces, (w_ref, x_ref, g_ref, res_ref, own_ref) = refs[0], refs[1:-5], refs[-5:]
    total = None
    for p, piece in enumerate(pieces):
        rows = pl.ds(pl.multiple_of((me_ref[0] + p) % count * part, part), part)
        product = jnp.dot(piece[...], w_ref[rows, :], preferred_element_type=F32)
        total = product if total is None else total + product
    normed = total * inv_rms(total)
    res_ref[...] = (x_ref[...].astype(F32) + normed * g_ref[...]).astype(BF)

    @pl.when(pl.program_id(0) == 0)
    def _():
        own_ref[...] = total


def ff_place(q):
    return jnp.where(q == 0, 3, jnp.where(q == 3, 1, jnp.where(q == 2, 2, 0)))


def out_project(me, pieces, w_out, x_all, gain, count):
    length, width = x_all.shape
    tokens = length // count
    part = pieces[0].shape[1]
    rolled = lambda p: pl.BlockSpec((tokens, part), lambda q, me: ((q + count - p) % count, 0))
    chunk = pl.BlockSpec((tokens, width), lambda q, me: (q, 0))
    moved = pl.BlockSpec((tokens, width), lambda q, me: (ff_place(q), 0))
    return pl.pallas_call(
        functools.partial(out_kernel, count, part),
        grid_spec=pltpu.PrefetchScalarGridSpec(
            num_scalar_prefetch=1,
            grid=(count,),
            in_specs=[rolled(p) for p in range(count)]
            + [pl.BlockSpec((width, width), lambda q, me: (0, 0), pipeline_mode=pl.Buffered(1))]
            + [chunk, pl.BlockSpec((1, width), lambda q, me: (0, 0))],
            out_specs=[moved, pl.BlockSpec((tokens, width), lambda q, me: (0, 0))],
        ),
        out_shape=[
            jax.ShapeDtypeStruct((length, width), BF),
            jax.ShapeDtypeStruct((tokens, width), F32),
        ],
        compiler_params=params(),
        cost_estimate=cost(0, 0),
        name="out_project",
    )(me, *pieces, w_out, x_all, gain[None])


def columns_to_parts(values, me, count):
    part = values.shape[1] // count
    columns = lambda p: lax.dynamic_slice_in_dim(values, (me + p) % count * part, part, 1)
    got = [columns(0)] + [
        lax.ppermute(columns(p), "seq", [(i, (i + p) % count) for i in range(count)])
        for p in range(1, count)
    ]
    return [got[(count - q) % count] for q in range(count)]


def build(dp_count, seq_count):
    assert seq_count == 4

    def shards(
        layer_input,
        segments,
        w_query,
        w_key,
        w_value,
        w_output,
        w_gate,
        w_up,
        w_down,
        query_gain,
        key_gain,
        attn_gain,
        ff_gain,
        cotangent,
    ):
        n = seq_count
        tokens, width = layer_input.shape[1:]
        shard_rows = w_query.shape[0]
        part = width // n
        ff_part = w_gate.shape[1] // n
        length = n * tokens
        devices = dp_count * n
        me = lax.axis_index("seq")
        me_ref = me[None].astype(jnp.int32)
        cot = cotangent[0]
        by_part = lambda w: w.reshape(shard_rows, n, -1).transpose(1, 0, 2)
        rows_of = lambda blocks: blocks.reshape(n * shard_rows, -1)

        fence = lax.optimization_barrier
        qkv_blocks = jnp.concatenate([by_part(w) for w in (w_query, w_key, w_value)], axis=2)
        qkv_blocks = swap_blocks(qkv_blocks)
        w_qkv = gather_dp(rows_of(qkv_blocks))
        natural = jnp.arange(length, dtype=jnp.int32)
        positions = (natural + me * tokens) % length
        seg_row = segments[0]
        seg = lax.dynamic_slice_in_dim(
            jnp.concatenate([seg_row, seg_row]), me * tokens, length, 0
        )
        tables = rope_tables(positions.astype(F32))
        own_gain = lambda g: lax.dynamic_slice_in_dim(g, me * part, part, 0)
        q_gain = own_gain(query_gain)
        k_gain = own_gain(key_gain)

        up_columns, down_columns = (part_columns(w, me, n) for w in (w_up, w_down.T))
        ready = (seg, tables, q_gain, k_gain, up_columns, down_columns)
        qkv_blocks, w_output, w_gate = fence((qkv_blocks, w_output, w_gate))
        out_blocks = gather_cyclic(w_output, n)
        gate_blocks = send_blocks(part_columns(w_gate, me, n))
        out_blocks, gate_blocks, x_own, ready = fence(
            (out_blocks, gate_blocks, layer_input[0], ready)
        )
        seg, tables, q_gain, k_gain, up_columns, down_columns = ready
        out_blocks = out_blocks[:1] + out_blocks[:0:-1]
        w_first = place_blocks(out_blocks, me, 0, width + ff_part)
        w_first = gather_dp(place_blocks(gate_blocks, me, width, width + ff_part, w_first))
        x_own, x_after, x_far, x_before, x_ends = gather_raw(x_own, n)
        saved = qkv_project(me_ref, 0, [x_own, x_far], w_qkv)
        x_sides, saved, up_columns = fence(([x_after, x_before, x_ends], saved, up_columns))
        up_blocks = send_blocks(up_columns)
        x_all, qkv, squares = qkv_project(me_ref, 1, x_sides, w_qkv, saved)
        squares, up_blocks = fence((squares, up_blocks))
        w_up_all = gather_dp(place_blocks(up_blocks, me, 0, ff_part))

        squares = sum_stats(squares, n)
        squares, down_columns = fence((squares, down_columns))
        down_blocks = send_blocks(down_columns)
        factors = lax.rsqrt(stat_columns(squares) / width + EPSILON)
        mixed, q_low, k_low, v_low = attend(me_ref, qkv, factors, q_gain, k_gain, tables, seg, n)

        mixed, down_blocks = fence((mixed, down_blocks))
        w_down_all = gather_dp(place_blocks(down_blocks, me, 0, ff_part))
        pieces = gather_cyclic(mixed, n)
        residual_all, attn_out = out_project(me_ref, pieces, w_first, x_all, attn_gain, n)
        attn_factor = inv_rms(attn_out)
        attn_normed = attn_out * attn_factor
        residual = x_own.astype(F32) + attn_normed * attn_gain

        *saved, far = ff_forward(me_ref, residual_all, w_first, w_up_all, w_down_all, 2, (BF,))
        across = lax.ppermute(far, "seq", [(0, 2), (3, 1)])
        *saved, after, before, ends = ff_forward(
            me_ref, residual_all, w_first, w_up_all, w_down_all, 0, (BF, BF, BF), saved
        )
        after, before, ends, across, residual_late = fence(
            (after, before, ends, across, residual_all)
        )
        sent = scatter_start(ends, after, before, n)
        gate, up, hidden, own = ff_forward(
            me_ref, residual_late, w_first, w_up_all, w_down_all, 3, (F32,), saved
        )
        own, sent[0] = fence((own, sent[0]))
        sent[0] = scatter_far(far, sent[0])
        ff_out = scatter_end(own, sent + [across])
        ff_factor = inv_rms(ff_out)
        ff_normed = ff_out * ff_factor
        activation = (residual + ff_normed * ff_gain).astype(BF)
        grad_ff_gain = jnp.sum(cot.astype(F32) * ff_normed, axis=0)
        d_ff = rms_back(ff_normed, ff_factor, ff_gain, cot.astype(F32)).astype(BF)
        d_ffs = gather_cyclic(d_ff, n)
        d_both, own = ff_backward(me_ref, d_ffs[:1], w_first, w_up_all, w_down_all, gate, up, 3, (F32,))
        d_both, far = ff_backward(
            me_ref, d_ffs[2:3], w_first, w_up_all, w_down_all, gate, up, 2, (BF,), (d_both,)
        )
        d_ffs, d_both, far = fence((d_ffs, d_both, far))
        across = lax.ppermute(far, "seq", [(0, 2), (3, 1)])
        d_both, after, before, ends = ff_backward(
            me_ref, d_ffs[1::2], w_first, w_up_all, w_down_all, gate, up, 0, (BF, BF, BF), (d_both,)
        )
        after, before, ends, across, d_ffs, hidden = fence(
            (after, before, ends, across, d_ffs, hidden)
        )
        ends, *sent = scatter_start(ends, after, before, n)
        down_grad = weight_grad([d_ffs[1], d_ffs[3], d_ffs[2], d_ffs[0]], hidden, SIDE_COST)
        ends, down_grad = fence((ends, down_grad))
        down_rows = scatter_dp(down_grad)
        sent = [scatter_far(far, ends)] + sent
        d_res, d_attn, grad_attn_gain, *d_pieces = residual_back(
            me_ref, own, sent + [across], cot, attn_out, attn_gain, w_first, n
        )
        d_mixed = [d_pieces[0]] + [None] * (n - 1)
        for p in range(1, n):
            d_mixed[n - p] = lax.ppermute(
                d_pieces[p], "seq", [(i, (i + p) % n) for i in range(n)]
            )
        residual_all, d_both, _ = fence((residual_all, d_both, d_pieces[0]))
        gate_up_grad = weight_grad([residual_all], d_both)
        d_mixed, d_attn, gate_up_grad = fence((d_mixed, d_attn, gate_up_grad))
        gate_up_rows = scatter_dp(gate_up_grad)
        d_attn_part = columns_to_parts(d_attn, me, n)
        d_query, d_key, d_v, inner, gain_sums = attend_back(
            me_ref, d_mixed, q_low, k_low, v_low, qkv, factors, q_gain, k_gain, tables, seg, n
        )
        inner, d_attn_part, down_back = fence(
            (inner, d_attn_part, row_blocks(down_rows, me, n))
        )
        inner = sum_stats(inner, n)
        inner, down_back = fence((inner, down_back))
        down_back = send_blocks(down_back)
        d_qkv, ends, after, before, far, own = input_back(
            me_ref, d_query, d_key, d_v, qkv, stat_columns(inner) / width, factors, w_qkv
        )
        d_qkv, ends, after, before, far, own, down_back = fence(
            (d_qkv, ends, after, before, far, own, down_back)
        )
        ends, *sent = scatter_start(ends, after, before, n)
        sent.append(lax.ppermute(far, "seq", [(0, 2), (3, 1)]))
        attn_grads = attn_grad(me_ref, x_all, d_qkv, pieces, d_attn_part)
        ends, attn_grads = fence((ends, attn_grads))
        attn_rows = scatter_dp(attn_grads)
        sent.append(scatter_far(far, ends))
        gate_up_back = row_blocks(gate_up_rows, me, n)
        sent[0], gate_up_back = fence((sent[0], gate_up_back))
        input_grad = add_up([d_res, own] + sent)
        spread = lambda g: lax.dynamic_update_slice(jnp.zeros(width, F32), g, (me * part,))
        gains = jnp.stack(
            [spread(gain_sums[0, 0]), spread(gain_sums[1, 0]), grad_attn_gain[0], grad_ff_gain]
        )
        input_grad, gains = fence((input_grad, gains))
        gate_up_back = send_blocks(gate_up_back)
        gains = sum_everywhere(gains, dp_count, n)
        attn_rows, input_grad, gate_up_back, down_back, gains = fence(
            (attn_rows, input_grad, gate_up_back, down_back, gains)
        )
        attn_back = send_blocks(row_blocks(attn_rows, me, n))
        grad_gate, grad_up = join_columns(me_ref, gate_up_back, 2)
        grad_down = join_columns(me_ref, down_back, 1)[0].T
        attn_back, grad_gate, grad_up, grad_down = fence(
            (attn_back, grad_gate, grad_up, grad_down)
        )
        grad_query, grad_key, grad_value, grad_output = join_columns(me_ref, attn_back, 4)

        share = width // devices
        gains = lax.dynamic_slice_in_dim(
            gains, (lax.axis_index("dp") * n + me) * share, share, 1
        )
        return (
            activation[None],
            input_grad[None],
            grad_query,
            grad_key,
            grad_value,
            grad_output,
            grad_gate,
            grad_up,
            grad_down,
            gains[0],
            gains[1],
            gains[2],
            gains[3],
        )

    return shards


def solution(mesh):
    both = P(("dp", "seq"), None)
    tokens = P("dp", "seq", None)
    columns = P(None, ("dp", "seq"))
    gain = P(("dp", "seq"))
    return jax.shard_map(
        build(mesh.shape["dp"], mesh.shape["seq"]),
        mesh=mesh,
        in_specs=(tokens, P("dp", None)) + (both,) * 6 + (columns,) + (P(),) * 4 + (tokens,),
        out_specs=(tokens, tokens) + (both,) * 6 + (columns,) + (gain,) * 4,
        check_vma=False,
    )
```

```python
import functools

import jax
import jax.numpy as jnp
from jax import lax
from jax.experimental import pallas as pl
from jax.experimental.pallas import tpu as pltpu
from jax.sharding import PartitionSpec as P

HD = 128
EPSILON = 1e-06
ROPE_BASE = 500000.0
MASKED = -1e30
LOG2E = 1.4426950408889634
BF = jnp.bfloat16
F32 = jnp.float32


def inv_rms(values):
    return lax.rsqrt(jnp.mean(values * values, axis=-1, keepdims=True) + EPSILON)


def rms_back(normed, factor, gain, grad):
    scaled = grad * gain
    inner = jnp.mean(scaled * normed, axis=-1, keepdims=True)
    return (scaled - normed * inner) * factor


def rope_tables(positions):
    half_dim = HD // 2
    frequency = jnp.power(F32(ROPE_BASE), -jnp.arange(half_dim, dtype=F32) * (2.0 / HD))
    angles = positions[:, None] * frequency[None, :]
    cosine, sine = jnp.cos(angles), jnp.sin(angles)
    return (jnp.concatenate([cosine, cosine], axis=-1), jnp.concatenate([-sine, sine], axis=-1))


def shift(values, count, step):
    return lax.ppermute(values, "seq", [((i + step) % count, i) for i in range(count)])


def gather_raw(values, count):
    far = lax.ppermute(values, "seq", [(i ^ 2, i) for i in range(count)])
    after = lax.ppermute(values, "seq", [(i + 1, i) for i in range(count - 1)])
    before = lax.ppermute(values, "seq", [(i, i + 1) for i in range(count - 1)])
    ends = lax.ppermute(far, "seq", [(2, 3), (1, 0)])
    return [values, after, far, before, ends]


def gather_cyclic(values, count):
    own, after, far, before, ends = gather_raw(values, count)
    me = lax.axis_index("seq")
    after = jnp.where(me == count - 1, ends, after)
    return [own, after, far, jnp.where(me == 0, ends, before)]


def scatter_start(ends, after, before, count):
    ends = lax.ppermute(ends, "seq", [(0, 1), (count - 1, count - 2)])
    step = [(i, i + 1) for i in range(count - 1)]
    after = lax.ppermute(after, "seq", step)
    before = lax.ppermute(before, "seq", [(j, i) for i, j in step])
    return [ends, after, before]


def scatter_far(far, ends):
    far = (far.astype(F32) + ends.astype(F32)).astype(BF)
    return lax.ppermute(far, "seq", [(1, 3), (2, 0)])


def scatter_end(own, got):
    for part in got:
        own = own + part.astype(F32)
    return own


def sum_stats(stats, count):
    total = stats
    for p in range(1, count):
        total = total + jnp.roll(shift(stats, count, p), p, axis=0)
    return total


def stat_columns(stats):
    return stats[:, :2].transpose(0, 2, 1).reshape(-1, 2)


def sum_everywhere(values, dp_count, seq_count):
    for name, count in (("dp", dp_count), ("seq", seq_count)):
        if count & (count - 1):
            values = lax.psum(values, name)
            continue
        bit = 1
        while bit < count:
            values = values + lax.ppermute(values, name, [(i, i ^ bit) for i in range(count)])
            bit *= 2
    return values


def swap_blocks(values):
    return lax.all_to_all(values, "seq", split_axis=0, concat_axis=0, tiled=True)


def part_columns(values, me, count):
    part = values.shape[1] // count
    return [
        lax.dynamic_slice_in_dim(values, (me + p) % count * part, part, 1) for p in range(count)
    ]


def place_blocks(blocks, me, first, width, total=None):
    count = len(blocks)
    rows = blocks[0].shape[0]
    if total is None:
        total = jnp.zeros((count * rows, width), blocks[0].dtype)
    for p, block in enumerate(blocks):
        total = lax.dynamic_update_slice(total, block, ((me - p) % count * rows, first))
    return total


def row_blocks(values, me, count):
    size = values.shape[0] // count
    return [
        lax.dynamic_slice_in_dim(values, (me + p) % count * size, size, 0) for p in range(count)
    ]


def send_blocks(blocks):
    count = len(blocks)
    return blocks[:1] + [
        lax.ppermute(blocks[p], "seq", [(i, (i + p) % count) for i in range(count)])
        for p in range(1, count)
    ]


def join_kernel(sides, me_ref, *refs):
    blocks, outs = refs[:-sides], refs[-sides:]
    for p, block in enumerate(blocks):

        @pl.when(pl.program_id(0) == p)
        def _(block=block):
            for j, out in enumerate(outs):
                tile = min(FF_TILE, out.shape[1])
                for at in range(0, out.shape[1], tile):
                    first = at * sides + j * tile
                    out[:, at : at + tile] = block[:, first : first + tile].astype(F32)


def join_columns(me, blocks, sides):
    count = len(blocks)
    rows, columns = blocks[0].shape
    part = columns // sides
    out = pl.BlockSpec((rows, part), lambda p, me: (0, (me[0] + count - p) % count))
    return pl.pallas_call(
        functools.partial(join_kernel, sides),
        grid_spec=pltpu.PrefetchScalarGridSpec(
            num_scalar_prefetch=1,
            grid=(count,),
            in_specs=[once((rows, columns), lambda p, me: (0, 0))] * count,
            out_specs=[out] * sides,
        ),
        out_shape=[jax.ShapeDtypeStruct((rows, count * part), F32)] * sides,
        compiler_params=params(),
        cost_estimate=cost(0, 0),
        name="join_columns",
    )(me, *blocks)


def gather_dp(values):
    return lax.all_gather(values, "dp", axis=0, tiled=True)


def scatter_dp(values):
    return lax.psum_scatter(values, "dp", scatter_dimension=0, tiled=True)


def softmax_window(q, k_ref, seg_q, seg_row_ref, valid_from, place, tokens, count, span):
    parts = []
    for w in range(span):
        at = ((place - w) % count) * tokens
        scores = lax.dot_general(
            q, k_ref[at : at + tokens, :], (((1,), (1,)), ((), ())), preferred_element_type=F32
        )
        seg = seg_q if w == 0 else jnp.where(valid_from >= w, seg_q, -1)
        allowed = seg == seg_row_ref[:, at : at + tokens]
        if w == 0:
            rows = lax.broadcasted_iota(jnp.int32, (tokens, tokens), 0)
            cols = lax.broadcasted_iota(jnp.int32, (tokens, tokens), 1)
            allowed = allowed & (cols <= rows)
        parts.append(jnp.where(allowed, scores, MASKED))
    top = parts[0]
    for part in parts[1:]:
        top = jnp.maximum(top, part)
    top = jnp.max(top, axis=-1, keepdims=True)
    exps = [jnp.exp2((part - top) * (HD**-0.5 * LOG2E)) for part in parts]
    total = exps[0]
    for part in exps[1:]:
        total = total + part
    inverse = 1.0 / jnp.sum(total, axis=-1, keepdims=True)
    return [part * inverse for part in exps]


def turn(values, cosine, sine):
    return values * cosine + pltpu.roll(values, HD // 2, 1) * sine


def attend_kernel(
    tokens, count, span,
    me_ref, q_ref, k_ref, v_ref, f_ref, qg_ref, kg_ref, cos_ref, sin_ref, segc_ref, segr_ref,
    o_ref, qb_ref, kb_ref, vb_ref,
):
    cosine, sine = cos_ref[...], sin_ref[...]
    factors = f_ref[...]
    qb_ref[...] = turn(q_ref[...] * factors[:, 0:1] * qg_ref[...], cosine, sine).astype(BF)
    kb_ref[...] = turn(k_ref[...] * factors[:, 1:2] * kg_ref[...], cosine, sine).astype(BF)
    vb_ref[...] = v_ref[...].astype(BF)
    for place in range(count):
        rows = slice(place * tokens, (place + 1) * tokens)
        chunk = (me_ref[0] + place) % count
        probs = softmax_window(
            qb_ref[rows, :], kb_ref, segc_ref[rows, :], segr_ref, chunk, place, tokens, count, span
        )
        mixed = None
        for w in range(span):
            at = ((place - w) % count) * tokens
            part = jnp.dot(probs[w].astype(BF), vb_ref[at : at + tokens, :], preferred_element_type=F32)
            mixed = part if mixed is None else mixed + part
        o_ref[rows, :] = mixed.astype(BF)


def attend_back_kernel(
    tokens, count, span, me_ref, *refs
):
    grads_in = refs[:count]
    (q_ref, k_ref, v_ref, qp_ref, kp_ref, f_ref, qg_ref, kg_ref, cos_ref, sin_ref, segc_ref, segr_ref,
     dq_ref, dk_ref, dv_ref, inner_ref, gain_ref, dk_sum, dv_sum) = refs[count:]
    scale = HD**-0.5
    dk_sum[...] = jnp.zeros_like(dk_sum)
    dv_sum[...] = jnp.zeros_like(dv_sum)
    for place in range(count):
        rows = slice(place * tokens, (place + 1) * tokens)
        chunk = (me_ref[0] + place) % count
        q = q_ref[rows, :]
        grad = grads_in[place][...]
        probs = softmax_window(
            q, k_ref, segc_ref[rows, :], segr_ref, chunk, place, tokens, count, span
        )
        grads = []
        inner = None
        for w in range(span):
            at = ((place - w) % count) * tokens
            part = nt_dot(grad, v_ref[at : at + tokens, :])
            grads.append(part)
            inner = probs[w] * part if inner is None else inner + probs[w] * part
            dv_sum[at : at + tokens, :] += lax.dot_general(
                probs[w].astype(BF), grad, (((0,), (0,)), ((), ())), preferred_element_type=F32
            )
        inner = jnp.sum(inner, axis=-1, keepdims=True)
        dq = None
        for w in range(span):
            at = ((place - w) % count) * tokens
            ds = (probs[w] * (grads[w] - inner)).astype(BF)
            part = jnp.dot(ds, k_ref[at : at + tokens, :], preferred_element_type=F32)
            dq = part if dq is None else dq + part
            dk_sum[at : at + tokens, :] += lax.dot_general(
                ds, q, (((0,), (0,)), ((), ())), preferred_element_type=F32
            )
        dq_ref[rows, :] = dq
    first = pl.program_id(0) == 0
    sums = []
    sides = ((dq_ref, dq_ref, qp_ref, qg_ref), (dk_sum, dk_ref, kp_ref, kg_ref))
    for j, (raw_ref, out_ref, proj_ref, g_ref) in enumerate(sides):
        raw = (raw_ref[...] * scale).astype(BF).astype(F32)
        back = turn(raw, cos_ref[...], -sin_ref[...])
        normed = proj_ref[...] * f_ref[:, j : j + 1]
        gain_ref[j] = jnp.broadcast_to(jnp.sum(back * normed, axis=0, keepdims=True), (8, HD))
        back = back * g_ref[...]
        out_ref[...] = back
        sums.append(feature_sums(back * normed))
    sums = two_rows(*sums)
    for place in range(count):
        part = sums[:, place * tokens : (place + 1) * tokens]
        inner_ref[place] = jnp.where(first, part, inner_ref[place] + part)
    dv_ref[...] = dv_sum[...].astype(BF)


def attend_specs(length, heads):
    head = lambda j: pl.BlockSpec((length, HD), lambda h, me: (0, j * heads + h))
    whole = lambda *shape: pl.BlockSpec(shape, lambda h, me: (0, 0))
    gain = pl.BlockSpec((1, HD), lambda h, me: (0, h))
    return head, whole, gain


def attend(me, qkv, factors, q_gain, k_gain, tables, seg, count):
    length = qkv.shape[0]
    part = qkv.shape[1] // 3
    heads = part // HD
    tokens = length // count
    span = min(count, (length // 2 - 1 + tokens - 1) // tokens + 1)
    head, whole, gain = attend_specs(length, heads)
    low = jax.ShapeDtypeStruct((length, part), BF)
    return pl.pallas_call(
        functools.partial(attend_kernel, tokens, count, span),
        grid_spec=pltpu.PrefetchScalarGridSpec(
            num_scalar_prefetch=1,
            grid=(heads,),
            in_specs=[head(0), head(1), head(2), whole(length, 2), gain, gain]
            + [whole(length, HD)] * 2
            + [whole(length, 1), whole(1, length)],
            out_specs=[head(0)] * 4,
        ),
        out_shape=[low] * 4,
        compiler_params=params(),
        cost_estimate=cost(0, 0),
        name="attend",
    )(me, qkv, qkv, qkv, factors, q_gain[None], k_gain[None], *tables, seg[:, None], seg[None])


def attend_back(me, pieces, query, key, value, qkv, factors, q_gain, k_gain, tables, seg, count):
    length, part = query.shape
    heads = part // HD
    tokens = length // count
    span = min(count, (length // 2 - 1 + tokens - 1) // tokens + 1)
    head, whole, gain = attend_specs(length, heads)
    return pl.pallas_call(
        functools.partial(attend_back_kernel, tokens, count, span),
        grid_spec=pltpu.PrefetchScalarGridSpec(
            num_scalar_prefetch=1,
            grid=(heads,),
            in_specs=[pl.BlockSpec((tokens, HD), lambda h, me: (0, h))] * count
            + [head(0)] * 3
            + [head(0), head(1), whole(length, 2), gain, gain]
            + [whole(length, HD)] * 2
            + [whole(length, 1), whole(1, length)],
            out_specs=[head(0)] * 3
            + [
                pl.BlockSpec((count, 8, tokens), lambda h, me: (0, 0, 0)),
                pl.BlockSpec((2, 8, HD), lambda h, me: (0, 0, h)),
            ],
            scratch_shapes=[pltpu.VMEM((length, HD), F32)] * 2,
        ),
        out_shape=[jax.ShapeDtypeStruct((length, part), t) for t in (F32, F32, BF)]
        + [jax.ShapeDtypeStruct(m, F32) for m in ((count, 8, tokens), (2, 8, part))],
        compiler_params=params(),
        cost_estimate=cost(0, 0),
        name="attend_back",
    )(me, *pieces, query, key, value, qkv, qkv, factors, q_gain[None], k_gain[None], *tables,
      seg[:, None], seg[None])


def residual_back_kernel(
    me_ref, own_ref, a_ref, b_ref, c_ref, e_ref, cot_ref, attn_ref, gain_ref, w_ref, res_ref, d_ref, sum_ref, *outs
):
    step = pl.program_id(0)

    @pl.when(step == 0)
    def _():
        grad = cot_ref[...].astype(F32) + own_ref[...]
        for ref in (a_ref, b_ref, c_ref, e_ref):
            grad = grad + ref[...].astype(F32)
        res_ref[...] = grad
        attn = attn_ref[...]
        factor = inv_rms(attn)
        normed = attn * factor
        sums = jnp.sum(grad * normed, axis=0, keepdims=True)
        sum_ref[...] = jnp.broadcast_to(sums, sum_ref.shape)
        d_ref[...] = rms_back(normed, factor, gain_ref[...], grad).astype(BF)

    piece = nt_dot(d_ref[...], w_ref[...]).astype(BF)
    for p, out in enumerate(outs):

        @pl.when(step == p)
        def _(out=out):
            out[...] = piece


def residual_back(me, own, got, cot, attn_out, gain, w_first, count):
    tokens, width = own.shape
    part = width // count
    piece = pl.BlockSpec((tokens, part), lambda p, me: (0, 0))
    full = once((tokens, width), lambda p, me: (0, 0))
    whole = lambda rows: pl.BlockSpec((rows, width), lambda p, me: (0, 0))
    return pl.pallas_call(
        residual_back_kernel,
        grid_spec=pltpu.PrefetchScalarGridSpec(
            num_scalar_prefetch=1,
            grid=(count,),
            in_specs=[full] * 7
            + [whole(1), pl.BlockSpec((part, width), lambda p, me: ((me[0] + p) % count, 0))],
            out_specs=[whole(tokens), whole(tokens), whole(8)] + [piece] * count,
        ),
        out_shape=[
            jax.ShapeDtypeStruct((tokens, width), F32),
            jax.ShapeDtypeStruct((tokens, width), BF),
            jax.ShapeDtypeStruct((8, width), F32),
        ]
        + [jax.ShapeDtypeStruct((tokens, part), BF)] * count,
        compiler_params=params(),
        cost_estimate=cost(LATE_COST, 0),
        name="residual_back",
    )(me, own, *got, cot, attn_out, gain[None], w_first)


def input_back_kernel(
    part, me_ref, q_ref, k_ref, v_ref, qp_ref, kp_ref, in_ref, f_ref, w_ref, d_ref, ends_ref, *outs
):
    for j, (grad, proj) in enumerate(((q_ref, qp_ref), (k_ref, kp_ref))):
        factor = f_ref[:, j : j + 1]
        normed = proj[...] * factor
        low = ((grad[...] - normed * in_ref[:, j : j + 1]) * factor).astype(BF)
        d_ref[:, j * part : (j + 1) * part] = low
    d_ref[:, 2 * part :] = v_ref[...]
    total = nt_dot(d_ref[...], w_ref[...])
    step = pl.program_id(0)
    for j, out in enumerate(outs):

        @pl.when(step == j)
        def _(out=out):
            out[...] = total.astype(out.dtype)

    @pl.when((step == 0) | ((step == 1) & (me_ref[0] == 0)))
    def _():
        ends_ref[...] = total.astype(BF)


def input_back(me, d_query, d_key, d_v, qkv, inner, factors, w_qkv):
    length, part = d_query.shape
    width = w_qkv.shape[0]
    tokens = length // 4
    place = lambda t: jnp.where(t == 0, 1, jnp.where(t == 1, 3, jnp.where(t == 2, 2, 0)))
    rows = lambda columns, at=0: pl.BlockSpec((tokens, columns), lambda t, me: (place(t), at))
    kinds = (BF, BF, BF, BF, F32)
    return pl.pallas_call(
        functools.partial(input_back_kernel, part),
        grid_spec=pltpu.PrefetchScalarGridSpec(
            num_scalar_prefetch=1,
            grid=(4,),
            in_specs=[rows(part)] * 3
            + [rows(part), rows(part, 1), rows(2), rows(2)]
            + [once((width, 3 * part), lambda t, me: (0, 0))],
            out_specs=[rows(3 * part)]
            + [pl.BlockSpec((tokens, width), lambda t, me: (0, 0))] * len(kinds),
        ),
        out_shape=[jax.ShapeDtypeStruct((length, 3 * part), BF)]
        + [jax.ShapeDtypeStruct((tokens, width), kind) for kind in kinds],
        compiler_params=params(),
        cost_estimate=cost(0, 0),
        name="input_back",
    )(me, d_query, d_key, d_v, qkv, qkv, inner, factors, w_qkv)


def add_up_kernel(*refs):
    total = refs[0][...]
    for ref in refs[1:-1]:
        total = total + ref[...].astype(F32)
    refs[-1][...] = total.astype(BF)


def add_up(parts):
    tokens, width = parts[0].shape
    tile = tokens // 4
    block = pl.BlockSpec((tile, width), lambda i: (i, 0))
    return pl.pallas_call(
        add_up_kernel,
        grid=(4,),
        in_specs=[block] * len(parts),
        out_specs=block,
        out_shape=jax.ShapeDtypeStruct((tokens, width), BF),
        compiler_params=params(),
        cost_estimate=cost(LATE_COST, 0),
        name="add_up",
    )(*parts)


def tn_dot(left, right):
    return lax.dot_general(left, right, (((0,), (0,)), ((), ())), preferred_element_type=F32)


def weight_grad_kernel(lefts, right_ref, out_ref):
    total, at = None, 0
    for left in lefts:
        rows = left.shape[0]
        product = tn_dot(left[...], right_ref[at : at + rows, :])
        total = product if total is None else total + product
        at += rows
    out_ref[...] = total.astype(BF)


def weight_grad(lefts, right, declared=0):
    width = lefts[0].shape[1]
    length, columns = right.shape
    tile, wide = 256, min(columns, 2048)
    return pl.pallas_call(
        lambda *refs: weight_grad_kernel(refs[:-2], *refs[-2:]),
        grid=(columns // wide, width // tile),
        in_specs=[pl.BlockSpec((left.shape[0], tile), lambda j, i: (0, i)) for left in lefts]
        + [pl.BlockSpec((length, wide), lambda j, i: (0, j))],
        out_specs=pl.BlockSpec((tile, wide), lambda j, i: (i, j)),
        out_shape=jax.ShapeDtypeStruct((width, columns), BF),
        compiler_params=params(),
        cost_estimate=cost(declared, 0),
        name="weight_grad",
    )(*lefts, right)


def attn_grad_kernel(count, me_ref, x_ref, d_ref, *refs):
    pieces, parts, out_ref = refs[:count], refs[count : 2 * count], refs[-1]
    columns = d_ref.shape[1]
    out_ref[:, :columns] = tn_dot(x_ref[...], d_ref[...]).astype(BF)
    source = (pl.program_id(0) // (pl.num_programs(0) // count) + count - me_ref[0]) % count
    for p, piece in enumerate(pieces):

        @pl.when(source == p)
        def _(p=p, piece=piece):
            total, tokens = None, parts[0].shape[0]
            for q in range(count):
                rows = slice(q * tokens, (q + 1) * tokens)
                product = tn_dot(piece[rows, :], parts[(q + p) % count][...])
                total = product if total is None else total + product
            out_ref[:, columns:] = total.astype(BF)


def attn_grad(me, x_all, d_qkv, pieces, d_parts):
    count = len(pieces)
    length, width = x_all.shape
    columns, part = d_qkv.shape[1], d_parts[0].shape[1]
    tile = min(256, part)
    per_part = part // tile
    return pl.pallas_call(
        functools.partial(attn_grad_kernel, count),
        grid_spec=pltpu.PrefetchScalarGridSpec(
            num_scalar_prefetch=1,
            grid=(width // tile,),
            in_specs=[
                pl.BlockSpec((length, tile), lambda i, me: (0, i)),
                once((length, columns), lambda i, me: (0, 0)),
            ]
            + [pl.BlockSpec((length, tile), lambda i, me: (0, i % per_part))] * count
            + [once((length // count, part), lambda i, me: (0, 0))] * count,
            out_specs=pl.BlockSpec((tile, columns + part), lambda i, me: (i, 0)),
        ),
        out_shape=jax.ShapeDtypeStruct((width, columns + part), BF),
        compiler_params=params(),
        cost_estimate=cost(SIDE_COST, 0),
        name="attn_grad",
    )(me, x_all, d_qkv, *pieces, *d_parts)


def cost(flops, moved, exps=0):
    return pl.CostEstimate(flops=flops, bytes_accessed=moved, transcendentals=exps)


def params():
    return pltpu.CompilerParams(vmem_limit_bytes=56 << 20)


def once(shape, index):
    return pl.BlockSpec(shape, index, pipeline_mode=pl.Buffered(1))


def nt_dot(left, right):
    return lax.dot_general(left, right, (((1,), (1,)), ((), ())), preferred_element_type=F32)


def feature_sums(values):
    ones = jnp.ones((8, values.shape[1]), BF)
    total = None
    for _ in range(3):
        term = values.astype(BF)
        values = values - term.astype(F32)
        total = nt_dot(ones, term) if total is None else total + nt_dot(ones, term)
    return total


def two_rows(first, second):
    return jnp.where(lax.broadcasted_iota(jnp.int32, first.shape, 0) == 0, first, second)


def qkv_kernel(part, saved, me_ref, *refs):
    chunks, w_ref, (x_ref, qkv_ref, sq_ref) = refs[: -4 - saved], refs[-4 - saved], refs[-3:]
    step, me = pl.program_id(0), me_ref[0]
    at_end = (step == 0) & (me == 3) | (step == 1) & (me == 0) if len(chunks) == 3 else step < 0
    for q in range(2):

        @pl.when((step == q) & jnp.logical_not(at_end))
        def _(q=q):
            x_ref[...] = chunks[q][...]

    @pl.when(at_end)
    def _():
        x_ref[...] = chunks[-1][...]

    qkv = jnp.dot(x_ref[...], w_ref[...], preferred_element_type=F32)
    qkv_ref[...] = qkv
    q, k = (qkv[:, j * part : (j + 1) * part] for j in range(2))
    sq_ref[0] = two_rows(feature_sums(q * q), feature_sums(k * k))


def qkv_project(me, first, chunks, w_qkv, saved=()):
    tokens, width = chunks[0].shape
    columns = w_qkv.shape[1]
    length = 4 * tokens
    place = lambda q: 2 * q + first
    return pl.pallas_call(
        functools.partial(qkv_kernel, columns // 3, len(saved)),
        grid_spec=pltpu.PrefetchScalarGridSpec(
            num_scalar_prefetch=1,
            grid=(2,),
            in_specs=[once((tokens, width), lambda q, me: (0, 0))] * len(chunks)
            + [once((width, columns), lambda q, me: (0, 0))]
            + [pl.BlockSpec(memory_space=pl.ANY)] * len(saved),
            out_specs=[
                pl.BlockSpec((tokens, width), lambda q, me: (place(q), 0)),
                pl.BlockSpec((tokens, columns), lambda q, me: (place(q), 0)),
                pl.BlockSpec((1, 8, tokens), lambda q, me: (place(q), 0, 0)),
            ],
        ),
        out_shape=[
            jax.ShapeDtypeStruct((length, width), BF),
            jax.ShapeDtypeStruct((length, columns), F32),
            jax.ShapeDtypeStruct((4, 8, tokens), F32),
        ],
        input_output_aliases={2 + len(chunks) + j: j for j in range(len(saved))},
        compiler_params=params(),
        cost_estimate=cost(0, 0),
        name="qkv_project",
    )(me, *chunks, w_qkv, *saved)


FF_TILE = 512
LATE_COST = 10**12
SIDE_COST = 10**11


def ff_finish(step, product, acc, me_ref, outs):
    @pl.when(step == 0)
    def _():
        acc[...] = product

    @pl.when(step > 0)
    def _():
        acc[...] += product

    @pl.when(step == pl.num_programs(0) - 1)
    def _():
        tokens = outs[0].shape[0]
        for j, out in enumerate(outs[:2]):
            out[...] = acc[j * tokens : (j + 1) * tokens].astype(out.dtype)
        if len(outs) == 3:
            at = pl.multiple_of(jnp.where(me_ref[0] == 0, tokens, 0), tokens)
            outs[2][...] = acc[pl.ds(at, tokens), :].astype(BF)


def ff_kernel(saved, me_ref, h_ref, wg_ref, wu_ref, wd_ref, *refs):
    gate_ref, up_ref, hid_ref = refs[saved : saved + 3]
    h = h_ref[...]
    gate = jnp.dot(h, wg_ref[...], preferred_element_type=F32)
    up = jnp.dot(h, wu_ref[...], preferred_element_type=F32)
    hidden = (gate * (1.0 / (1.0 + jnp.exp(-gate))) * up).astype(BF)
    gate_ref[...] = gate
    up_ref[...] = up
    hid_ref[...] = hidden
    product = nt_dot(hidden, wd_ref[...])
    ff_finish(pl.program_id(0), product, refs[-1], me_ref, refs[saved + 3 : -1])


def ff_back_kernel(saved, groups, me_ref, *refs):
    d_refs, (wg_ref, wu_ref, wd_ref, gate_ref, up_ref) = refs[:groups], refs[groups : groups + 5]
    refs = refs[groups + 5 :]
    dgu_ref = refs[saved]
    tile = wg_ref.shape[1]
    d_ff = d_refs[0][...] if groups == 1 else jnp.concatenate([d[...] for d in d_refs], axis=0)
    d_hidden = jnp.dot(d_ff, wd_ref[...], preferred_element_type=F32)
    gate = gate_ref[...]
    sig = 1.0 / (1.0 + jnp.exp(-gate))
    d_gate = (d_hidden * up_ref[...] * sig * (1.0 + gate * (1.0 - sig))).astype(BF)
    d_up = (d_hidden * gate * sig).astype(BF)
    dgu_ref[:, :tile] = d_gate
    dgu_ref[:, tile:] = d_up
    product = nt_dot(d_gate, wg_ref[...]) + nt_dot(d_up, wu_ref[...])
    ff_finish(pl.program_id(0), product, refs[-1], me_ref, refs[saved + 1 : -1])


def ff_specs(width, tile, gate_at):
    rest = pl.BlockSpec((width, tile), lambda t: (0, t))
    return [pl.BlockSpec((width, tile), lambda t: (0, gate_at // tile + t)), rest, rest]


def ff_forward(me, residual_all, w_first, w_up, w_down, place, kinds, saved=()):
    length, width = residual_all.shape
    tokens = length // 4
    group = min(len(kinds), 2)
    rows = group * tokens
    ff_part = w_up.shape[1]
    tile = min(FF_TILE, ff_part)
    block = pl.BlockSpec((rows, tile), lambda t: (place // group, t))
    whole = pl.BlockSpec((tokens, width), lambda t: (0, 0))
    shape = lambda kind: jax.ShapeDtypeStruct((length, ff_part), kind)
    return pl.pallas_call(
        functools.partial(ff_kernel, len(saved)),
        grid=(ff_part // tile,),
        in_specs=[pl.BlockSpec(memory_space=pltpu.SMEM)]
        + [once((rows, width), lambda t: (place // group, 0))]
        + ff_specs(width, tile, w_first.shape[1] - ff_part)
        + [pl.BlockSpec(memory_space=pl.ANY)] * len(saved),
        out_specs=[block] * 3 + [whole] * len(kinds),
        out_shape=[shape(F32), shape(F32), shape(BF)]
        + [jax.ShapeDtypeStruct((tokens, width), kind) for kind in kinds],
        scratch_shapes=[pltpu.VMEM((rows, width), F32)],
        input_output_aliases={5 + j: j for j in range(len(saved))},
        compiler_params=params(),
        cost_estimate=cost(0, 0),
        name="ff_forward",
    )(me, residual_all, w_first, w_up, w_down, *saved)


def ff_backward(me, d_ffs, w_first, w_up, w_down, gate, up, place, kinds, saved=()):
    tokens, width = d_ffs[0].shape
    group = len(d_ffs)
    rows = group * tokens
    length = gate.shape[0]
    ff_part = w_up.shape[1]
    tile = min(FF_TILE, ff_part)
    block = pl.BlockSpec((rows, tile), lambda t: (place // group, t))
    whole = pl.BlockSpec((tokens, width), lambda t: (0, 0))
    return pl.pallas_call(
        functools.partial(ff_back_kernel, len(saved), group),
        grid=(ff_part // tile,),
        in_specs=[pl.BlockSpec(memory_space=pltpu.SMEM)]
        + [once((tokens, width), lambda t: (0, 0))] * group
        + ff_specs(width, tile, w_first.shape[1] - ff_part)
        + [block, block]
        + [pl.BlockSpec(memory_space=pl.ANY)] * len(saved),
        out_specs=[pl.BlockSpec((rows, 2 * tile), lambda t: (place // group, t))]
        + [whole] * len(kinds),
        out_shape=[jax.ShapeDtypeStruct((length, 2 * ff_part), BF)]
        + [jax.ShapeDtypeStruct((tokens, width), kind) for kind in kinds],
        scratch_shapes=[pltpu.VMEM((rows, width), F32)],
        input_output_aliases={6 + group + j: j for j in range(len(saved))},
        compiler_params=params(),
        cost_estimate=cost(SIDE_COST, 0),
        name="ff_backward",
    )(me, *d_ffs, w_first, w_up, w_down, gate, up, *saved)


def out_kernel(count, part, *refs):
    me_ref, pieces, (w_ref, x_ref, g_ref, res_ref, own_ref) = refs[0], refs[1:-5], refs[-5:]
    total = None
    for p, piece in enumerate(pieces):
        rows = pl.ds(pl.multiple_of((me_ref[0] + p) % count * part, part), part)
        product = jnp.dot(piece[...], w_ref[rows, :], preferred_element_type=F32)
        total = product if total is None else total + product
    normed = total * inv_rms(total)
    res_ref[...] = (x_ref[...].astype(F32) + normed * g_ref[...]).astype(BF)

    @pl.when(pl.program_id(0) == 0)
    def _():
        own_ref[...] = total


def ff_place(q):
    return jnp.where(q == 0, 3, jnp.where(q == 3, 1, jnp.where(q == 2, 2, 0)))


def out_project(me, pieces, w_out, x_all, gain, count):
    length, width = x_all.shape
    tokens = length // count
    part = pieces[0].shape[1]
    rolled = lambda p: pl.BlockSpec((tokens, part), lambda q, me: ((q + count - p) % count, 0))
    chunk = pl.BlockSpec((tokens, width), lambda q, me: (q, 0))
    moved = pl.BlockSpec((tokens, width), lambda q, me: (ff_place(q), 0))
    return pl.pallas_call(
        functools.partial(out_kernel, count, part),
        grid_spec=pltpu.PrefetchScalarGridSpec(
            num_scalar_prefetch=1,
            grid=(count,),
            in_specs=[rolled(p) for p in range(count)]
            + [pl.BlockSpec((width, width), lambda q, me: (0, 0), pipeline_mode=pl.Buffered(1))]
            + [chunk, pl.BlockSpec((1, width), lambda q, me: (0, 0))],
            out_specs=[moved, pl.BlockSpec((tokens, width), lambda q, me: (0, 0))],
        ),
        out_shape=[
            jax.ShapeDtypeStruct((length, width), BF),
            jax.ShapeDtypeStruct((tokens, width), F32),
        ],
        compiler_params=params(),
        cost_estimate=cost(0, 0),
        name="out_project",
    )(me, *pieces, w_out, x_all, gain[None])


def columns_to_parts(values, me, count):
    part = values.shape[1] // count
    columns = lambda p: lax.dynamic_slice_in_dim(values, (me + p) % count * part, part, 1)
    got = [columns(0)] + [
        lax.ppermute(columns(p), "seq", [(i, (i + p) % count) for i in range(count)])
        for p in range(1, count)
    ]
    return [got[(count - q) % count] for q in range(count)]


def build(dp_count, seq_count):
    assert seq_count == 4

    def shards(
        layer_input,
        segments,
        w_query,
        w_key,
        w_value,
        w_output,
        w_gate,
        w_up,
        w_down,
        query_gain,
        key_gain,
        attn_gain,
        ff_gain,
        cotangent,
    ):
        n = seq_count
        tokens, width = layer_input.shape[1:]
        shard_rows = w_query.shape[0]
        part = width // n
        ff_part = w_gate.shape[1] // n
        length = n * tokens
        devices = dp_count * n
        me = lax.axis_index("seq")
        me_ref = me[None].astype(jnp.int32)
        cot = cotangent[0]
        by_part = lambda w: w.reshape(shard_rows, n, -1).transpose(1, 0, 2)
        rows_of = lambda blocks: blocks.reshape(n * shard_rows, -1)

        fence = lax.optimization_barrier
        qkv_blocks = jnp.concatenate([by_part(w) for w in (w_query, w_key, w_value)], axis=2)
        qkv_blocks = swap_blocks(qkv_blocks)
        w_qkv = gather_dp(rows_of(qkv_blocks))
        natural = jnp.arange(length, dtype=jnp.int32)
        positions = (natural + me * tokens) % length
        seg_row = segments[0]
        seg = lax.dynamic_slice_in_dim(
            jnp.concatenate([seg_row, seg_row]), me * tokens, length, 0
        )
        tables = rope_tables(positions.astype(F32))
        own_gain = lambda g: lax.dynamic_slice_in_dim(g, me * part, part, 0)
        q_gain = own_gain(query_gain)
        k_gain = own_gain(key_gain)

        up_columns, down_columns = (part_columns(w, me, n) for w in (w_up, w_down.T))
        ready = (seg, tables, q_gain, k_gain, up_columns, down_columns)
        qkv_blocks, w_output, w_gate = fence((qkv_blocks, w_output, w_gate))
        out_blocks = gather_cyclic(w_output, n)
        gate_blocks = send_blocks(part_columns(w_gate, me, n))
        out_blocks, gate_blocks, x_own, ready = fence(
            (out_blocks, gate_blocks, layer_input[0], ready)
        )
        seg, tables, q_gain, k_gain, up_columns, down_columns = ready
        out_blocks = out_blocks[:1] + out_blocks[:0:-1]
        w_first = place_blocks(out_blocks, me, 0, width + ff_part)
        w_first = gather_dp(place_blocks(gate_blocks, me, width, width + ff_part, w_first))
        x_own, x_after, x_far, x_before, x_ends = gather_raw(x_own, n)
        saved = qkv_project(me_ref, 0, [x_own, x_far], w_qkv)
        x_sides, saved, up_columns = fence(([x_after, x_before, x_ends], saved, up_columns))
        up_blocks = send_blocks(up_columns)
        x_all, qkv, squares = qkv_project(me_ref, 1, x_sides, w_qkv, saved)
        squares, up_blocks = fence((squares, up_blocks))
        w_up_all = gather_dp(place_blocks(up_blocks, me, 0, ff_part))

        squares = sum_stats(squares, n)
        squares, down_columns = fence((squares, down_columns))
        down_blocks = send_blocks(down_columns)
        factors = lax.rsqrt(stat_columns(squares) / width + EPSILON)
        mixed, q_low, k_low, v_low = attend(me_ref, qkv, factors, q_gain, k_gain, tables, seg, n)

        mixed, down_blocks = fence((mixed, down_blocks))
        w_down_all = gather_dp(place_blocks(down_blocks, me, 0, ff_part))
        pieces = gather_cyclic(mixed, n)
        residual_all, attn_out = out_project(me_ref, pieces, w_first, x_all, attn_gain, n)
        attn_factor = inv_rms(attn_out)
        attn_normed = attn_out * attn_factor
        residual = x_own.astype(F32) + attn_normed * attn_gain

        *saved, far = ff_forward(me_ref, residual_all, w_first, w_up_all, w_down_all, 2, (BF,))
        across = lax.ppermute(far, "seq", [(0, 2), (3, 1)])
        *saved, after, before, ends = ff_forward(
            me_ref, residual_all, w_first, w_up_all, w_down_all, 0, (BF, BF, BF), saved
        )
        after, before, ends, across, residual_late = fence(
            (after, before, ends, across, residual_all)
        )
        sent = scatter_start(ends, after, before, n)
        gate, up, hidden, own = ff_forward(
            me_ref, residual_late, w_first, w_up_all, w_down_all, 3, (F32,), saved
        )
        own, sent[0] = fence((own, sent[0]))
        sent[0] = scatter_far(far, sent[0])
        ff_out = scatter_end(own, sent + [across])
        ff_factor = inv_rms(ff_out)
        ff_normed = ff_out * ff_factor
        activation = (residual + ff_normed * ff_gain).astype(BF)
        grad_ff_gain = jnp.sum(cot.astype(F32) * ff_normed, axis=0)
        d_ff = rms_back(ff_normed, ff_factor, ff_gain, cot.astype(F32)).astype(BF)
        d_ffs = gather_cyclic(d_ff, n)
        d_both, own = ff_backward(me_ref, d_ffs[:1], w_first, w_up_all, w_down_all, gate, up, 3, (F32,))
        d_both, far = ff_backward(
            me_ref, d_ffs[2:3], w_first, w_up_all, w_down_all, gate, up, 2, (BF,), (d_both,)
        )
        d_ffs, d_both, far = fence((d_ffs, d_both, far))
        across = lax.ppermute(far, "seq", [(0, 2), (3, 1)])
        d_both, after, before, ends = ff_backward(
            me_ref, d_ffs[1::2], w_first, w_up_all, w_down_all, gate, up, 0, (BF, BF, BF), (d_both,)
        )
        after, before, ends, across, d_ffs, hidden = fence(
            (after, before, ends, across, d_ffs, hidden)
        )
        ends, *sent = scatter_start(ends, after, before, n)
        down_grad = weight_grad([d_ffs[1], d_ffs[3], d_ffs[2], d_ffs[0]], hidden, SIDE_COST)
        ends, down_grad = fence((ends, down_grad))
        down_rows = scatter_dp(down_grad)
        sent = [scatter_far(far, ends)] + sent
        gate_up_grad = weight_grad([residual_all], d_both)
        sent, across, gate_up_grad = fence((sent, across, gate_up_grad))
        gate_up_rows = scatter_dp(gate_up_grad)
        d_res, d_attn, grad_attn_gain, *d_pieces = residual_back(
            me_ref, own, sent + [across], cot, attn_out, attn_gain, w_first, n
        )
        d_mixed = [d_pieces[0]] + [None] * (n - 1)
        for p in range(1, n):
            d_mixed[n - p] = lax.ppermute(
                d_pieces[p], "seq", [(i, (i + p) % n) for i in range(n)]
            )
        d_mixed, d_attn = fence((d_mixed, d_attn))
        d_attn_part = columns_to_parts(d_attn, me, n)
        d_query, d_key, d_v, inner, gain_sums = attend_back(
            me_ref, d_mixed, q_low, k_low, v_low, qkv, factors, q_gain, k_gain, tables, seg, n
        )
        inner, d_attn_part, down_back = fence(
            (inner, d_attn_part, row_blocks(down_rows, me, n))
        )
        inner = sum_stats(inner, n)
        inner, down_back = fence((inner, down_back))
        down_back = send_blocks(down_back)
        d_qkv, ends, after, before, far, own = input_back(
            me_ref, d_query, d_key, d_v, qkv, stat_columns(inner) / width, factors, w_qkv
        )
        d_qkv, ends, after, before, far, own, down_back = fence(
            (d_qkv, ends, after, before, far, own, down_back)
        )
        ends, *sent = scatter_start(ends, after, before, n)
        sent.append(lax.ppermute(far, "seq", [(0, 2), (3, 1)]))
        attn_grads = attn_grad(me_ref, x_all, d_qkv, pieces, d_attn_part)
        ends, attn_grads = fence((ends, attn_grads))
        attn_rows = scatter_dp(attn_grads)
        sent.append(scatter_far(far, ends))
        gate_up_back = row_blocks(gate_up_rows, me, n)
        sent[0], gate_up_back = fence((sent[0], gate_up_back))
        input_grad = add_up([d_res, own] + sent)
        spread = lambda g: lax.dynamic_update_slice(jnp.zeros(width, F32), g, (me * part,))
        gains = jnp.stack(
            [spread(gain_sums[0, 0]), spread(gain_sums[1, 0]), grad_attn_gain[0], grad_ff_gain]
        )
        input_grad, gains = fence((input_grad, gains))
        gate_up_back = send_blocks(gate_up_back)
        gains = sum_everywhere(gains, dp_count, n)
        attn_rows, input_grad, gate_up_back, down_back, gains = fence(
            (attn_rows, input_grad, gate_up_back, down_back, gains)
        )
        attn_back = send_blocks(row_blocks(attn_rows, me, n))
        grad_gate, grad_up = join_columns(me_ref, gate_up_back, 2)
        grad_down = join_columns(me_ref, down_back, 1)[0].T
        attn_back, grad_gate, grad_up, grad_down = fence(
            (attn_back, grad_gate, grad_up, grad_down)
        )
        grad_query, grad_key, grad_value, grad_output = join_columns(me_ref, attn_back, 4)

        share = width // devices
        gains = lax.dynamic_slice_in_dim(
            gains, (lax.axis_index("dp") * n + me) * share, share, 1
        )
        return (
            activation[None],
            input_grad[None],
            grad_query,
            grad_key,
            grad_value,
            grad_output,
            grad_gate,
            grad_up,
            grad_down,
            gains[0],
            gains[1],
            gains[2],
            gains[3],
        )

    return shards


def solution(mesh):
    both = P(("dp", "seq"), None)
    tokens = P("dp", "seq", None)
    columns = P(None, ("dp", "seq"))
    gain = P(("dp", "seq"))
    return jax.shard_map(
        build(mesh.shape["dp"], mesh.shape["seq"]),
        mesh=mesh,
        in_specs=(tokens, P("dp", None)) + (both,) * 6 + (columns,) + (P(),) * 4 + (tokens,),
        out_specs=(tokens, tokens) + (both,) * 6 + (columns,) + (gain,) * 4,
        check_vma=False,
    )
```
